32 devices in a mesh: dp: 4 (over z), seq: 4 (over y, core), tensor: 2 (over x).
Axes of the slice: x: 2, y: 2, z: 4, core: 2. Of those that a mesh axis runs over, the one named last changes fastest.
Arguments:
- q_self: bfloat16 [4, 512, 4096], P('dp', 'seq', 'tensor'), may hold values from -162 to 162
- k_self: bfloat16 [4, 512, 1024], P('dp', 'seq', 'tensor'), may hold values from -6 to 6
- v_self: bfloat16 [4, 512, 1024], P('dp', 'seq', 'tensor'), may hold values from -6 to 6
- docs: int32 [4, 512], P('dp', 'seq'), may hold values from 0 to 3, never falling along the last dimension, each value on 1 to 384 neighbouring positions
- q_cross: bfloat16 [4, 512, 4096], P('dp', 'seq', 'tensor'), may hold values from -162 to 162
- cotangent: bfloat16 [4, 512, 4096], P('dp', 'seq', 'tensor'), may hold values from -6 to 6
- img_keys: bfloat16 [4, 128, 1024], P('dp', 'seq', 'tensor'), may hold values from -6 to 6
- features: bfloat16 [4, 128, 1280], P('dp', 'seq'), may hold values from -6 to 6
- w_value: bfloat16 [1280, 1024], P(None, 'tensor'), may hold values from -0.15625 to 0.15625
- tiles: int32 [4, 4], P('dp'), may hold values from 1 to 4
- cite: int32 [4, 4], P('dp'), may hold values from 0 to 3, each once within a row
Outputs:
- combined: bfloat16 [4, 512, 4096], P('dp', 'seq', 'tensor')
- weight_grad: float32 [1280, 1024], P(('dp', 'seq'), 'tensor')
The draws below stay inside these ranges and needn't reach their ends.
Inputs may be any that keep to these rules, and one draw needn't show every extreme that they name: `docs`: along each sample the document numbers never fall; every document 0 to 3 has one or more tokens. `cite`: each sample's row names every image exactly once.
All inputs are finite; a program needn't handle non-finite values.
Results may differ from the reference program's by a relative error of at most 0.029.
Values may be sent and summed in bfloat16 or wider, within the bound.
No kernel may reach another device: no remote copies, remote signals or barrier semaphores. Data moves between devices by JAX's collectives and lax.ppermute only.
A program may use at most 64 MiB of HBM per device.

```python
import math
import jax
import jax.numpy as jnp
import numpy as np
from jax import lax

HEADS = 32
KVH = 8
HD = 128
VIS = 1280
TILES = 4
TILE_TOK = 8
SAMPLES = 4
TOKENS = 512
IMAGES = 4
DOCS = 4
IMG_TOK = 32


def clipped_normal(seed_key, shape):
    return jnp.clip(jax.random.normal(seed_key, shape, jnp.float32), -6.0, 6.0)


def self_pair(seed_key):
    key_query, key_keys = jax.random.split(seed_key, 2)
    key_field = clipped_normal(key_keys, (SAMPLES, TOKENS, KVH, HD))
    queries = clipped_normal(key_query, (SAMPLES, TOKENS, HEADS, HD))
    return (queries.reshape(SAMPLES, TOKENS, HEADS * HD), key_field.reshape(SAMPLES, TOKENS, KVH * HD))


def cross_pair(seed_key):
    key_query, key_keys = jax.random.split(seed_key, 2)
    slot_count = TILES * TILE_TOK
    key_field = clipped_normal(key_keys, (SAMPLES, IMAGES, slot_count, KVH, HD))
    queries = clipped_normal(key_query, (SAMPLES, TOKENS, HEADS, HD))
    return (queries.reshape(SAMPLES, TOKENS, HEADS * HD), key_field.reshape(SAMPLES, IMAGES * slot_count, KVH * HD))


def draw_q_self(key, part):
    return self_pair(jax.random.fold_in(key, 3))[0].astype(jnp.bfloat16)


def draw_k_self(key, part):
    return self_pair(jax.random.fold_in(key, 3))[1].astype(jnp.bfloat16)


def draw_q_cross(key, part):
    return cross_pair(jax.random.fold_in(key, 5))[0].astype(jnp.bfloat16)


def draw_img_keys(key, part):
    return cross_pair(jax.random.fold_in(key, 5))[1].astype(jnp.bfloat16)


def plant(values, rng, low, high):
    index_at = [jax.random.randint(jax.random.fold_in(rng, axis), (), 0, length) for axis, length in enumerate(values.shape)]
    longest = values.shape.index(max(values.shape))
    next_to = index_at[:longest] + [(index_at[longest] + 1) % values.shape[longest]] + index_at[longest + 1:]
    return values.at[tuple(index_at)].set(low).at[tuple(next_to)].set(high)


def raised(entries, own_key, source, target, blocks, factor):
    owner, partner = [(jnp.arange(entries.shape[axis_at]) // (entries.shape[axis_at] // blocks)).reshape([-1 if axis == axis_at else 1 for axis in range(entries.ndim)]) for axis_at in (source, target)]
    chosen = jax.random.permutation(own_key, blocks)[partner]
    strong = (owner == chosen) | (owner == (partner + blocks // 2) % blocks)
    return jnp.where(strong, factor * entries, entries)


def level_of(own_key, shape, shards, low, largest):
    def one(position, parts):
        heights = jax.random.uniform(jax.random.fold_in(jax.random.fold_in(own_key, 6), position), (parts,), jnp.float32, low / len(shards), largest / len(shards))
        return jnp.repeat(jnp.exp(heights), shape[position] // parts).reshape((-1,) + (1,) * (len(shape) - position - 1))

    gain = one(*shards[0])
    for cut in shards[1:]:
        gain = gain * one(*cut)
    return gain


def split_up(amount, total, limit, skew):
    portions = [(1 << 20) // math.isqrt(grade ** skew) + 1 for grade in range(2, amount + 1)]
    rest, counts = total - limit - (amount - 1), [1] * (amount - 1)
    while rest > 0:
        movable = [i for i in range(amount - 1) if counts[i] < limit]
        mass, remaining = sum([portions[i] for i in movable]), rest
        for i in movable:
            more = min(limit - counts[i], max(1, remaining * portions[i] // mass), rest)
            counts[i] = counts[i] + more
            rest = rest - more
    return np.array([limit] + counts)


def ragged(key, count, total, reach, lean):
    if count == 2:
        one = jax.random.randint(key, (), max(1, total - reach), min(reach, total - 1) + 1)
        return jnp.stack([one, total - one])
    lengths = jnp.asarray(split_up(count, total, reach, lean), jnp.int32)
    couples = (count - 1) // 2
    source_of, taker = lengths[1:1 + 2 * couples:2], lengths[2:2 + 2 * couples:2]
    slack = jnp.minimum(source_of - 1, reach - taker)
    passed = jax.random.randint(jax.random.fold_in(key, 1), (couples,), 0, 1 << 20) % (slack + 1)
    lengths = lengths.at[1:1 + 2 * couples:2].set(source_of - passed).at[2:2 + 2 * couples:2].set(taker + passed)
    return lengths[jax.random.permutation(jax.random.fold_in(key, 2), count)]


def scatter_about(rng, dims, scale, limit, shards=(), held_as=jnp.bfloat16):
    loudness = level_of(rng, dims, shards, -0.22, 0.18) if shards else 1.0
    drawn = jax.random.normal(rng, dims, jnp.float32) * scale * loudness
    return jnp.minimum(jnp.maximum(drawn, -limit), limit).astype(held_as)


def bell_draw_with(own_key, dims, width, most, shards, heavy, kind=jnp.bfloat16):
    result = width * jax.random.normal(own_key, dims, jnp.float32)
    if shards:
        result = result * level_of(own_key, dims, shards, -0.22, 0.18)
    return jnp.clip(raised(result, jax.random.fold_in(own_key, 3), *heavy), -most, most).astype(kind)


def setup_inputs(seed: int = 0) -> dict:
    key_list = jax.random.split(jax.random.key(seed), 12)
    q_self = draw_q_self(jax.random.fold_in(key_list[11], 71), 0)
    k_self = draw_k_self(jax.random.fold_in(key_list[11], 71), 0)
    v_self = scatter_about(key_list[2], (SAMPLES, TOKENS, KVH * HD), 1.0, 6.0, ((0, 4), (1, 4), (2, 2)))
    docs = jax.vmap(lambda own: jnp.searchsorted(jnp.cumsum(ragged(own, DOCS, TOKENS, 3 * TOKENS // 4, 2)), jnp.arange(TOKENS), side="right"))(jax.random.split(key_list[3], SAMPLES)).reshape((SAMPLES, TOKENS)).astype(jnp.int32)
    q_cross = draw_q_cross(jax.random.fold_in(key_list[11], 71), 0)
    cotangent = scatter_about(key_list[5], (SAMPLES, TOKENS, HEADS * HD), 1.0, 6.0, ((0, 4), (1, 4), (2, 2)))
    img_keys = draw_img_keys(jax.random.fold_in(key_list[11], 71), 0)
    features = bell_draw_with(key_list[7], (SAMPLES, IMAGES * IMG_TOK, VIS), 1.0, 6.0, ((0, 4), (1, 4)), (1, 2, 4, 2.0))
    w_value = scatter_about(key_list[8], (VIS, KVH * HD), VIS ** -0.5, 0.15625, ((1, 2),))
    tiles = plant(jax.random.randint(key_list[9], (SAMPLES, IMAGES), 1, TILES + 1), jax.random.fold_in(key_list[9], 1), 1, TILES).astype(jnp.int32)
    cite = jax.vmap(lambda own: jax.random.permutation(own, IMAGES))(jax.random.split(key_list[10], SAMPLES)).reshape((SAMPLES, DOCS)).astype(jnp.int32)
    return dict(q_self=q_self, k_self=k_self, v_self=v_self, docs=docs, q_cross=q_cross, cotangent=cotangent, img_keys=img_keys, features=features, w_value=w_value, tiles=tiles, cite=cite)


MASK_FILL = -1e30


def rounded(values):
    half = lax.optimization_barrier(values.astype(jnp.bfloat16))
    return half.astype(jnp.float32)


def one_sample(q_self, k_self, v_self, docs, q_cross, cotangent, img_keys, features, w_value, tiles, cite):
    tok_count = q_self.shape[0]
    group_size = HEADS // KVH
    score_scale = HD ** -0.5
    key_count = img_keys.shape[0]
    slot_count = key_count // tiles.shape[0]
    values_img = jnp.dot(features, w_value, preferred_element_type=jnp.float32).astype(jnp.bfloat16)
    keys_self = k_self.reshape(tok_count, KVH, HD).astype(jnp.float32)
    vals_self = v_self.reshape(tok_count, KVH, HD).astype(jnp.float32)
    keys_image = img_keys.reshape(key_count, KVH, HD).astype(jnp.float32)
    vals_image = values_img.reshape(key_count, KVH, HD).astype(jnp.float32)
    positions = jnp.arange(tok_count, dtype=jnp.int32)
    slot_ids = jnp.arange(key_count, dtype=jnp.int32)
    key_image = slot_ids // slot_count
    usable = (slot_ids % slot_count) < jnp.repeat(tiles, slot_count, total_repeat_length=key_count) * TILE_TOK
    image_of = cite[docs]
    block_rows = math.gcd(tok_count, 512)

    def block_of(array, offset):
        return lax.dynamic_slice_in_dim(array, offset, block_rows, 0)

    def block_step(grad_sum, offset):
        query_pos = offset + jnp.arange(block_rows, dtype=jnp.int32)
        block_docs = block_of(docs, offset)
        queries = block_of(q_self, offset).reshape(block_rows, KVH, group_size, HD).astype(jnp.float32)
        scores = jnp.einsum("tgcd,sgd->gcts", queries, keys_self) * score_scale
        kept = (query_pos[:, None] >= positions[None, :]) & (block_docs[:, None] == docs[None, :])
        scores = jnp.where(kept, scores, MASK_FILL)
        exp_self = jnp.where(kept, jnp.exp(scores - jnp.max(scores, axis=-1, keepdims=True)), 0.0)
        self_out = jnp.einsum("gcts,sgd->gctd", rounded(exp_self), vals_self) / jnp.sum(exp_self, axis=-1)[..., None]
        cross_q = block_of(q_cross, offset).reshape(block_rows, KVH, group_size, HD).astype(jnp.float32)
        cross_scores = jnp.einsum("tgcd,sgd->gcts", cross_q, keys_image) * score_scale
        cross_kept = (block_of(image_of, offset)[:, None] == key_image[None, :]) & usable[None, :]
        cross_scores = jnp.where(cross_kept, cross_scores, MASK_FILL)
        cross_exp = jnp.where(cross_kept, jnp.exp(cross_scores - jnp.max(cross_scores, axis=-1, keepdims=True)), 0.0)
        cross_weights = rounded(cross_exp / jnp.sum(cross_exp, axis=-1, keepdims=True))
        cross_out = jnp.einsum("gcts,sgd->gctd", cross_weights, vals_image)
        merged = (self_out + cross_out).astype(jnp.bfloat16).transpose(2, 0, 1, 3).reshape(block_rows, HEADS * HD)
        cot_rows = block_of(cotangent, offset).reshape(block_rows, KVH, group_size, HD).astype(jnp.float32)
        grad_sum = grad_sum + jnp.einsum("gcts,tgcd->sgd", cross_weights, cot_rows)
        return grad_sum, merged

    starts = jnp.arange(0, tok_count, block_rows, dtype=jnp.int32)
    grad_sum, out_blocks = lax.scan(block_step, jnp.zeros((key_count, KVH, HD), jnp.float32), starts)
    value_grad = grad_sum.reshape(key_count, KVH * HD).astype(jnp.bfloat16)
    weight_term = jnp.dot(features.T, value_grad, preferred_element_type=jnp.float32)
    return out_blocks.reshape(tok_count, HEADS * HD), weight_term


def reference(q_self, k_self, v_self, docs, q_cross, cotangent, img_keys, features, w_value, tiles, cite):
    outputs = []
    weight_grad = jnp.zeros((VIS, KVH * HD), jnp.float32)
    for sample in range(SAMPLES):
        merged, weight_term = one_sample(q_self[sample], k_self[sample], v_self[sample], docs[sample], q_cross[sample], cotangent[sample], img_keys[sample], features[sample], w_value, tiles[sample], cite[sample])
        outputs.append(merged)
        weight_grad = weight_grad + weight_term
    return jnp.stack(outputs, axis=0), weight_grad
```

```python
import functools
import math

import jax
import jax.numpy as jnp
from jax import lax
from jax.experimental import pallas as pl
from jax.experimental.pallas import tpu as pltpu
from jax.sharding import PartitionSpec as P

HD = 128
TILE_TOK = 8


MASK_FILL = -1e30
LOG2E = math.log2(math.e)


def absorb_block(
    running, queries, key_rows, value_rows, key_docs, key_pos, query_pos, my_docs, score_scale
):
    running_max, denominator, numerator = running
    kv_local = queries.shape[1]
    key_count = key_rows.shape[0]
    key_heads = key_rows.reshape(key_count, kv_local, HD)
    value_heads = value_rows.reshape(key_count, kv_local, HD)
    scores = (
        jnp.einsum("tgcd,sgd->gcts", queries, key_heads, preferred_element_type=jnp.float32)
        * score_scale
    )
    kept = (query_pos[:, None] >= key_pos[None, :]) & (my_docs[:, None] == key_docs[None, :])
    scores = jnp.where(kept, scores, MASK_FILL)
    new_max = jnp.maximum(running_max, jnp.max(scores, axis=-1))
    factor = jnp.exp(running_max - new_max)
    weights = jnp.where(kept, jnp.exp(scores - new_max[..., None]), 0.0)
    denominator = factor * denominator + jnp.sum(weights, axis=-1)
    numerator = factor[..., None] * numerator + jnp.einsum(
        "gcts,sgd->gctd",
        weights.astype(jnp.bfloat16),
        value_heads,
        preferred_element_type=jnp.float32,
    )
    return (new_max, denominator, numerator)


def on_device_general(
    q_self, k_self, v_self, docs, q_cross, cotangent, img_keys, features, w_value, tiles, cite
):
    tok_rows = q_self.shape[1]
    kv_local = k_self.shape[2] // HD
    heads_local = q_self.shape[2] // HD
    group_size = heads_local // kv_local
    score_scale = HD ** (-0.5)
    first_row = lax.axis_index("seq") * tok_rows
    query_pos = first_row + jnp.arange(tok_rows, dtype=jnp.int32)
    my_docs = docs[0]
    queries = q_self[0].reshape(tok_rows, kv_local, group_size, HD)
    start_state = (
        jnp.full((kv_local, group_size, tok_rows), MASK_FILL, jnp.float32),
        jnp.zeros((kv_local, group_size, tok_rows), jnp.float32),
        jnp.zeros((kv_local, group_size, tok_rows, HD), jnp.float32),
    )
    piece_keys = lax.all_gather(k_self, "seq", axis=1, tiled=True)
    piece_values = lax.all_gather(v_self, "seq", axis=1, tiled=True)
    piece_docs = lax.all_gather(docs, "seq", axis=1, tiled=True)
    key_count = piece_keys.shape[1]
    block_rows = math.gcd(key_count, 512)
    block_count = key_count // block_rows
    key_blocks = piece_keys[0].reshape(block_count, block_rows, -1)
    value_blocks = piece_values[0].reshape(block_count, block_rows, -1)
    doc_blocks = piece_docs[0].reshape(block_count, block_rows)
    pos_blocks = jnp.arange(key_count, dtype=jnp.int32).reshape(block_count, block_rows)

    def absorb_step(state_now, block_item):
        key_part, value_part, doc_part, pos_part = block_item
        return (
            absorb_block(
                state_now,
                queries,
                key_part,
                value_part,
                doc_part,
                pos_part,
                query_pos,
                my_docs,
                score_scale,
            ),
            None,
        )

    running_max, denominator, numerator = lax.scan(
        absorb_step, start_state, (key_blocks, value_blocks, doc_blocks, pos_blocks)
    )[0]
    self_out = numerator / denominator[..., None]
    values_own = jnp.dot(features[0], w_value, preferred_element_type=jnp.float32).astype(
        jnp.bfloat16
    )
    image_keys, image_values = (
        lax.all_gather(img_keys[0], "seq", axis=0, tiled=True),
        lax.all_gather(values_own, "seq", axis=0, tiled=True),
    )
    key_count = image_keys.shape[0]
    image_count = tiles.shape[1]
    slot_count = key_count // image_count
    doc_hit = my_docs[:, None] == jnp.arange(cite.shape[1], dtype=jnp.int32)[None, :]
    image_of = jnp.sum(jnp.where(doc_hit, cite[0][None, :], 0), axis=1)
    slot_ids = jnp.arange(key_count, dtype=jnp.int32)
    key_image = slot_ids // slot_count
    owner_hit = key_image[:, None] == jnp.arange(image_count, dtype=jnp.int32)[None, :]
    tile_limit = jnp.sum(jnp.where(owner_hit, tiles[0][None, :], 0), axis=1) * TILE_TOK
    cross_kept = (image_of[:, None] == key_image[None, :]) & (slot_ids % slot_count < tile_limit)[
        None, :
    ]
    cross_q = q_cross[0].reshape(tok_rows, kv_local, group_size, HD)
    cross_scores = (
        jnp.einsum(
            "tgcd,sgd->gcts",
            cross_q,
            image_keys.reshape(key_count, kv_local, HD),
            preferred_element_type=jnp.float32,
        )
        * score_scale
    )
    cross_scores = jnp.where(cross_kept, cross_scores, MASK_FILL)
    cross_exp = jnp.where(
        cross_kept, jnp.exp(cross_scores - jnp.max(cross_scores, axis=-1, keepdims=True)), 0.0
    )
    cross_weights = (cross_exp / jnp.sum(cross_exp, axis=-1, keepdims=True)).astype(jnp.bfloat16)
    cross_out = jnp.einsum(
        "gcts,sgd->gctd",
        cross_weights,
        image_values.reshape(key_count, kv_local, HD),
        preferred_element_type=jnp.float32,
    )
    merged = (
        (self_out + cross_out)
        .astype(jnp.bfloat16)
        .transpose(2, 0, 1, 3)
        .reshape(1, tok_rows, heads_local * HD)
    )
    cot_rows = cotangent[0].reshape(tok_rows, kv_local, group_size, HD)
    grad_terms = jnp.einsum(
        "gcts,tgcd->sgd", cross_weights, cot_rows, preferred_element_type=jnp.float32
    ).reshape(key_count, kv_local * HD)
    value_grad = lax.psum_scatter(
        grad_terms.astype(jnp.bfloat16), "seq", scatter_dimension=0, tiled=True
    )
    own_features = features[0]
    summed_samples = lax.psum_scatter(
        lax.dot_general(
            own_features, value_grad, (((0,), (0,)), ((), ())), preferred_element_type=jnp.float32
        ).astype(jnp.bfloat16),
        "dp",
        scatter_dimension=0,
        tiled=True,
    )
    weight_grad = lax.psum_scatter(summed_samples, "seq", scatter_dimension=0, tiled=True).astype(
        jnp.float32
    )
    return (merged, weight_grad)


def dot_nt(left, right):
    return lax.dot_general(
        left, right, (((1,), (1,)), ((), ())), preferred_element_type=jnp.float32
    )


def dot_nn(left, right):
    return lax.dot_general(
        left, right, (((1,), (0,)), ((), ())), preferred_element_type=jnp.float32
    )


def dot_tn(left, right):
    return lax.dot_general(
        left, right, (((0,), (0,)), ((), ())), preferred_element_type=jnp.float32
    )


def stacked_heads(ref, group, group_size):
    first = group * group_size
    return jnp.concatenate(
        [ref[:, (first + c) * HD : (first + c + 1) * HD] for c in range(group_size)], axis=0
    )


def cross_kernel(
    sizes, tiles_ref, cite_ref, docs_ref, head_ref, q_ref, cot_ref, grad_ref, weights_ref
):
    kv_local, group_size, slots, images, slot_count = sizes
    blocks = head_ref.shape[0]
    key_count = blocks * slots
    docs = docs_ref[...]
    tok_rows = docs.shape[1]
    image_of = jnp.zeros_like(docs)
    for doc in range(cite_ref.shape[1]):
        image_of = jnp.where(docs == doc, cite_ref[0, doc], image_of)
    slot_ids = lax.broadcasted_iota(jnp.int32, (key_count, tok_rows), 0)
    bias = jnp.full((key_count, tok_rows), MASK_FILL, jnp.float32)
    for image in range(images):
        first = image * slot_count
        usable = (slot_ids >= first) & (slot_ids < first + tiles_ref[0, image] * TILE_TOK)
        bias = jnp.where(usable & (image_of == image), 0.0, bias)
    bias = jnp.concatenate([bias] * group_size, axis=1)
    scale = HD ** (-0.5) * LOG2E
    for group in range(kv_local):
        columns = slice(group * HD, (group + 1) * HD)
        keys = jnp.concatenate([head_ref[b, :slots, columns] for b in range(blocks)], axis=0)
        scores = dot_nt(keys, stacked_heads(q_ref, group, group_size)) * scale + bias
        exps = jnp.exp2(scores - jnp.max(scores, axis=0, keepdims=True))
        inverse = 1.0 / jnp.sum(exps, axis=0, keepdims=True)
        weights = (exps * inverse).astype(jnp.bfloat16)
        weights_ref[group] = weights
        grad_ref[:, columns] = dot_nn(weights, stacked_heads(cot_ref, group, group_size)).astype(
            jnp.bfloat16
        )


def attend_kernel(sizes, where_ref, docs_ref, head_ref, q_ref, w_ref, weights_ref, *rest):
    kv_local, group_size, slots, feature_rows = sizes
    blocks = head_ref.shape[0]
    packs, out_ref, values_ref = rest[:blocks], rest[blocks], rest[blocks + 1]
    seq_at = where_ref[0]
    tok_rows = q_ref.shape[0]
    key_rows = (packs[0].shape[0] - feature_rows) // 2
    width = packs[0].shape[1]
    vision = w_ref.shape[0]
    parts = feature_rows // slots
    total = None
    for part in range(parts):
        cut = min(width, vision - part * width)
        rows = jnp.concatenate(
            [pack[part * slots : (part + 1) * slots, :cut] for pack in packs], axis=0
        )
        term = dot_nn(rows, w_ref[part * width : part * width + cut, :])
        total = term if total is None else total + term
    values = total.astype(jnp.bfloat16)
    for x in range(blocks):
        owner = pl.multiple_of((seq_at ^ x) * slots, slots)
        values_ref[pl.ds(owner, slots), :] = values[x * slots : (x + 1) * slots]
    docs = docs_ref[...].astype(jnp.float32)
    start = jnp.zeros((1, tok_rows), jnp.float32)
    for b in range(blocks):
        row = head_ref[b, slots : slots + 16, :tok_rows].astype(jnp.float32)[0:1]
        column = jnp.transpose(jnp.broadcast_to(row, (tok_rows, tok_rows)))
        start = start + jnp.sum(jnp.where(column < docs, 1.0, 0.0), axis=0, keepdims=True)
    start = start.astype(jnp.int32)
    query_pos = seq_at * tok_rows + lax.broadcasted_iota(jnp.int32, (1, tok_rows), 1)
    bias = []
    for x in range(blocks):
        key_pos = (seq_at ^ x) * key_rows + lax.broadcasted_iota(
            jnp.int32, (key_rows, tok_rows), 0
        )
        kept = (key_pos >= start) & (key_pos <= query_pos)
        bias.append(jnp.where(kept, 0.0, MASK_FILL))
    bias = jnp.concatenate(bias, axis=0)
    bias = jnp.concatenate([bias] * group_size, axis=1)
    scale = HD ** (-0.5) * LOG2E
    first_key, first_value = feature_rows, feature_rows + key_rows
    for group in range(kv_local):
        columns = slice(group * HD, (group + 1) * HD)
        keys = jnp.concatenate(
            [pack[first_key : first_key + key_rows, columns] for pack in packs], axis=0
        )
        vals = jnp.concatenate(
            [pack[first_value : first_value + key_rows, columns] for pack in packs], axis=0
        )
        scores = dot_nt(keys, stacked_heads(q_ref, group, group_size)) * scale + bias
        exps = jnp.exp2(scores - jnp.max(scores, axis=0, keepdims=True))
        inverse = 1.0 / jnp.sum(exps, axis=0, keepdims=True)
        self_out = dot_tn(vals, exps.astype(jnp.bfloat16)) * inverse
        cross_out = dot_tn(values_ref[:, columns], weights_ref[group])
        merged = (self_out + cross_out).astype(jnp.bfloat16)
        for c in range(group_size):
            head = group * group_size + c
            out_ref[:, head * HD : (head + 1) * HD] = jnp.transpose(
                merged[:, c * tok_rows : (c + 1) * tok_rows]
            )


def product_kernel(sizes, where_ref, terms_ref, *rest):
    slots, vision, out_rows, steps = sizes
    blocks = terms_ref.shape[0]
    packs, outs = rest[:blocks], rest[blocks : blocks + steps]
    sum_ref, turned_ref = rest[blocks + steps :]
    seq_at, dp_at = where_ref[0], where_ref[1]
    width = packs[0].shape[1]
    total = terms_ref[0].astype(jnp.float32)
    for b in range(1, blocks):
        total = total + terms_ref[b].astype(jnp.float32)
    sum_ref[...] = total.astype(jnp.bfloat16)
    grads = jnp.concatenate(
        [
            sum_ref[pl.ds(pl.multiple_of((seq_at ^ x) * slots, slots), slots), :]
            for x in range(blocks)
        ],
        axis=0,
    )
    for part in range(-(-vision // width)):
        cut = min(width, vision - part * width)
        rows = jnp.concatenate(
            [pack[part * slots : (part + 1) * slots, :cut] for pack in packs], axis=0
        )
        turned_ref[part * width : part * width + cut, :] = jnp.transpose(rows)
    for x in range(steps):
        row = pl.multiple_of(((dp_at ^ x) * blocks + seq_at) * out_rows, out_rows)
        block = dot_nn(turned_ref[pl.ds(row, out_rows), :], grads)
        outs[x][...] = block.astype(outs[x].dtype)


def vmem_specs(count):
    return [pl.BlockSpec(memory_space=pltpu.VMEM)] * count


def swap(array, axis, size, x):
    return lax.ppermute(array, axis, [(i, i ^ x) for i in range(size)])


def on_device_small(
    seq_size,
    dp_size,
    q_self,
    k_self,
    v_self,
    docs,
    q_cross,
    cotangent,
    img_keys,
    features,
    w_value,
    tiles,
    cite,
):
    tok_rows = q_self.shape[1]
    width = k_self.shape[2]
    kv_local = width // HD
    heads_local = q_self.shape[2] // HD
    group_size = heads_local // kv_local
    slots = img_keys.shape[1]
    vision = features.shape[2]
    images = tiles.shape[1]
    out_rows = vision // (seq_size * dp_size)
    key_count = slots * seq_size
    smem = pl.BlockSpec(memory_space=pltpu.SMEM)
    seq_at = lax.axis_index("seq")
    dp_at = lax.axis_index("dp")
    where_at = jnp.stack([seq_at, dp_at]).astype(jnp.int32)

    doc_row = jnp.pad(docs.astype(jnp.bfloat16), ((0, 15), (0, width - tok_rows)))
    heads_all = lax.all_gather(jnp.concatenate([img_keys[0], doc_row], axis=0), "seq", axis=0)

    parts = -(-vision // width)
    feature_rows = parts * slots
    padded = jnp.pad(features[0], ((0, 0), (0, parts * width - vision)))
    pieces = [padded[:, p * width : (p + 1) * width] for p in range(parts)]
    packs = [jnp.concatenate(pieces + [k_self[0], v_self[0]], axis=0)]
    bit = seq_size // 2
    order = {0: packs[0]}
    while bit:
        for x in list(order):
            order[x ^ bit] = swap(order[x], "seq", seq_size, bit)
        bit //= 2
    packs = [order[x] for x in range(seq_size)]

    grad_terms, weights = pl.pallas_call(
        functools.partial(
            cross_kernel, (kv_local, group_size, slots, images, key_count // images)
        ),
        out_shape=(
            jax.ShapeDtypeStruct((key_count, width), jnp.bfloat16),
            jax.ShapeDtypeStruct((kv_local, key_count, group_size * tok_rows), jnp.bfloat16),
        ),
        in_specs=[smem, smem] + vmem_specs(4),
        out_specs=tuple(vmem_specs(2)),
        compiler_params=pltpu.CompilerParams(vmem_limit_bytes=24 << 20),
        name="cross",
    )(tiles, cite, docs, heads_all, q_cross[0], cotangent[0])

    terms_all = lax.all_gather(grad_terms, "seq", axis=0)
    blocks_out = pl.pallas_call(
        functools.partial(product_kernel, (slots, vision, out_rows, dp_size)),
        out_shape=tuple(
            jax.ShapeDtypeStruct((out_rows, width), jnp.bfloat16 if x else jnp.float32)
            for x in range(dp_size)
        ),
        in_specs=[smem] + vmem_specs(1 + seq_size),
        out_specs=tuple(vmem_specs(dp_size)),
        scratch_shapes=[
            pltpu.VMEM((key_count, width), jnp.bfloat16),
            pltpu.VMEM((vision, key_count), jnp.bfloat16),
        ],
        compiler_params=pltpu.CompilerParams(vmem_limit_bytes=16 << 20),
        name="product",
    )(where_at, terms_all, *packs)
    weight_grad = blocks_out[0]
    for x in range(1, dp_size):
        weight_grad = weight_grad + swap(blocks_out[x], "dp", dp_size, x).astype(jnp.float32)

    merged = pl.pallas_call(
        functools.partial(attend_kernel, (kv_local, group_size, slots, feature_rows)),
        out_shape=jax.ShapeDtypeStruct((tok_rows, heads_local * HD), jnp.bfloat16),
        in_specs=[smem] + vmem_specs(5 + seq_size),
        out_specs=vmem_specs(1)[0],
        scratch_shapes=[pltpu.VMEM((key_count, width), jnp.bfloat16)],
        compiler_params=pltpu.CompilerParams(vmem_limit_bytes=32 << 20),
        name="attend",
    )(where_at, docs, heads_all, q_self[0], w_value, weights, *packs)
    return (merged[None], weight_grad)


def fits_small(mesh, shapes):
    seq_size, dp_size = mesh.shape["seq"], mesh.shape["dp"]
    q_self, k_self, img_keys, features, w_value, cite = shapes
    tensor = mesh.shape["tensor"]
    powers = all(n & (n - 1) == 0 for n in (seq_size, dp_size))
    tok_rows, width = q_self[1] // seq_size, k_self[2] // tensor
    slots = img_keys[1] // seq_size
    rows, left = divmod(features[2], seq_size * dp_size)
    return (
        powers
        and seq_size <= 4
        and dp_size <= 8
        and tok_rows == HD
        and tok_rows <= width
        and slots % 32 == 0
        and slots * seq_size == HD
        and left == 0
        and rows % 16 == 0
        and features[2] % HD == 0
        and width % HD == 0
        and cite[1] <= 256
    )


def solution(mesh):
    in_specs = (
        P("dp", "seq", "tensor"),
        P("dp", "seq", "tensor"),
        P("dp", "seq", "tensor"),
        P("dp", "seq"),
        P("dp", "seq", "tensor"),
        P("dp", "seq", "tensor"),
        P("dp", "seq", "tensor"),
        P("dp", "seq", None),
        P(None, "tensor"),
        P("dp", None),
        P("dp", None),
    )
    out_specs = (P("dp", "seq", "tensor"), P(("dp", "seq"), "tensor"))

    def run(*arrays):
        shapes = [arrays[i].shape for i in (0, 1, 6, 7, 8, 10)]
        body = on_device_general
        if fits_small(mesh, shapes):
            body = functools.partial(on_device_small, mesh.shape["seq"], mesh.shape["dp"])
        return jax.shard_map(
            body, mesh=mesh, in_specs=in_specs, out_specs=out_specs, check_vma=False
        )(*arrays)

    return run
```

```python
import functools
import math

import jax
import jax.numpy as jnp
from jax import lax
from jax.experimental import pallas as pl
from jax.experimental.pallas import tpu as pltpu
from jax.sharding import PartitionSpec as P


HD = 128
TILE_TOK = 8


MASK_FILL = -1e30
LOG2E = math.log2(math.e)


def absorb_block(
    running, queries, key_rows, value_rows, key_docs, key_pos, query_pos, my_docs, score_scale
):
    running_max, denominator, numerator = running
    kv_local = queries.shape[1]
    key_count = key_rows.shape[0]
    key_heads = key_rows.reshape(key_count, kv_local, HD)
    value_heads = value_rows.reshape(key_count, kv_local, HD)
    scores = (
        jnp.einsum("tgcd,sgd->gcts", queries, key_heads, preferred_element_type=jnp.float32)
        * score_scale
    )
    kept = (query_pos[:, None] >= key_pos[None, :]) & (my_docs[:, None] == key_docs[None, :])
    scores = jnp.where(kept, scores, MASK_FILL)
    new_max = jnp.maximum(running_max, jnp.max(scores, axis=-1))
    factor = jnp.exp(running_max - new_max)
    weights = jnp.where(kept, jnp.exp(scores - new_max[..., None]), 0.0)
    denominator = factor * denominator + jnp.sum(weights, axis=-1)
    numerator = factor[..., None] * numerator + jnp.einsum(
        "gcts,sgd->gctd",
        weights.astype(jnp.bfloat16),
        value_heads,
        preferred_element_type=jnp.float32,
    )
    return (new_max, denominator, numerator)


def on_device_general(
    q_self, k_self, v_self, docs, q_cross, cotangent, img_keys, features, w_value, tiles, cite
):
    tok_rows = q_self.shape[1]
    kv_local = k_self.shape[2] // HD
    heads_local = q_self.shape[2] // HD
    group_size = heads_local // kv_local
    score_scale = HD ** (-0.5)
    first_row = lax.axis_index("seq") * tok_rows
    query_pos = first_row + jnp.arange(tok_rows, dtype=jnp.int32)
    my_docs = docs[0]
    queries = q_self[0].reshape(tok_rows, kv_local, group_size, HD)
    start_state = (
        jnp.full((kv_local, group_size, tok_rows), MASK_FILL, jnp.float32),
        jnp.zeros((kv_local, group_size, tok_rows), jnp.float32),
        jnp.zeros((kv_local, group_size, tok_rows, HD), jnp.float32),
    )
    piece_keys = lax.all_gather(k_self, "seq", axis=1, tiled=True)
    piece_values = lax.all_gather(v_self, "seq", axis=1, tiled=True)
    piece_docs = lax.all_gather(docs, "seq", axis=1, tiled=True)
    key_count = piece_keys.shape[1]
    block_rows = math.gcd(key_count, 512)
    block_count = key_count // block_rows
    key_blocks = piece_keys[0].reshape(block_count, block_rows, -1)
    value_blocks = piece_values[0].reshape(block_count, block_rows, -1)
    doc_blocks = piece_docs[0].reshape(block_count, block_rows)
    pos_blocks = jnp.arange(key_count, dtype=jnp.int32).reshape(block_count, block_rows)

    def absorb_step(state_now, block_item):
        key_part, value_part, doc_part, pos_part = block_item
        return (
            absorb_block(
                state_now,
                queries,
                key_part,
                value_part,
                doc_part,
                pos_part,
                query_pos,
                my_docs,
                score_scale,
            ),
            None,
        )

    _, denominator, numerator = lax.scan(
        absorb_step, start_state, (key_blocks, value_blocks, doc_blocks, pos_blocks)
    )[0]
    self_out = numerator / denominator[..., None]
    values_own = jnp.dot(features[0], w_value, preferred_element_type=jnp.float32).astype(
        jnp.bfloat16
    )
    image_keys, image_values = (
        lax.all_gather(img_keys[0], "seq", axis=0, tiled=True),
        lax.all_gather(values_own, "seq", axis=0, tiled=True),
    )
    key_count = image_keys.shape[0]
    image_count = tiles.shape[1]
    slot_count = key_count // image_count
    doc_hit = my_docs[:, None] == jnp.arange(cite.shape[1], dtype=jnp.int32)[None, :]
    image_of = jnp.sum(jnp.where(doc_hit, cite[0][None, :], 0), axis=1)
    slot_ids = jnp.arange(key_count, dtype=jnp.int32)
    key_image = slot_ids // slot_count
    owner_hit = key_image[:, None] == jnp.arange(image_count, dtype=jnp.int32)[None, :]
    tile_limit = jnp.sum(jnp.where(owner_hit, tiles[0][None, :], 0), axis=1) * TILE_TOK
    cross_kept = (image_of[:, None] == key_image[None, :]) & (slot_ids % slot_count < tile_limit)[
        None, :
    ]
    cross_q = q_cross[0].reshape(tok_rows, kv_local, group_size, HD)
    cross_scores = (
        jnp.einsum(
            "tgcd,sgd->gcts",
            cross_q,
            image_keys.reshape(key_count, kv_local, HD),
            preferred_element_type=jnp.float32,
        )
        * score_scale
    )
    cross_scores = jnp.where(cross_kept, cross_scores, MASK_FILL)
    cross_exp = jnp.where(
        cross_kept, jnp.exp(cross_scores - jnp.max(cross_scores, axis=-1, keepdims=True)), 0.0
    )
    cross_weights = (cross_exp / jnp.sum(cross_exp, axis=-1, keepdims=True)).astype(jnp.bfloat16)
    cross_out = jnp.einsum(
        "gcts,sgd->gctd",
        cross_weights,
        image_values.reshape(key_count, kv_local, HD),
        preferred_element_type=jnp.float32,
    )
    merged = (
        (self_out + cross_out)
        .astype(jnp.bfloat16)
        .transpose(2, 0, 1, 3)
        .reshape(1, tok_rows, heads_local * HD)
    )
    cot_rows = cotangent[0].reshape(tok_rows, kv_local, group_size, HD)
    grad_terms = jnp.einsum(
        "gcts,tgcd->sgd", cross_weights, cot_rows, preferred_element_type=jnp.float32
    ).reshape(key_count, kv_local * HD)
    value_grad = lax.psum_scatter(
        grad_terms.astype(jnp.bfloat16), "seq", scatter_dimension=0, tiled=True
    )
    own_features = features[0]
    summed_samples = lax.psum_scatter(
        lax.dot_general(
            own_features, value_grad, (((0,), (0,)), ((), ())), preferred_element_type=jnp.float32
        ).astype(jnp.bfloat16),
        "dp",
        scatter_dimension=0,
        tiled=True,
    )
    weight_grad = lax.psum_scatter(summed_samples, "seq", scatter_dimension=0, tiled=True).astype(
        jnp.float32
    )
    return (merged, weight_grad)


def dot_nt(left, right):
    return lax.dot_general(
        left, right, (((1,), (1,)), ((), ())), preferred_element_type=jnp.float32
    )


def dot_nn(left, right):
    return lax.dot_general(
        left, right, (((1,), (0,)), ((), ())), preferred_element_type=jnp.float32
    )


def dot_tn(left, right):
    return lax.dot_general(
        left, right, (((0,), (0,)), ((), ())), preferred_element_type=jnp.float32
    )


def stacked_heads(ref, group, group_size):
    first = group * group_size
    return jnp.concatenate(
        [ref[:, (first + c) * HD : (first + c + 1) * HD] for c in range(group_size)], axis=0
    )


def pack_kernel(
    sizes,
    docs_hbm,
    tiles_hbm,
    cite_hbm,
    img_hbm,
    features_hbm,
    k_hbm,
    v_hbm,
    head_ref,
    pack_ref,
    meta_ref,
    docs_ref,
    tiles_ref,
    cite_ref,
    sems,
):
    slots, parts, slot_count = sizes
    tok_rows = docs_ref.shape[1]
    width = pack_ref.shape[1]
    vision = features_hbm.shape[2]
    feature_rows = parts * slots
    pairs = [
        (docs_hbm, docs_ref),
        (tiles_hbm, tiles_ref),
        (cite_hbm, cite_ref),
        (img_hbm.at[0], head_ref.at[pl.ds(0, slots), :]),
        (k_hbm.at[0], pack_ref.at[pl.ds(feature_rows, tok_rows), :]),
        (v_hbm.at[0], pack_ref.at[pl.ds(feature_rows + tok_rows, tok_rows), :]),
    ]
    for part in range(parts):
        cut = min(width, vision - part * width)
        pairs.append(
            (
                features_hbm.at[0, :, pl.ds(part * width, cut)],
                pack_ref.at[pl.ds(part * slots, slots), pl.ds(0, cut)],
            )
        )
    copies = [
        pltpu.make_async_copy(source, target, sems.at[n])
        for n, (source, target) in enumerate(pairs)
    ]
    for copy in copies:
        copy.start()
    for copy in copies[:3]:
        copy.wait()
    docs = docs_ref[...]
    image_of = jnp.zeros_like(docs)
    for doc in range(cite_ref.shape[1]):
        image_of = jnp.where(docs == doc, cite_ref[0, doc], image_of)
    count = jnp.zeros_like(docs)
    for image in range(tiles_ref.shape[1]):
        count = jnp.where(image_of == image, tiles_ref[0, image] * TILE_TOK, count)
    first = image_of * slot_count
    row = lax.broadcasted_iota(jnp.int32, meta_ref.shape, 0)
    meta_ref[...] = jnp.where(
        row == 0, docs, jnp.where(row == 1, first, jnp.where(row == 2, first + count, 0))
    )
    extra = head_ref.shape[0] - slots
    doc_rows = jnp.broadcast_to(docs.astype(jnp.float32), (extra, tok_rows))
    head_ref[slots:, :tok_rows] = doc_rows.astype(jnp.bfloat16)
    if width > tok_rows:
        head_ref[slots:, tok_rows:] = jnp.zeros((extra, width - tok_rows), jnp.bfloat16)
    for copy in copies[3:]:
        copy.wait()
    last = vision - (parts - 1) * width
    if last < width:
        pack_ref[(parts - 1) * slots : feature_rows, last:] = jnp.zeros(
            (slots, width - last), jnp.bfloat16
        )


def cross_kernel(sizes, meta_ref, head_ref, q_ref, cot_ref, grad_ref, weights_ref):
    kv_local, group_size, slots = sizes
    blocks = head_ref.shape[0]
    key_count = blocks * slots
    tok_rows = q_ref.shape[0]
    slot_ids = lax.broadcasted_iota(jnp.int32, (key_count, tok_rows), 0)
    kept = (slot_ids >= meta_ref[1:2, :]) & (slot_ids < meta_ref[2:3, :])
    bias = jnp.where(kept, 0.0, MASK_FILL)
    bias = jnp.concatenate([bias] * group_size, axis=1)
    scale = HD ** (-0.5) * LOG2E
    for group in range(kv_local):
        columns = slice(group * HD, (group + 1) * HD)
        keys = jnp.concatenate([head_ref[b, :slots, columns] for b in range(blocks)], axis=0)
        scores = dot_nt(keys, stacked_heads(q_ref, group, group_size)) * scale + bias
        exps = jnp.exp2(scores - jnp.max(scores, axis=0, keepdims=True))
        inverse = 1.0 / jnp.sum(exps, axis=0, keepdims=True)
        weights = (exps * inverse).astype(jnp.bfloat16)
        weights_ref[group] = weights
        grad_ref[:, columns] = dot_nn(weights, stacked_heads(cot_ref, group, group_size)).astype(
            jnp.bfloat16
        )


def attend_kernel(sizes, where_ref, meta_ref, head_ref, q_ref, w_ref, weights_ref, *rest):
    kv_local, group_size, slots, feature_rows = sizes
    blocks = head_ref.shape[0]
    packs, out_ref, values_ref = rest[:blocks], rest[blocks], rest[blocks + 1]
    seq_at = where_ref[0]
    tok_rows = q_ref.shape[0]
    key_rows = (packs[0].shape[0] - feature_rows) // 2
    width = packs[0].shape[1]
    vision = w_ref.shape[0]
    parts = feature_rows // slots
    total = None
    for part in range(parts):
        cut = min(width, vision - part * width)
        rows = jnp.concatenate(
            [pack[part * slots : (part + 1) * slots, :cut] for pack in packs], axis=0
        )
        term = dot_nn(rows, w_ref[part * width : part * width + cut, :])
        total = term if total is None else total + term
    values = total.astype(jnp.bfloat16)
    for x in range(blocks):
        owner = pl.multiple_of((seq_at ^ x) * slots, slots)
        values_ref[pl.ds(owner, slots), :] = values[x * slots : (x + 1) * slots]
    docs = meta_ref[0:1, :].astype(jnp.float32)
    start = jnp.zeros((1, tok_rows), jnp.float32)
    for b in range(blocks):
        row = head_ref[b, slots : slots + 16, :tok_rows].astype(jnp.float32)[0:1]
        column = jnp.transpose(jnp.broadcast_to(row, (tok_rows, tok_rows)))
        start = start + jnp.sum(jnp.where(column < docs, 1.0, 0.0), axis=0, keepdims=True)
    start = start.astype(jnp.int32)
    query_pos = seq_at * tok_rows + lax.broadcasted_iota(jnp.int32, (1, tok_rows), 1)
    bias = []
    for x in range(blocks):
        key_pos = (seq_at ^ x) * key_rows + lax.broadcasted_iota(
            jnp.int32, (key_rows, tok_rows), 0
        )
        kept = (key_pos >= start) & (key_pos <= query_pos)
        bias.append(jnp.where(kept, 0.0, MASK_FILL))
    bias = jnp.concatenate(bias, axis=0)
    bias = jnp.concatenate([bias] * group_size, axis=1)
    scale = HD ** (-0.5) * LOG2E
    first_key, first_value = feature_rows, feature_rows + key_rows
    for group in range(kv_local):
        columns = slice(group * HD, (group + 1) * HD)
        keys = jnp.concatenate(
            [pack[first_key : first_key + key_rows, columns] for pack in packs], axis=0
        )
        vals = jnp.concatenate(
            [pack[first_value : first_value + key_rows, columns] for pack in packs], axis=0
        )
        scores = dot_nt(keys, stacked_heads(q_ref, group, group_size)) * scale + bias
        exps = jnp.exp2(scores - jnp.max(scores, axis=0, keepdims=True))
        inverse = 1.0 / jnp.sum(exps, axis=0, keepdims=True)
        self_out = dot_tn(vals, exps.astype(jnp.bfloat16)) * inverse
        cross_out = dot_tn(values_ref[:, columns], weights_ref[group])
        merged = (self_out + cross_out).astype(jnp.bfloat16)
        for c in range(group_size):
            head = group * group_size + c
            out_ref[:, head * HD : (head + 1) * HD] = jnp.transpose(
                merged[:, c * tok_rows : (c + 1) * tok_rows]
            )


def product_kernel(sizes, where_ref, terms_ref, *rest):
    slots, vision, out_rows, steps = sizes
    blocks = terms_ref.shape[0]
    packs, outs = rest[:blocks], rest[blocks : blocks + steps]
    sum_ref, turned_ref = rest[blocks + steps :]
    seq_at, dp_at = where_ref[0], where_ref[1]
    width = packs[0].shape[1]
    total = terms_ref[0].astype(jnp.float32)
    for b in range(1, blocks):
        total = total + terms_ref[b].astype(jnp.float32)
    sum_ref[...] = total.astype(jnp.bfloat16)
    grads = jnp.concatenate(
        [
            sum_ref[pl.ds(pl.multiple_of((seq_at ^ x) * slots, slots), slots), :]
            for x in range(blocks)
        ],
        axis=0,
    )
    for part in range(-(-vision // width)):
        cut = min(width, vision - part * width)
        rows = jnp.concatenate(
            [pack[part * slots : (part + 1) * slots, :cut] for pack in packs], axis=0
        )
        turned_ref[part * width : part * width + cut, :] = jnp.transpose(rows)
    for x in range(steps):
        row = pl.multiple_of(((dp_at ^ x) * blocks + seq_at) * out_rows, out_rows)
        block = dot_nn(turned_ref[pl.ds(row, out_rows), :], grads)
        outs[x][...] = block.astype(outs[x].dtype)


def vmem_specs(count):
    return [pl.BlockSpec(memory_space=pltpu.VMEM)] * count


def swap(array, axis, size, x):
    return lax.ppermute(array, axis, [(i, i ^ x) for i in range(size)])


def on_device_small(
    seq_size,
    dp_size,
    q_self,
    k_self,
    v_self,
    docs,
    q_cross,
    cotangent,
    img_keys,
    features,
    w_value,
    tiles,
    cite,
):
    tok_rows = q_self.shape[1]
    width = k_self.shape[2]
    kv_local = width // HD
    heads_local = q_self.shape[2] // HD
    group_size = heads_local // kv_local
    slots = img_keys.shape[1]
    vision = features.shape[2]
    images = tiles.shape[1]
    out_rows = vision // (seq_size * dp_size)
    key_count = slots * seq_size
    smem = pl.BlockSpec(memory_space=pltpu.SMEM)
    hbm = pl.BlockSpec(memory_space=pltpu.HBM)
    where_at = jnp.stack([lax.axis_index("seq"), lax.axis_index("dp")]).astype(jnp.int32)
    parts = -(-vision // width)
    feature_rows = parts * slots

    head, own, meta = pl.pallas_call(
        functools.partial(pack_kernel, (slots, parts, key_count // images)),
        out_shape=(
            jax.ShapeDtypeStruct((slots + 16, width), jnp.bfloat16),
            jax.ShapeDtypeStruct((feature_rows + 2 * tok_rows, width), jnp.bfloat16),
            jax.ShapeDtypeStruct((8, tok_rows), jnp.int32),
        ),
        in_specs=[hbm] * 7,
        out_specs=tuple(vmem_specs(3)),
        scratch_shapes=[
            pltpu.VMEM(docs.shape, jnp.int32),
            pltpu.SMEM(tiles.shape, jnp.int32),
            pltpu.SMEM(cite.shape, jnp.int32),
            pltpu.SemaphoreType.DMA((6 + parts,)),
        ],
        compiler_params=pltpu.CompilerParams(vmem_limit_bytes=8 << 20),
        cost_estimate=pl.CostEstimate(flops=4 << 30, bytes_accessed=16 << 20, transcendentals=0),
        name="pack",
    )(*[pltpu.with_memory_space_constraint(a, pltpu.HBM) for a in (docs, tiles, cite, img_keys, features, k_self, v_self)])
    heads_all = lax.all_gather(head, "seq", axis=0)
    bit = seq_size // 2
    order = {0: own}
    while bit:
        for x in list(order):
            order[x ^ bit] = swap(order[x], "seq", seq_size, bit)
        bit //= 2
    packs = [order[x] for x in range(seq_size)]

    grad_terms, weights = pl.pallas_call(
        functools.partial(cross_kernel, (kv_local, group_size, slots)),
        out_shape=(
            jax.ShapeDtypeStruct((key_count, width), jnp.bfloat16),
            jax.ShapeDtypeStruct((kv_local, key_count, group_size * tok_rows), jnp.bfloat16),
        ),
        in_specs=vmem_specs(4),
        out_specs=tuple(vmem_specs(2)),
        compiler_params=pltpu.CompilerParams(vmem_limit_bytes=24 << 20),
        name="cross",
    )(meta, heads_all, q_cross[0], cotangent[0])
    terms_all = lax.all_gather(grad_terms, "seq", axis=0)
    blocks_out = pl.pallas_call(
        functools.partial(product_kernel, (slots, vision, out_rows, dp_size)),
        out_shape=tuple(
            jax.ShapeDtypeStruct((out_rows, width), jnp.bfloat16 if x else jnp.float32)
            for x in range(dp_size)
        ),
        in_specs=[smem] + vmem_specs(1 + seq_size),
        out_specs=tuple(vmem_specs(dp_size)),
        scratch_shapes=[
            pltpu.VMEM((key_count, width), jnp.bfloat16),
            pltpu.VMEM((vision, key_count), jnp.bfloat16),
        ],
        compiler_params=pltpu.CompilerParams(vmem_limit_bytes=16 << 20),
        name="product",
    )(where_at, terms_all, *packs)
    arrived = []
    for x in range(dp_size - 1, 0, -1):
        arrived.append(swap(blocks_out[x], "dp", dp_size, x))
    weight_grad = blocks_out[0]
    for block in arrived:
        weight_grad = weight_grad + block.astype(jnp.float32)

    merged = pl.pallas_call(
        functools.partial(attend_kernel, (kv_local, group_size, slots, feature_rows)),
        out_shape=jax.ShapeDtypeStruct((tok_rows, heads_local * HD), jnp.bfloat16),
        in_specs=[smem] + vmem_specs(5 + seq_size),
        out_specs=vmem_specs(1)[0],
        scratch_shapes=[pltpu.VMEM((key_count, width), jnp.bfloat16)],
        compiler_params=pltpu.CompilerParams(vmem_limit_bytes=32 << 20),
        name="attend",
    )(where_at, meta, heads_all, q_self[0], w_value, weights, *packs)
    return (merged[None], weight_grad)


def fits_small(mesh, shapes):
    seq_size, dp_size = mesh.shape["seq"], mesh.shape["dp"]
    q_self, k_self, img_keys, features, _, cite = shapes
    tensor = mesh.shape["tensor"]
    powers = all(n & (n - 1) == 0 for n in (seq_size, dp_size))
    tok_rows, width = q_self[1] // seq_size, k_self[2] // tensor
    slots = img_keys[1] // seq_size
    rows, left = divmod(features[2], seq_size * dp_size)
    return (
        powers
        and seq_size <= 4
        and dp_size <= 8
        and tok_rows == HD
        and tok_rows <= width
        and slots % 32 == 0
        and slots * seq_size == HD
        and left == 0
        and rows % 16 == 0
        and features[2] % HD == 0
        and width % HD == 0
        and cite[1] <= 256
    )


def solution(mesh):
    in_specs = (
        P("dp", "seq", "tensor"),
        P("dp", "seq", "tensor"),
        P("dp", "seq", "tensor"),
        P("dp", "seq"),
        P("dp", "seq", "tensor"),
        P("dp", "seq", "tensor"),
        P("dp", "seq", "tensor"),
        P("dp", "seq", None),
        P(None, "tensor"),
        P("dp", None),
        P("dp", None),
    )
    out_specs = (P("dp", "seq", "tensor"), P(("dp", "seq"), "tensor"))

    def run(*arrays):
        shapes = [arrays[i].shape for i in (0, 1, 6, 7, 8, 10)]
        body = on_device_general
        if fits_small(mesh, shapes):
            body = functools.partial(on_device_small, mesh.shape["seq"], mesh.shape["dp"])
        return jax.shard_map(
            body, mesh=mesh, in_specs=in_specs, out_specs=out_specs, check_vma=False
        )(*arrays)

    return run
```

```python
import functools
import math

import jax
import jax.numpy as jnp
from jax import lax
from jax.experimental import pallas as pl
from jax.experimental.pallas import tpu as pltpu
from jax.sharding import PartitionSpec as P


HD = 128
TILE_TOK = 8


MASK_FILL = -1e30
LOG2E = math.log2(math.e)


def absorb_block(
    running, queries, key_rows, value_rows, key_docs, key_pos, query_pos, my_docs, score_scale
):
    running_max, denominator, numerator = running
    kv_local = queries.shape[1]
    key_count = key_rows.shape[0]
    key_heads = key_rows.reshape(key_count, kv_local, HD)
    value_heads = value_rows.reshape(key_count, kv_local, HD)
    scores = (
        jnp.einsum("tgcd,sgd->gcts", queries, key_heads, preferred_element_type=jnp.float32)
        * score_scale
    )
    kept = (query_pos[:, None] >= key_pos[None, :]) & (my_docs[:, None] == key_docs[None, :])
    scores = jnp.where(kept, scores, MASK_FILL)
    new_max = jnp.maximum(running_max, jnp.max(scores, axis=-1))
    factor = jnp.exp(running_max - new_max)
    weights = jnp.where(kept, jnp.exp(scores - new_max[..., None]), 0.0)
    denominator = factor * denominator + jnp.sum(weights, axis=-1)
    numerator = factor[..., None] * numerator + jnp.einsum(
        "gcts,sgd->gctd",
        weights.astype(jnp.bfloat16),
        value_heads,
        preferred_element_type=jnp.float32,
    )
    return (new_max, denominator, numerator)


def on_device_general(
    q_self, k_self, v_self, docs, q_cross, cotangent, img_keys, features, w_value, tiles, cite
):
    tok_rows = q_self.shape[1]
    kv_local = k_self.shape[2] // HD
    heads_local = q_self.shape[2] // HD
    group_size = heads_local // kv_local
    score_scale = HD ** (-0.5)
    first_row = lax.axis_index("seq") * tok_rows
    query_pos = first_row + jnp.arange(tok_rows, dtype=jnp.int32)
    my_docs = docs[0]
    queries = q_self[0].reshape(tok_rows, kv_local, group_size, HD)
    start_state = (
        jnp.full((kv_local, group_size, tok_rows), MASK_FILL, jnp.float32),
        jnp.zeros((kv_local, group_size, tok_rows), jnp.float32),
        jnp.zeros((kv_local, group_size, tok_rows, HD), jnp.float32),
    )
    piece_keys = lax.all_gather(k_self, "seq", axis=1, tiled=True)
    piece_values = lax.all_gather(v_self, "seq", axis=1, tiled=True)
    piece_docs = lax.all_gather(docs, "seq", axis=1, tiled=True)
    key_count = piece_keys.shape[1]
    block_rows = math.gcd(key_count, 512)
    block_count = key_count // block_rows
    key_blocks = piece_keys[0].reshape(block_count, block_rows, -1)
    value_blocks = piece_values[0].reshape(block_count, block_rows, -1)
    doc_blocks = piece_docs[0].reshape(block_count, block_rows)
    pos_blocks = jnp.arange(key_count, dtype=jnp.int32).reshape(block_count, block_rows)

    def absorb_step(state_now, block_item):
        key_part, value_part, doc_part, pos_part = block_item
        return (
            absorb_block(
                state_now,
                queries,
                key_part,
                value_part,
                doc_part,
                pos_part,
                query_pos,
                my_docs,
                score_scale,
            ),
            None,
        )

    _, denominator, numerator = lax.scan(
        absorb_step, start_state, (key_blocks, value_blocks, doc_blocks, pos_blocks)
    )[0]
    self_out = numerator / denominator[..., None]
    values_own = jnp.dot(features[0], w_value, preferred_element_type=jnp.float32).astype(
        jnp.bfloat16
    )
    image_keys, image_values = (
        lax.all_gather(img_keys[0], "seq", axis=0, tiled=True),
        lax.all_gather(values_own, "seq", axis=0, tiled=True),
    )
    key_count = image_keys.shape[0]
    image_count = tiles.shape[1]
    slot_count = key_count // image_count
    doc_hit = my_docs[:, None] == jnp.arange(cite.shape[1], dtype=jnp.int32)[None, :]
    image_of = jnp.sum(jnp.where(doc_hit, cite[0][None, :], 0), axis=1)
    slot_ids = jnp.arange(key_count, dtype=jnp.int32)
    key_image = slot_ids // slot_count
    owner_hit = key_image[:, None] == jnp.arange(image_count, dtype=jnp.int32)[None, :]
    tile_limit = jnp.sum(jnp.where(owner_hit, tiles[0][None, :], 0), axis=1) * TILE_TOK
    cross_kept = (image_of[:, None] == key_image[None, :]) & (slot_ids % slot_count < tile_limit)[
        None, :
    ]
    cross_q = q_cross[0].reshape(tok_rows, kv_local, group_size, HD)
    cross_scores = (
        jnp.einsum(
            "tgcd,sgd->gcts",
            cross_q,
            image_keys.reshape(key_count, kv_local, HD),
            preferred_element_type=jnp.float32,
        )
        * score_scale
    )
    cross_scores = jnp.where(cross_kept, cross_scores, MASK_FILL)
    cross_exp = jnp.where(
        cross_kept, jnp.exp(cross_scores - jnp.max(cross_scores, axis=-1, keepdims=True)), 0.0
    )
    cross_weights = (cross_exp / jnp.sum(cross_exp, axis=-1, keepdims=True)).astype(jnp.bfloat16)
    cross_out = jnp.einsum(
        "gcts,sgd->gctd",
        cross_weights,
        image_values.reshape(key_count, kv_local, HD),
        preferred_element_type=jnp.float32,
    )
    merged = (
        (self_out + cross_out)
        .astype(jnp.bfloat16)
        .transpose(2, 0, 1, 3)
        .reshape(1, tok_rows, heads_local * HD)
    )
    cot_rows = cotangent[0].reshape(tok_rows, kv_local, group_size, HD)
    grad_terms = jnp.einsum(
        "gcts,tgcd->sgd", cross_weights, cot_rows, preferred_element_type=jnp.float32
    ).reshape(key_count, kv_local * HD)
    value_grad = lax.psum_scatter(
        grad_terms.astype(jnp.bfloat16), "seq", scatter_dimension=0, tiled=True
    )
    own_features = features[0]
    summed_samples = lax.psum_scatter(
        lax.dot_general(
            own_features, value_grad, (((0,), (0,)), ((), ())), preferred_element_type=jnp.float32
        ).astype(jnp.bfloat16),
        "dp",
        scatter_dimension=0,
        tiled=True,
    )
    weight_grad = lax.psum_scatter(summed_samples, "seq", scatter_dimension=0, tiled=True).astype(
        jnp.float32
    )
    return (merged, weight_grad)


def dot_nt(left, right):
    return lax.dot_general(
        left, right, (((1,), (1,)), ((), ())), preferred_element_type=jnp.float32
    )


def dot_nn(left, right):
    return lax.dot_general(
        left, right, (((1,), (0,)), ((), ())), preferred_element_type=jnp.float32
    )


def dot_tn(left, right):
    return lax.dot_general(
        left, right, (((0,), (0,)), ((), ())), preferred_element_type=jnp.float32
    )


def stacked_heads(ref, group, group_size):
    first = group * group_size
    return jnp.concatenate(
        [ref[:, (first + c) * HD : (first + c + 1) * HD] for c in range(group_size)], axis=0
    )


def pack_kernel(
    sizes,
    docs_hbm,
    tiles_hbm,
    cite_hbm,
    img_hbm,
    features_hbm,
    k_hbm,
    v_hbm,
    keys_ref,
    rows_ref,
    kv_ref,
    all_ref,
    meta_ref,
    docs_ref,
    tiles_ref,
    cite_ref,
    sems,
):
    slots, parts, slot_count = sizes
    tok_rows = docs_ref.shape[1]
    width = keys_ref.shape[1]
    vision = features_hbm.shape[2]
    feature_rows = parts * slots
    pairs = [(docs_hbm, docs_ref), (tiles_hbm, tiles_ref), (cite_hbm, cite_ref)]
    places = ((keys_ref, rows_ref, kv_ref, 0, 0, 0),)
    places += ((all_ref, all_ref, all_ref, 0, slots, slots + feature_rows),)
    for keys_to, rows_to, kv_to, keys_at, rows_at, kv_at in places:
        pairs.append((img_hbm.at[0], keys_to.at[pl.ds(keys_at, slots), :]))
        for part in range(parts):
            cut = min(width, vision - part * width)
            pairs.append(
                (
                    features_hbm.at[0, :, pl.ds(part * width, cut)],
                    rows_to.at[pl.ds(rows_at + part * slots, slots), pl.ds(0, cut)],
                )
            )
        pairs.append((k_hbm.at[0], kv_to.at[pl.ds(kv_at, tok_rows), :]))
        pairs.append((v_hbm.at[0], kv_to.at[pl.ds(kv_at + tok_rows, tok_rows), :]))
    copies = [
        pltpu.make_async_copy(source, target, sems.at[n])
        for n, (source, target) in enumerate(pairs)
    ]
    for copy in copies:
        copy.start()
    for copy in copies[:3]:
        copy.wait()
    docs = docs_ref[...]
    image_of = jnp.zeros_like(docs)
    for doc in range(cite_ref.shape[1]):
        image_of = jnp.where(docs == doc, cite_ref[0, doc], image_of)
    count = jnp.zeros_like(docs)
    for image in range(tiles_ref.shape[1]):
        count = jnp.where(image_of == image, tiles_ref[0, image] * TILE_TOK, count)
    first = image_of * slot_count
    row = lax.broadcasted_iota(jnp.int32, meta_ref.shape, 0)
    meta_ref[...] = jnp.where(
        row == 0, docs, jnp.where(row == 1, first, jnp.where(row == 2, first + count, 0))
    )
    doc_rows = jnp.broadcast_to(docs.astype(jnp.float32), (slots, tok_rows))
    spare = jnp.zeros((slots, parts * width - vision - tok_rows), jnp.float32)
    tail = jnp.concatenate([doc_rows, spare], axis=1).astype(jnp.bfloat16)
    for copy in copies[3:]:
        copy.wait()
    last = vision - (parts - 1) * width
    rows_ref[feature_rows - slots : feature_rows, last:] = tail
    all_ref[feature_rows : feature_rows + slots, last:] = tail


def cross_kernel(sizes, meta_ref, q_ref, cot_ref, *rest):
    kv_local, group_size, slots, blocks = sizes
    key_refs = rest[:blocks]
    grad_ref, weights_ref = rest[blocks:]
    seq_at = lax.axis_index("seq")
    tok_rows = q_ref.shape[0]
    bias = []
    for x in range(blocks):
        slot_ids = (seq_at ^ x) * slots + lax.broadcasted_iota(jnp.int32, (slots, tok_rows), 0)
        kept = (slot_ids >= meta_ref[1:2, :]) & (slot_ids < meta_ref[2:3, :])
        bias.append(jnp.where(kept, 0.0, MASK_FILL))
    bias = jnp.concatenate(bias, axis=0)
    bias = jnp.concatenate([bias] * group_size, axis=1)
    scale = HD ** (-0.5) * LOG2E
    for group in range(kv_local):
        columns = slice(group * HD, (group + 1) * HD)
        keys = jnp.concatenate([ref[:slots, columns] for ref in key_refs], axis=0)
        scores = dot_nt(keys, stacked_heads(q_ref, group, group_size)) * scale + bias
        exps = jnp.exp2(scores - jnp.max(scores, axis=0, keepdims=True))
        inverse = 1.0 / jnp.sum(exps, axis=0, keepdims=True)
        weights = (exps * inverse).astype(jnp.bfloat16)
        weights_ref[group] = weights
        grads = dot_nn(weights, stacked_heads(cot_ref, group, group_size)).astype(jnp.bfloat16)
        for x in range(blocks):
            at = pl.multiple_of((seq_at ^ x) * slots, slots)
            grad_ref[pl.ds(at, slots), columns] = grads[x * slots : (x + 1) * slots]


def stacked_features(rows, part, slots, cut):
    return jnp.concatenate(
        [ref[first + part * slots : first + (part + 1) * slots, :cut] for ref, first in rows],
        axis=0,
    )


def attend_kernel(sizes, meta_ref, q_ref, w_ref, weights_ref, *rest):
    kv_local, group_size, slots, parts, row_firsts, kv_firsts = sizes
    blocks = len(row_firsts)
    out_ref = rest[-1]
    rows = list(zip(rest[:blocks], row_firsts))
    pairs = list(zip(rest[blocks : 2 * blocks], kv_firsts))
    seq_at = lax.axis_index("seq")
    tok_rows = q_ref.shape[0]
    width = pairs[0][0].shape[1]
    vision = w_ref.shape[0]
    total = None
    for part in range(parts):
        cut = min(width, vision - part * width)
        term = dot_nn(
            stacked_features(rows, part, slots, cut), w_ref[part * width : part * width + cut, :]
        )
        total = term if total is None else total + term
    values = total.astype(jnp.bfloat16)
    last = vision - (parts - 1) * width
    docs = meta_ref[0:1, :].astype(jnp.float32)
    start = jnp.zeros((1, tok_rows), jnp.float32)
    for ref, first in rows:
        at = first + (parts - 1) * slots
        row = ref[at : at + 16, last : last + tok_rows].astype(jnp.float32)[0:1]
        column = jnp.transpose(jnp.broadcast_to(row, (tok_rows, tok_rows)))
        start = start + jnp.sum(jnp.where(column < docs, 1.0, 0.0), axis=0, keepdims=True)
    start = start.astype(jnp.int32)
    query_pos = seq_at * tok_rows + lax.broadcasted_iota(jnp.int32, (1, tok_rows), 1)
    bias = []
    for x in range(blocks):
        key_pos = (seq_at ^ x) * tok_rows + lax.broadcasted_iota(
            jnp.int32, (tok_rows, tok_rows), 0
        )
        kept = (key_pos >= start) & (key_pos <= query_pos)
        bias.append(jnp.where(kept, 0.0, MASK_FILL))
    bias = jnp.concatenate(bias, axis=0)
    bias = jnp.concatenate([bias] * group_size, axis=1)
    scale = HD ** (-0.5) * LOG2E
    for group in range(kv_local):
        columns = slice(group * HD, (group + 1) * HD)
        keys = jnp.concatenate([r[f : f + tok_rows, columns] for r, f in pairs], axis=0)
        vals = jnp.concatenate(
            [r[f + tok_rows : f + 2 * tok_rows, columns] for r, f in pairs], axis=0
        )
        scores = dot_nt(keys, stacked_heads(q_ref, group, group_size)) * scale + bias
        exps = jnp.exp2(scores - jnp.max(scores, axis=0, keepdims=True))
        inverse = 1.0 / jnp.sum(exps, axis=0, keepdims=True)
        self_out = dot_tn(vals, exps.astype(jnp.bfloat16)) * inverse
        cross_out = dot_tn(values[:, columns], weights_ref[group])
        merged = (self_out + cross_out).astype(jnp.bfloat16)
        for c in range(group_size):
            head = group * group_size + c
            out_ref[:, head * HD : (head + 1) * HD] = jnp.transpose(
                merged[:, c * tok_rows : (c + 1) * tok_rows]
            )


def product_kernel(sizes, terms_ref, *rest):
    slots, vision, out_rows, steps, parts, row_firsts = sizes
    blocks = len(row_firsts)
    rows, outs = list(zip(rest[:blocks], row_firsts)), rest[blocks : blocks + steps]
    sum_ref, turned_ref = rest[blocks + steps :]
    seq_at, dp_at = lax.axis_index("seq"), lax.axis_index("dp")
    width = terms_ref.shape[2]
    total = terms_ref[0].astype(jnp.float32)
    for b in range(1, blocks):
        total = total + terms_ref[b].astype(jnp.float32)
    sum_ref[...] = total.astype(jnp.bfloat16)
    grads = jnp.concatenate(
        [
            sum_ref[pl.ds(pl.multiple_of((seq_at ^ x) * slots, slots), slots), :]
            for x in range(blocks)
        ],
        axis=0,
    )
    for part in range(parts):
        cut = min(width, vision - part * width)
        turned_ref[part * width : part * width + cut, :] = jnp.transpose(
            stacked_features(rows, part, slots, cut)
        )
    for x in range(steps):
        row = pl.multiple_of(((dp_at ^ x) * blocks + seq_at) * out_rows, out_rows)
        block = dot_nn(turned_ref[pl.ds(row, out_rows), :], grads)
        outs[x][...] = block.astype(outs[x].dtype)


def vmem_specs(count):
    return [pl.BlockSpec(memory_space=pltpu.VMEM)] * count


def swap(array, axis, size, x):
    return lax.ppermute(array, axis, [(i, i ^ x) for i in range(size)])


def on_device_small(
    seq_size,
    dp_size,
    q_self,
    k_self,
    v_self,
    docs,
    q_cross,
    cotangent,
    img_keys,
    features,
    w_value,
    tiles,
    cite,
):
    tok_rows = q_self.shape[1]
    width = k_self.shape[2]
    kv_local = width // HD
    heads_local = q_self.shape[2] // HD
    group_size = heads_local // kv_local
    slots = img_keys.shape[1]
    vision = features.shape[2]
    images = tiles.shape[1]
    out_rows = vision // (seq_size * dp_size)
    key_count = slots * seq_size
    hbm = pl.BlockSpec(memory_space=pltpu.HBM)
    parts = -(-vision // width)
    feature_rows = parts * slots
    kv_rows = 2 * tok_rows
    all_rows = slots + feature_rows + kv_rows

    keys_own, rows_own, kv_own, all_own, meta = pl.pallas_call(
        functools.partial(pack_kernel, (slots, parts, key_count // images)),
        out_shape=tuple(
            jax.ShapeDtypeStruct((rows, width), jnp.bfloat16)
            for rows in (slots, feature_rows, kv_rows, all_rows)
        )
        + (jax.ShapeDtypeStruct((8, tok_rows), jnp.int32),),
        in_specs=[hbm] * 7,
        out_specs=tuple(vmem_specs(5)),
        scratch_shapes=[
            pltpu.VMEM(docs.shape, jnp.int32),
            pltpu.SMEM(tiles.shape, jnp.int32),
            pltpu.SMEM(cite.shape, jnp.int32),
            pltpu.SemaphoreType.DMA((9 + 2 * parts,)),
        ],
        compiler_params=pltpu.CompilerParams(vmem_limit_bytes=8 << 20),
        cost_estimate=pl.CostEstimate(flops=4 << 30, bytes_accessed=16 << 20, transcendentals=0),
        name="pack",
    )(
        *[
            pltpu.with_memory_space_constraint(array, pltpu.HBM)
            for array in (docs, tiles, cite, img_keys, features, k_self, v_self)
        ]
    )
    far, near = seq_size // 2, 1

    def far_and_across(array):
        there = swap(array, "seq", seq_size, far)
        return there, swap(there, "seq", seq_size, near)

    keys_far, keys_across = far_and_across(keys_own)
    rows_far, rows_across = far_and_across(rows_own)
    kv_far, kv_across = far_and_across(kv_own)
    all_near = swap(all_own, "seq", seq_size, near)
    key_blocks = (all_own, all_near, keys_far, keys_across)
    row_blocks = (all_own, all_near, rows_far, rows_across)
    kv_blocks = (all_own, all_near, kv_far, kv_across)
    row_firsts = (slots, slots, 0, 0)
    kv_firsts = (slots + feature_rows, slots + feature_rows, 0, 0)

    grad_terms, weights = pl.pallas_call(
        functools.partial(cross_kernel, (kv_local, group_size, slots, seq_size)),
        out_shape=(
            jax.ShapeDtypeStruct((key_count, width), jnp.bfloat16),
            jax.ShapeDtypeStruct((kv_local, key_count, group_size * tok_rows), jnp.bfloat16),
        ),
        in_specs=vmem_specs(3 + seq_size),
        out_specs=tuple(vmem_specs(2)),
        compiler_params=pltpu.CompilerParams(vmem_limit_bytes=24 << 20),
        name="cross",
    )(meta, q_cross[0], cotangent[0], *key_blocks)
    terms_all = lax.all_gather(grad_terms, "seq", axis=0)
    blocks_out = pl.pallas_call(
        functools.partial(product_kernel, (slots, vision, out_rows, dp_size, parts, row_firsts)),
        out_shape=tuple(
            jax.ShapeDtypeStruct((out_rows, width), jnp.bfloat16 if x else jnp.float32)
            for x in range(dp_size)
        ),
        in_specs=vmem_specs(1 + seq_size),
        out_specs=tuple(vmem_specs(dp_size)),
        scratch_shapes=[
            pltpu.VMEM((key_count, width), jnp.bfloat16),
            pltpu.VMEM((vision, key_count), jnp.bfloat16),
        ],
        compiler_params=pltpu.CompilerParams(vmem_limit_bytes=16 << 20),
        name="product",
    )(terms_all, *row_blocks)
    arrived = []
    for x in range(dp_size - 1, 0, -1):
        arrived.append(swap(blocks_out[x], "dp", dp_size, x))
    weight_grad = blocks_out[0]
    for block in arrived:
        weight_grad = weight_grad + block.astype(jnp.float32)

    merged = pl.pallas_call(
        functools.partial(
            attend_kernel, (kv_local, group_size, slots, parts, row_firsts, kv_firsts)
        ),
        out_shape=jax.ShapeDtypeStruct((tok_rows, heads_local * HD), jnp.bfloat16),
        in_specs=vmem_specs(4 + 2 * seq_size),
        out_specs=vmem_specs(1)[0],
        compiler_params=pltpu.CompilerParams(vmem_limit_bytes=32 << 20),
        name="attend",
    )(meta, q_self[0], w_value, weights, *row_blocks, *kv_blocks)
    return (merged[None], weight_grad)


def fits_small(mesh, shapes):
    seq_size, dp_size = mesh.shape["seq"], mesh.shape["dp"]
    q_self, k_self, img_keys, features, _, cite = shapes
    tensor = mesh.shape["tensor"]
    powers = all(n & (n - 1) == 0 for n in (seq_size, dp_size))
    tok_rows, width = q_self[1] // seq_size, k_self[2] // tensor
    slots = img_keys[1] // seq_size
    rows, left = divmod(features[2], seq_size * dp_size)
    return (
        powers
        and seq_size == 4
        and dp_size <= 8
        and tok_rows == HD
        and tok_rows <= width
        and slots % 32 == 0
        and slots * seq_size == HD
        and left == 0
        and rows % 16 == 0
        and features[2] % HD == 0
        and width % HD == 0
        and -features[2] % width >= tok_rows
        and cite[1] <= 256
    )


def solution(mesh):
    in_specs = (
        P("dp", "seq", "tensor"),
        P("dp", "seq", "tensor"),
        P("dp", "seq", "tensor"),
        P("dp", "seq"),
        P("dp", "seq", "tensor"),
        P("dp", "seq", "tensor"),
        P("dp", "seq", "tensor"),
        P("dp", "seq", None),
        P(None, "tensor"),
        P("dp", None),
        P("dp", None),
    )
    out_specs = (P("dp", "seq", "tensor"), P(("dp", "seq"), "tensor"))

    def run(*arrays):
        shapes = [arrays[i].shape for i in (0, 1, 6, 7, 8, 10)]
        body = on_device_general
        if fits_small(mesh, shapes):
            body = functools.partial(on_device_small, mesh.shape["seq"], mesh.shape["dp"])
        return jax.shard_map(
            body, mesh=mesh, in_specs=in_specs, out_specs=out_specs, check_vma=False
        )(*arrays)

    return run
```

```python
import functools
import math

import jax
import jax.numpy as jnp
from jax import lax
from jax.experimental import pallas as pl
from jax.experimental.pallas import tpu as pltpu
from jax.sharding import PartitionSpec as P


HD = 128
TILE_TOK = 8


MASK_FILL = -1e30
LOG2E = math.log2(math.e)


def absorb_block(
    running, queries, key_rows, value_rows, key_docs, key_pos, query_pos, my_docs, score_scale
):
    running_max, denominator, numerator = running
    kv_local = queries.shape[1]
    key_count = key_rows.shape[0]
    key_heads = key_rows.reshape(key_count, kv_local, HD)
    value_heads = value_rows.reshape(key_count, kv_local, HD)
    scores = (
        jnp.einsum("tgcd,sgd->gcts", queries, key_heads, preferred_element_type=jnp.float32)
        * score_scale
    )
    kept = (query_pos[:, None] >= key_pos[None, :]) & (my_docs[:, None] == key_docs[None, :])
    scores = jnp.where(kept, scores, MASK_FILL)
    new_max = jnp.maximum(running_max, jnp.max(scores, axis=-1))
    factor = jnp.exp(running_max - new_max)
    weights = jnp.where(kept, jnp.exp(scores - new_max[..., None]), 0.0)
    denominator = factor * denominator + jnp.sum(weights, axis=-1)
    numerator = factor[..., None] * numerator + jnp.einsum(
        "gcts,sgd->gctd",
        weights.astype(jnp.bfloat16),
        value_heads,
        preferred_element_type=jnp.float32,
    )
    return (new_max, denominator, numerator)


def on_device_general(
    q_self, k_self, v_self, docs, q_cross, cotangent, img_keys, features, w_value, tiles, cite
):
    tok_rows = q_self.shape[1]
    kv_local = k_self.shape[2] // HD
    heads_local = q_self.shape[2] // HD
    group_size = heads_local // kv_local
    score_scale = HD ** (-0.5)
    first_row = lax.axis_index("seq") * tok_rows
    query_pos = first_row + jnp.arange(tok_rows, dtype=jnp.int32)
    my_docs = docs[0]
    queries = q_self[0].reshape(tok_rows, kv_local, group_size, HD)
    start_state = (
        jnp.full((kv_local, group_size, tok_rows), MASK_FILL, jnp.float32),
        jnp.zeros((kv_local, group_size, tok_rows), jnp.float32),
        jnp.zeros((kv_local, group_size, tok_rows, HD), jnp.float32),
    )
    piece_keys = lax.all_gather(k_self, "seq", axis=1, tiled=True)
    piece_values = lax.all_gather(v_self, "seq", axis=1, tiled=True)
    piece_docs = lax.all_gather(docs, "seq", axis=1, tiled=True)
    key_count = piece_keys.shape[1]
    block_rows = math.gcd(key_count, 512)
    block_count = key_count // block_rows
    key_blocks = piece_keys[0].reshape(block_count, block_rows, -1)
    value_blocks = piece_values[0].reshape(block_count, block_rows, -1)
    doc_blocks = piece_docs[0].reshape(block_count, block_rows)
    pos_blocks = jnp.arange(key_count, dtype=jnp.int32).reshape(block_count, block_rows)

    def absorb_step(state_now, block_item):
        key_part, value_part, doc_part, pos_part = block_item
        return (
            absorb_block(
                state_now,
                queries,
                key_part,
                value_part,
                doc_part,
                pos_part,
                query_pos,
                my_docs,
                score_scale,
            ),
            None,
        )

    _, denominator, numerator = lax.scan(
        absorb_step, start_state, (key_blocks, value_blocks, doc_blocks, pos_blocks)
    )[0]
    self_out = numerator / denominator[..., None]
    values_own = jnp.dot(features[0], w_value, preferred_element_type=jnp.float32).astype(
        jnp.bfloat16
    )
    image_keys, image_values = (
        lax.all_gather(img_keys[0], "seq", axis=0, tiled=True),
        lax.all_gather(values_own, "seq", axis=0, tiled=True),
    )
    key_count = image_keys.shape[0]
    image_count = tiles.shape[1]
    slot_count = key_count // image_count
    doc_hit = my_docs[:, None] == jnp.arange(cite.shape[1], dtype=jnp.int32)[None, :]
    image_of = jnp.sum(jnp.where(doc_hit, cite[0][None, :], 0), axis=1)
    slot_ids = jnp.arange(key_count, dtype=jnp.int32)
    key_image = slot_ids // slot_count
    owner_hit = key_image[:, None] == jnp.arange(image_count, dtype=jnp.int32)[None, :]
    tile_limit = jnp.sum(jnp.where(owner_hit, tiles[0][None, :], 0), axis=1) * TILE_TOK
    cross_kept = (image_of[:, None] == key_image[None, :]) & (slot_ids % slot_count < tile_limit)[
        None, :
    ]
    cross_q = q_cross[0].reshape(tok_rows, kv_local, group_size, HD)
    cross_scores = (
        jnp.einsum(
            "tgcd,sgd->gcts",
            cross_q,
            image_keys.reshape(key_count, kv_local, HD),
            preferred_element_type=jnp.float32,
        )
        * score_scale
    )
    cross_scores = jnp.where(cross_kept, cross_scores, MASK_FILL)
    cross_exp = jnp.where(
        cross_kept, jnp.exp(cross_scores - jnp.max(cross_scores, axis=-1, keepdims=True)), 0.0
    )
    cross_weights = (cross_exp / jnp.sum(cross_exp, axis=-1, keepdims=True)).astype(jnp.bfloat16)
    cross_out = jnp.einsum(
        "gcts,sgd->gctd",
        cross_weights,
        image_values.reshape(key_count, kv_local, HD),
        preferred_element_type=jnp.float32,
    )
    merged = (
        (self_out + cross_out)
        .astype(jnp.bfloat16)
        .transpose(2, 0, 1, 3)
        .reshape(1, tok_rows, heads_local * HD)
    )
    cot_rows = cotangent[0].reshape(tok_rows, kv_local, group_size, HD)
    grad_terms = jnp.einsum(
        "gcts,tgcd->sgd", cross_weights, cot_rows, preferred_element_type=jnp.float32
    ).reshape(key_count, kv_local * HD)
    value_grad = lax.psum_scatter(
        grad_terms.astype(jnp.bfloat16), "seq", scatter_dimension=0, tiled=True
    )
    own_features = features[0]
    summed_samples = lax.psum_scatter(
        lax.dot_general(
            own_features, value_grad, (((0,), (0,)), ((), ())), preferred_element_type=jnp.float32
        ).astype(jnp.bfloat16),
        "dp",
        scatter_dimension=0,
        tiled=True,
    )
    weight_grad = lax.psum_scatter(summed_samples, "seq", scatter_dimension=0, tiled=True).astype(
        jnp.float32
    )
    return (merged, weight_grad)


def dot_nt(left, right):
    return lax.dot_general(
        left, right, (((1,), (1,)), ((), ())), preferred_element_type=jnp.float32
    )


def dot_nn(left, right):
    return lax.dot_general(
        left, right, (((1,), (0,)), ((), ())), preferred_element_type=jnp.float32
    )


def dot_tn(left, right):
    return lax.dot_general(
        left, right, (((0,), (0,)), ((), ())), preferred_element_type=jnp.float32
    )


def stacked_heads(ref, group, group_size):
    first = group * group_size
    return jnp.concatenate(
        [ref[:, (first + c) * HD : (first + c + 1) * HD] for c in range(group_size)], axis=0
    )


def pack_kernel(
    sizes,
    docs_hbm,
    tiles_hbm,
    cite_hbm,
    features_hbm,
    k_hbm,
    v_hbm,
    rows_ref,
    kv_ref,
    meta_ref,
    docs_ref,
    tiles_ref,
    cite_ref,
    sems,
):
    slots, parts, slot_count = sizes
    tok_rows = docs_ref.shape[1]
    width = kv_ref.shape[1]
    vision = features_hbm.shape[2]
    feature_rows = parts * slots
    pairs = [(docs_hbm, docs_ref), (tiles_hbm, tiles_ref), (cite_hbm, cite_ref)]
    for part in range(parts):
        cut = min(width, vision - part * width)
        pairs.append(
            (
                features_hbm.at[0, :, pl.ds(part * width, cut)],
                rows_ref.at[pl.ds(part * slots, slots), pl.ds(0, cut)],
            )
        )
    pairs.append((k_hbm.at[0], kv_ref.at[pl.ds(0, tok_rows), :]))
    pairs.append((v_hbm.at[0], kv_ref.at[pl.ds(tok_rows, tok_rows), :]))
    copies = [
        pltpu.make_async_copy(source, target, sems.at[n])
        for n, (source, target) in enumerate(pairs)
    ]
    for copy in copies:
        copy.start()
    for copy in copies[:3]:
        copy.wait()
    docs = docs_ref[...]
    image_of = jnp.zeros_like(docs)
    for doc in range(cite_ref.shape[1]):
        image_of = jnp.where(docs == doc, cite_ref[0, doc], image_of)
    count = jnp.zeros_like(docs)
    for image in range(tiles_ref.shape[1]):
        count = jnp.where(image_of == image, tiles_ref[0, image] * TILE_TOK, count)
    first = image_of * slot_count
    row = lax.broadcasted_iota(jnp.int32, meta_ref.shape, 0)
    meta_ref[...] = jnp.where(
        row == 0, docs, jnp.where(row == 1, first, jnp.where(row == 2, first + count, 0))
    )
    doc_rows = jnp.broadcast_to(docs.astype(jnp.float32), (slots, tok_rows))
    spare = jnp.zeros((slots, parts * width - vision - tok_rows), jnp.float32)
    tail = jnp.concatenate([doc_rows, spare], axis=1).astype(jnp.bfloat16)
    for copy in copies[3:]:
        copy.wait()
    last = vision - (parts - 1) * width
    rows_ref[feature_rows - slots : feature_rows, last:] = tail


def cross_kernel(sizes, meta_ref, q_ref, cot_ref, *rest):
    kv_local, group_size, slots, blocks = sizes
    key_refs = rest[:blocks]
    grad_ref, weights_ref = rest[blocks:]
    seq_at = lax.axis_index("seq")
    tok_rows = q_ref.shape[0]
    bias = []
    for x in range(blocks):
        slot_ids = (seq_at ^ x) * slots + lax.broadcasted_iota(jnp.int32, (slots, tok_rows), 0)
        kept = (slot_ids >= meta_ref[1:2, :]) & (slot_ids < meta_ref[2:3, :])
        bias.append(jnp.where(kept, 0.0, MASK_FILL))
    bias = jnp.concatenate(bias, axis=0)
    bias = jnp.concatenate([bias] * group_size, axis=1)
    scale = HD ** (-0.5) * LOG2E
    spans = [slice(group * HD, (group + 1) * HD) for group in range(kv_local)]
    scores = [
        dot_nt(
            jnp.concatenate([ref[:, columns] for ref in key_refs], axis=0),
            stacked_heads(q_ref, group, group_size),
        )
        for group, columns in enumerate(spans)
    ]
    for group in range(kv_local):
        scaled = scores[group] * scale + bias
        exps = jnp.exp2(scaled - jnp.max(scaled, axis=0, keepdims=True))
        inverse = 1.0 / jnp.sum(exps, axis=0, keepdims=True)
        weights_ref[group] = (exps * inverse).astype(jnp.bfloat16)
    for group, columns in enumerate(spans):
        grads = dot_nn(weights_ref[group], stacked_heads(cot_ref, group, group_size)).astype(
            jnp.bfloat16
        )
        for x in range(blocks):
            at = pl.multiple_of((seq_at ^ x) * slots, slots)
            grad_ref[pl.ds(at, slots), columns] = grads[x * slots : (x + 1) * slots]


def stacked_features(rows, part, slots, cut):
    return jnp.concatenate(
        [ref[part * slots : (part + 1) * slots, :cut] for ref in rows], axis=0
    )


def first_positions(sizes, meta_ref, rows):
    slots, parts, last = sizes
    docs = meta_ref[0:1, :].astype(jnp.float32)
    tok_rows = docs.shape[1]
    start = jnp.zeros((1, tok_rows), jnp.float32)
    at = (parts - 1) * slots
    for ref in rows:
        row = ref[at : at + 16, last : last + tok_rows].astype(jnp.float32)[0:1]
        column = jnp.transpose(jnp.broadcast_to(row, (tok_rows, tok_rows)))
        start = start + jnp.sum(jnp.where(column < docs, 1.0, 0.0), axis=0, keepdims=True)
    return start


def kept_bias(seq_at, first, blocks, start, group_size):
    tok_rows = start.shape[1]
    query_pos = seq_at * tok_rows + lax.broadcasted_iota(jnp.int32, (1, tok_rows), 1)
    bias = []
    for x in range(first, first + blocks):
        key_pos = (seq_at ^ x) * tok_rows + lax.broadcasted_iota(
            jnp.int32, (tok_rows, tok_rows), 0
        )
        kept = (key_pos >= start) & (key_pos <= query_pos)
        bias.append(jnp.where(kept, 0.0, MASK_FILL))
    return jnp.concatenate([jnp.concatenate(bias, axis=0)] * group_size, axis=1)


def scaled_scores(pairs, columns, queries, bias):
    tok_rows = pairs[0].shape[0] // 2
    keys = jnp.concatenate([ref[:tok_rows, columns] for ref in pairs], axis=0)
    return dot_nt(keys, queries) * (HD ** (-0.5) * LOG2E) + bias


def weighted_values(pairs, columns, exps):
    tok_rows = pairs[0].shape[0] // 2
    vals = jnp.concatenate([ref[tok_rows:, columns] for ref in pairs], axis=0)
    return dot_tn(vals, exps)


def early_kernel(sizes, meta_ref, q_ref, w_ref, weights_ref, *rest):
    kv_local, group_size, slots, parts, blocks, count = sizes
    rows, pairs = rest[:blocks], rest[blocks : blocks + count]
    cross_ref, self_ref, stats_ref = rest[blocks + count :]
    width = pairs[0].shape[1]
    vision = w_ref.shape[0]
    seq_at = lax.axis_index("seq")
    start = first_positions((slots, parts, vision - (parts - 1) * width), meta_ref, rows)
    stats_ref[kv_local, 0:1, :] = jnp.concatenate([start] * group_size, axis=1)
    bias = kept_bias(seq_at, 0, count, start.astype(jnp.int32), group_size)
    spans = [slice(group * HD, (group + 1) * HD) for group in range(kv_local)]
    scores = [
        scaled_scores(pairs, columns, stacked_heads(q_ref, group, group_size), bias)
        for group, columns in enumerate(spans)
    ]
    weighted = []
    for group in range(kv_local):
        top = jnp.max(scores[group], axis=0, keepdims=True)
        exps = jnp.exp2(scores[group] - top)
        stats_ref[group, 0:1, :] = top
        stats_ref[group, 1:2, :] = jnp.sum(exps, axis=0, keepdims=True)
        weighted.append(exps.astype(jnp.bfloat16))
    for group, columns in enumerate(spans):
        self_ref[group] = weighted_values(pairs, columns, weighted[group])
    total = None
    for part in range(parts):
        cut = min(width, vision - part * width)
        term = dot_nn(
            stacked_features(rows, part, slots, cut), w_ref[part * width : part * width + cut, :]
        )
        total = term if total is None else total + term
    values = total.astype(jnp.bfloat16)
    for group in range(kv_local):
        columns = slice(group * HD, (group + 1) * HD)
        cross_ref[group] = dot_tn(values[:, columns], weights_ref[group])


def absorbed(sizes, first, pair_ref, q_ref, stats_ref):
    kv_local, group_size = sizes
    seq_at = lax.axis_index("seq")
    start = stats_ref[kv_local, 0:1, : q_ref.shape[0]]
    bias = kept_bias(seq_at, first, 1, start.astype(jnp.int32), group_size)
    spans = [slice(group * HD, (group + 1) * HD) for group in range(kv_local)]
    pairs = (pair_ref,)
    scores = [
        scaled_scores(pairs, columns, stacked_heads(q_ref, group, group_size), bias)
        for group, columns in enumerate(spans)
    ]
    found = []
    for group in range(kv_local):
        before = stats_ref[group, 0:1, :]
        top = jnp.maximum(before, jnp.max(scores[group], axis=0, keepdims=True))
        exps = jnp.exp2(scores[group] - top)
        factor = jnp.exp2(before - top)
        total = factor * stats_ref[group, 1:2, :] + jnp.sum(exps, axis=0, keepdims=True)
        found.append((top, factor, total, exps.astype(jnp.bfloat16)))
    return [
        (top, factor, total, weighted_values(pairs, columns, exps))
        for columns, (top, factor, total, exps) in zip(spans, found)
    ]


def middle_kernel(sizes, q_ref, self_ref, stats_ref, pair_ref, out_ref, stats_out_ref):
    kv_local, group_size, first = sizes
    stats_out_ref[kv_local, 0:1, :] = stats_ref[kv_local, 0:1, :]
    found = absorbed((kv_local, group_size), first, pair_ref, q_ref, stats_ref)
    for group, (top, factor, total, added) in enumerate(found):
        out_ref[group] = self_ref[group] * factor + added
        stats_out_ref[group, 0:1, :] = top
        stats_out_ref[group, 1:2, :] = total


def late_kernel(
    sizes, q_ref, cross_ref, self_ref, stats_ref, pair_ref, out_hbm, out_ref, sems
):
    kv_local, group_size, first = sizes
    tok_rows = q_ref.shape[0]
    found = absorbed((kv_local, group_size), first, pair_ref, q_ref, stats_ref)
    copies = []
    for group, (_, factor, total, added) in enumerate(found):
        inverse = 1.0 / total
        self_out = self_ref[group] * (factor * inverse) + added * inverse
        merged = (self_out + cross_ref[group]).astype(jnp.bfloat16)
        for c in range(group_size):
            out_ref[group, :, c * HD : (c + 1) * HD] = jnp.transpose(
                merged[:, c * tok_rows : (c + 1) * tok_rows]
            )
        span = group_size * HD
        copies.append(
            pltpu.make_async_copy(
                out_ref.at[group], out_hbm.at[:, pl.ds(group * span, span)], sems.at[group]
            )
        )
        copies[-1].start()
    for copy in copies:
        copy.wait()


def product_kernel(sizes, *rest):
    slots, vision, out_rows, steps, parts, blocks = sizes
    terms, rows, outs = rest[:blocks], rest[blocks : 2 * blocks], rest[2 * blocks : -2]
    sum_ref, turned_ref = rest[-2:]
    seq_at, dp_at = lax.axis_index("seq"), lax.axis_index("dp")
    width = sum_ref.shape[1]
    total = terms[0][...].astype(jnp.float32)
    for ref in terms[1:]:
        total = total + ref[...].astype(jnp.float32)
    sum_ref[...] = total.astype(jnp.bfloat16)
    grads = jnp.concatenate(
        [
            sum_ref[pl.ds(pl.multiple_of((seq_at ^ x) * slots, slots), slots), :]
            for x in range(blocks)
        ],
        axis=0,
    )
    for part in range(parts):
        cut = min(width, vision - part * width)
        turned_ref[part * width : part * width + cut, :] = jnp.transpose(
            stacked_features(rows, part, slots, cut)
        )
    for x in range(steps):
        row = pl.multiple_of(((dp_at ^ x) * blocks + seq_at) * out_rows, out_rows)
        block = dot_nn(turned_ref[pl.ds(row, out_rows), :], grads)
        outs[x][...] = block.astype(outs[x].dtype)


def vmem_specs(count):
    return [pl.BlockSpec(memory_space=pltpu.VMEM)] * count


def dp_order(size):
    return sorted(range(1, size), key=lambda x: (x == 1, x))


def on_device_small(
    seq_size,
    dp_size,
    q_self,
    k_self,
    v_self,
    docs,
    q_cross,
    cotangent,
    img_keys,
    features,
    w_value,
    tiles,
    cite,
):
    tok_rows = q_self.shape[1]
    width = k_self.shape[2]
    kv_local = width // HD
    heads_local = q_self.shape[2] // HD
    group_size = heads_local // kv_local
    slots = img_keys.shape[1]
    vision = features.shape[2]
    images = tiles.shape[1]
    out_rows = vision // (seq_size * dp_size)
    key_count = slots * seq_size
    hbm = pl.BlockSpec(memory_space=pltpu.HBM)
    parts = -(-vision // width)
    feature_rows = parts * slots
    far, near = seq_size // 2, 1

    def swapped(array, axis, size, x):
        return lax.ppermute(array, axis, [(i, i ^ x) for i in range(size)])

    def gathered(array):
        there = swapped(array, "seq", seq_size, far)
        beside = swapped(array, "seq", seq_size, near)
        across = swapped(there, "seq", seq_size, near)
        return (array, beside, there, across)

    key_blocks = gathered(img_keys[0])

    rows_own, kv_own, meta = pl.pallas_call(
        functools.partial(pack_kernel, (slots, parts, key_count // images)),
        out_shape=(
            jax.ShapeDtypeStruct((feature_rows, width), jnp.bfloat16),
            jax.ShapeDtypeStruct((2 * tok_rows, width), jnp.bfloat16),
            jax.ShapeDtypeStruct((8, tok_rows), jnp.int32),
        ),
        in_specs=[hbm] * 6,
        out_specs=tuple(vmem_specs(3)),
        scratch_shapes=[
            pltpu.VMEM(docs.shape, jnp.int32),
            pltpu.SMEM(tiles.shape, jnp.int32),
            pltpu.SMEM(cite.shape, jnp.int32),
            pltpu.SemaphoreType.DMA((5 + parts,)),
        ],
        compiler_params=pltpu.CompilerParams(vmem_limit_bytes=8 << 20),
        cost_estimate=pl.CostEstimate(flops=4 << 30, bytes_accessed=16 << 20, transcendentals=0),
        name="pack",
    )(
        *[
            pltpu.with_memory_space_constraint(array, pltpu.HBM)
            for array in (docs, tiles, cite, features, k_self, v_self)
        ]
    )
    row_blocks = gathered(rows_own)

    grad_terms, weights = pl.pallas_call(
        functools.partial(cross_kernel, (kv_local, group_size, slots, seq_size)),
        out_shape=(
            jax.ShapeDtypeStruct((key_count, width), jnp.bfloat16),
            jax.ShapeDtypeStruct((kv_local, key_count, group_size * tok_rows), jnp.bfloat16),
        ),
        in_specs=vmem_specs(3 + seq_size),
        out_specs=tuple(vmem_specs(2)),
        compiler_params=pltpu.CompilerParams(vmem_limit_bytes=24 << 20),
        name="cross",
    )(meta, q_cross[0], cotangent[0], *key_blocks)
    term_blocks = gathered(grad_terms)
    kv_blocks = gathered(kv_own)
    blocks_out = pl.pallas_call(
        functools.partial(
            product_kernel, (slots, vision, out_rows, dp_size, parts, seq_size)
        ),
        out_shape=tuple(
            jax.ShapeDtypeStruct((out_rows, width), jnp.bfloat16 if x else jnp.float32)
            for x in range(dp_size)
        ),
        in_specs=vmem_specs(2 * seq_size),
        out_specs=tuple(vmem_specs(dp_size)),
        scratch_shapes=[
            pltpu.VMEM((key_count, width), jnp.bfloat16),
            pltpu.VMEM((vision, key_count), jnp.bfloat16),
        ],
        compiler_params=pltpu.CompilerParams(vmem_limit_bytes=16 << 20),
        name="product",
    )(*term_blocks, *row_blocks)
    weight_grad = blocks_out[0]
    for x in dp_order(dp_size):
        arrived = swapped(blocks_out[x], "dp", dp_size, x)
        weight_grad = weight_grad + arrived.astype(jnp.float32)

    chip = seq_size // 2
    columns = group_size * tok_rows
    partial_shape = jax.ShapeDtypeStruct((kv_local, HD, columns), jnp.float32)
    stats_shape = jax.ShapeDtypeStruct((kv_local + 1, 8, columns), jnp.float32)
    cross_out, partial, stats = pl.pallas_call(
        functools.partial(early_kernel, (kv_local, group_size, slots, parts, seq_size, chip)),
        out_shape=(partial_shape, partial_shape, stats_shape),
        in_specs=vmem_specs(4 + seq_size + chip),
        out_specs=tuple(vmem_specs(3)),
        compiler_params=pltpu.CompilerParams(vmem_limit_bytes=24 << 20),
        name="early",
    )(meta, q_self[0], w_value, weights, *row_blocks, *kv_blocks[:chip])
    partial, stats = pl.pallas_call(
        functools.partial(middle_kernel, (kv_local, group_size, chip)),
        out_shape=(partial_shape, stats_shape),
        in_specs=vmem_specs(4),
        out_specs=tuple(vmem_specs(2)),
        compiler_params=pltpu.CompilerParams(vmem_limit_bytes=16 << 20),
        name="middle",
    )(q_self[0], partial, stats, kv_blocks[chip])
    merged = pl.pallas_call(
        functools.partial(late_kernel, (kv_local, group_size, chip + 1)),
        out_shape=jax.ShapeDtypeStruct((tok_rows, heads_local * HD), jnp.bfloat16),
        in_specs=vmem_specs(5),
        out_specs=hbm,
        scratch_shapes=[
            pltpu.VMEM((kv_local, tok_rows, group_size * HD), jnp.bfloat16),
            pltpu.SemaphoreType.DMA((kv_local,)),
        ],
        compiler_params=pltpu.CompilerParams(vmem_limit_bytes=16 << 20),
        name="late",
    )(q_self[0], cross_out, partial, stats, kv_blocks[chip + 1])
    return (merged[None], weight_grad)


def fits_small(mesh, shapes):
    seq_size, dp_size = mesh.shape["seq"], mesh.shape["dp"]
    q_self, k_self, img_keys, features, _, cite = shapes
    tensor = mesh.shape["tensor"]
    powers = all(n & (n - 1) == 0 for n in (seq_size, dp_size))
    tok_rows, width = q_self[1] // seq_size, k_self[2] // tensor
    slots = img_keys[1] // seq_size
    rows, left = divmod(features[2], seq_size * dp_size)
    return (
        powers
        and seq_size == 4
        and dp_size <= 8
        and tok_rows == HD
        and tok_rows <= width
        and slots % 32 == 0
        and slots * seq_size == HD
        and left == 0
        and rows % 16 == 0
        and features[2] % HD == 0
        and width % HD == 0
        and -features[2] % width >= tok_rows
        and cite[1] <= 256
    )


def solution(mesh):
    in_specs = (
        P("dp", "seq", "tensor"),
        P("dp", "seq", "tensor"),
        P("dp", "seq", "tensor"),
        P("dp", "seq"),
        P("dp", "seq", "tensor"),
        P("dp", "seq", "tensor"),
        P("dp", "seq", "tensor"),
        P("dp", "seq", None),
        P(None, "tensor"),
        P("dp", None),
        P("dp", None),
    )
    out_specs = (P("dp", "seq", "tensor"), P(("dp", "seq"), "tensor"))

    def run(*arrays):
        shapes = [arrays[i].shape for i in (0, 1, 6, 7, 8, 10)]
        body = on_device_general
        if fits_small(mesh, shapes):
            body = functools.partial(on_device_small, mesh.shape["seq"], mesh.shape["dp"])
        return jax.shard_map(
            body, mesh=mesh, in_specs=in_specs, out_specs=out_specs, check_vma=False
        )(*arrays)

    return run
```

```python
import functools
import math

import jax
import jax.numpy as jnp
from jax import lax
from jax.experimental import pallas as pl
from jax.experimental.pallas import tpu as pltpu
from jax.sharding import PartitionSpec as P


HD = 128
TILE_TOK = 8


MASK_FILL = -1e30
LOG2E = math.log2(math.e)


def absorb_block(
    running, queries, key_rows, value_rows, key_docs, key_pos, query_pos, my_docs, score_scale
):
    running_max, denominator, numerator = running
    kv_local = queries.shape[1]
    key_count = key_rows.shape[0]
    key_heads = key_rows.reshape(key_count, kv_local, HD)
    value_heads = value_rows.reshape(key_count, kv_local, HD)
    scores = (
        jnp.einsum("tgcd,sgd->gcts", queries, key_heads, preferred_element_type=jnp.float32)
        * score_scale
    )
    kept = (query_pos[:, None] >= key_pos[None, :]) & (my_docs[:, None] == key_docs[None, :])
    scores = jnp.where(kept, scores, MASK_FILL)
    new_max = jnp.maximum(running_max, jnp.max(scores, axis=-1))
    factor = jnp.exp(running_max - new_max)
    weights = jnp.where(kept, jnp.exp(scores - new_max[..., None]), 0.0)
    denominator = factor * denominator + jnp.sum(weights, axis=-1)
    numerator = factor[..., None] * numerator + jnp.einsum(
        "gcts,sgd->gctd",
        weights.astype(jnp.bfloat16),
        value_heads,
        preferred_element_type=jnp.float32,
    )
    return (new_max, denominator, numerator)


def on_device_general(
    q_self, k_self, v_self, docs, q_cross, cotangent, img_keys, features, w_value, tiles, cite
):
    tok_rows = q_self.shape[1]
    kv_local = k_self.shape[2] // HD
    heads_local = q_self.shape[2] // HD
    group_size = heads_local // kv_local
    score_scale = HD ** (-0.5)
    first_row = lax.axis_index("seq") * tok_rows
    query_pos = first_row + jnp.arange(tok_rows, dtype=jnp.int32)
    my_docs = docs[0]
    queries = q_self[0].reshape(tok_rows, kv_local, group_size, HD)
    start_state = (
        jnp.full((kv_local, group_size, tok_rows), MASK_FILL, jnp.float32),
        jnp.zeros((kv_local, group_size, tok_rows), jnp.float32),
        jnp.zeros((kv_local, group_size, tok_rows, HD), jnp.float32),
    )
    piece_keys = lax.all_gather(k_self, "seq", axis=1, tiled=True)
    piece_values = lax.all_gather(v_self, "seq", axis=1, tiled=True)
    piece_docs = lax.all_gather(docs, "seq", axis=1, tiled=True)
    key_count = piece_keys.shape[1]
    block_rows = math.gcd(key_count, 512)
    block_count = key_count // block_rows
    key_blocks = piece_keys[0].reshape(block_count, block_rows, -1)
    value_blocks = piece_values[0].reshape(block_count, block_rows, -1)
    doc_blocks = piece_docs[0].reshape(block_count, block_rows)
    pos_blocks = jnp.arange(key_count, dtype=jnp.int32).reshape(block_count, block_rows)

    def absorb_step(state_now, block_item):
        key_part, value_part, doc_part, pos_part = block_item
        return (
            absorb_block(
                state_now,
                queries,
                key_part,
                value_part,
                doc_part,
                pos_part,
                query_pos,
                my_docs,
                score_scale,
            ),
            None,
        )

    _, denominator, numerator = lax.scan(
        absorb_step, start_state, (key_blocks, value_blocks, doc_blocks, pos_blocks)
    )[0]
    self_out = numerator / denominator[..., None]
    values_own = jnp.dot(features[0], w_value, preferred_element_type=jnp.float32).astype(
        jnp.bfloat16
    )
    image_keys, image_values = (
        lax.all_gather(img_keys[0], "seq", axis=0, tiled=True),
        lax.all_gather(values_own, "seq", axis=0, tiled=True),
    )
    key_count = image_keys.shape[0]
    image_count = tiles.shape[1]
    slot_count = key_count // image_count
    doc_hit = my_docs[:, None] == jnp.arange(cite.shape[1], dtype=jnp.int32)[None, :]
    image_of = jnp.sum(jnp.where(doc_hit, cite[0][None, :], 0), axis=1)
    slot_ids = jnp.arange(key_count, dtype=jnp.int32)
    key_image = slot_ids // slot_count
    owner_hit = key_image[:, None] == jnp.arange(image_count, dtype=jnp.int32)[None, :]
    tile_limit = jnp.sum(jnp.where(owner_hit, tiles[0][None, :], 0), axis=1) * TILE_TOK
    cross_kept = (image_of[:, None] == key_image[None, :]) & (slot_ids % slot_count < tile_limit)[
        None, :
    ]
    cross_q = q_cross[0].reshape(tok_rows, kv_local, group_size, HD)
    cross_scores = (
        jnp.einsum(
            "tgcd,sgd->gcts",
            cross_q,
            image_keys.reshape(key_count, kv_local, HD),
            preferred_element_type=jnp.float32,
        )
        * score_scale
    )
    cross_scores = jnp.where(cross_kept, cross_scores, MASK_FILL)
    cross_exp = jnp.where(
        cross_kept, jnp.exp(cross_scores - jnp.max(cross_scores, axis=-1, keepdims=True)), 0.0
    )
    cross_weights = (cross_exp / jnp.sum(cross_exp, axis=-1, keepdims=True)).astype(jnp.bfloat16)
    cross_out = jnp.einsum(
        "gcts,sgd->gctd",
        cross_weights,
        image_values.reshape(key_count, kv_local, HD),
        preferred_element_type=jnp.float32,
    )
    merged = (
        (self_out + cross_out)
        .astype(jnp.bfloat16)
        .transpose(2, 0, 1, 3)
        .reshape(1, tok_rows, heads_local * HD)
    )
    cot_rows = cotangent[0].reshape(tok_rows, kv_local, group_size, HD)
    grad_terms = jnp.einsum(
        "gcts,tgcd->sgd", cross_weights, cot_rows, preferred_element_type=jnp.float32
    ).reshape(key_count, kv_local * HD)
    value_grad = lax.psum_scatter(
        grad_terms.astype(jnp.bfloat16), "seq", scatter_dimension=0, tiled=True
    )
    own_features = features[0]
    summed_samples = lax.psum_scatter(
        lax.dot_general(
            own_features, value_grad, (((0,), (0,)), ((), ())), preferred_element_type=jnp.float32
        ).astype(jnp.bfloat16),
        "dp",
        scatter_dimension=0,
        tiled=True,
    )
    weight_grad = lax.psum_scatter(summed_samples, "seq", scatter_dimension=0, tiled=True).astype(
        jnp.float32
    )
    return (merged, weight_grad)


def dot_nt(left, right):
    return lax.dot_general(
        left, right, (((1,), (1,)), ((), ())), preferred_element_type=jnp.float32
    )


def dot_nn(left, right):
    return lax.dot_general(
        left, right, (((1,), (0,)), ((), ())), preferred_element_type=jnp.float32
    )


def dot_tn(left, right):
    return lax.dot_general(
        left, right, (((0,), (0,)), ((), ())), preferred_element_type=jnp.float32
    )


def stacked_heads(ref, group, group_size):
    first = group * group_size
    return jnp.concatenate(
        [ref[:, (first + c) * HD : (first + c + 1) * HD] for c in range(group_size)], axis=0
    )


def pack_kernel(
    sizes,
    docs_hbm,
    tiles_hbm,
    cite_hbm,
    features_hbm,
    k_hbm,
    v_hbm,
    rows_ref,
    kv_ref,
    meta_ref,
    docs_ref,
    tiles_ref,
    cite_ref,
    sems,
):
    slots, parts, slot_count = sizes
    tok_rows = docs_ref.shape[1]
    width = kv_ref.shape[1]
    vision = features_hbm.shape[2]
    feature_rows = parts * slots
    pairs = [(docs_hbm, docs_ref), (tiles_hbm, tiles_ref), (cite_hbm, cite_ref)]
    for part in range(parts):
        cut = min(width, vision - part * width)
        pairs.append(
            (
                features_hbm.at[0, :, pl.ds(part * width, cut)],
                rows_ref.at[pl.ds(part * slots, slots), pl.ds(0, cut)],
            )
        )
    pairs.append((k_hbm.at[0], kv_ref.at[pl.ds(0, tok_rows), :]))
    pairs.append((v_hbm.at[0], kv_ref.at[pl.ds(tok_rows, tok_rows), :]))
    copies = [
        pltpu.make_async_copy(source, target, sems.at[n])
        for n, (source, target) in enumerate(pairs)
    ]
    for copy in copies:
        copy.start()
    for copy in copies[:3]:
        copy.wait()
    docs = docs_ref[...]
    image_of = jnp.zeros_like(docs)
    for doc in range(cite_ref.shape[1]):
        image_of = jnp.where(docs == doc, cite_ref[0, doc], image_of)
    count = jnp.zeros_like(docs)
    for image in range(tiles_ref.shape[1]):
        count = jnp.where(image_of == image, tiles_ref[0, image] * TILE_TOK, count)
    first = image_of * slot_count
    row = lax.broadcasted_iota(jnp.int32, meta_ref.shape, 0)
    meta_ref[...] = jnp.where(
        row == 0, docs, jnp.where(row == 1, first, jnp.where(row == 2, first + count, 0))
    )
    doc_rows = jnp.broadcast_to(docs.astype(jnp.float32), (slots, tok_rows))
    spare = jnp.zeros((slots, parts * width - vision - tok_rows), jnp.float32)
    tail = jnp.concatenate([doc_rows, spare], axis=1).astype(jnp.bfloat16)
    for copy in copies[3:]:
        copy.wait()
    last = vision - (parts - 1) * width
    rows_ref[feature_rows - slots : feature_rows, last:] = tail


def cross_kernel(sizes, meta_ref, q_ref, cot_ref, *rest):
    kv_local, group_size, slots, blocks = sizes
    key_refs, weights_ref, grad_refs = rest[:blocks], rest[blocks], rest[blocks + 1 :]
    share = kv_local // len(grad_refs)
    seq_at = lax.axis_index("seq")
    tok_rows = q_ref.shape[0]
    bias = []
    for x in range(blocks):
        slot_ids = (seq_at ^ x) * slots + lax.broadcasted_iota(jnp.int32, (slots, tok_rows), 0)
        kept = (slot_ids >= meta_ref[1:2, :]) & (slot_ids < meta_ref[2:3, :])
        bias.append(jnp.where(kept, 0.0, MASK_FILL))
    bias = jnp.concatenate(bias, axis=0)
    bias = jnp.concatenate([bias] * group_size, axis=1)
    scale = HD ** (-0.5) * LOG2E
    spans = [slice(group * HD, (group + 1) * HD) for group in range(kv_local)]
    scores = [
        dot_nt(
            jnp.concatenate([ref[:, columns] for ref in key_refs], axis=0),
            stacked_heads(q_ref, group, group_size),
        )
        for group, columns in enumerate(spans)
    ]
    for group in range(kv_local):
        scaled = scores[group] * scale + bias
        exps = jnp.exp2(scaled - jnp.max(scaled, axis=0, keepdims=True))
        inverse = 1.0 / jnp.sum(exps, axis=0, keepdims=True)
        weights_ref[group] = (exps * inverse).astype(jnp.bfloat16)
    for group, columns in enumerate(spans):
        grads = dot_nn(weights_ref[group], stacked_heads(cot_ref, group, group_size)).astype(
            jnp.bfloat16
        )
        for x in range(blocks):
            at = pl.multiple_of((seq_at ^ x) * slots, slots)
            grad_refs[group // share][pl.ds(at, slots), spans[group % share]] = grads[
                x * slots : (x + 1) * slots
            ]


def stacked_features(rows, part, slots, cut):
    return jnp.concatenate(
        [ref[part * slots : (part + 1) * slots, :cut] for ref in rows], axis=0
    )


def first_positions(sizes, meta_ref, rows):
    slots, parts, last = sizes
    docs = meta_ref[0:1, :].astype(jnp.float32)
    tok_rows = docs.shape[1]
    start = jnp.zeros((1, tok_rows), jnp.float32)
    at = (parts - 1) * slots
    for ref in rows:
        row = ref[at : at + 16, last : last + tok_rows].astype(jnp.float32)[0:1]
        column = jnp.transpose(jnp.broadcast_to(row, (tok_rows, tok_rows)))
        start = start + jnp.sum(jnp.where(column < docs, 1.0, 0.0), axis=0, keepdims=True)
    return start


def kept_bias(seq_at, first, blocks, start, group_size):
    tok_rows = start.shape[1]
    query_pos = seq_at * tok_rows + lax.broadcasted_iota(jnp.int32, (1, tok_rows), 1)
    bias = []
    for x in range(first, first + blocks):
        key_pos = (seq_at ^ x) * tok_rows + lax.broadcasted_iota(
            jnp.int32, (tok_rows, tok_rows), 0
        )
        kept = (key_pos >= start) & (key_pos <= query_pos)
        bias.append(jnp.where(kept, 0.0, MASK_FILL))
    return jnp.concatenate([jnp.concatenate(bias, axis=0)] * group_size, axis=1)


def scaled_scores(pairs, columns, queries, bias):
    tok_rows = pairs[0].shape[0] // 2
    keys = jnp.concatenate([ref[:tok_rows, columns] for ref in pairs], axis=0)
    return dot_nt(keys, queries) * (HD ** (-0.5) * LOG2E) + bias


def weighted_values(pairs, columns, exps):
    tok_rows = pairs[0].shape[0] // 2
    vals = jnp.concatenate([ref[tok_rows:, columns] for ref in pairs], axis=0)
    return dot_tn(vals, exps)


def early_kernel(sizes, meta_ref, q_ref, w_ref, weights_ref, *rest):
    kv_local, group_size, slots, parts, blocks, count = sizes
    rows, pairs = rest[:blocks], rest[blocks : blocks + count]
    cross_ref, self_ref, stats_ref, turned_ref = rest[blocks + count :]
    width = pairs[0].shape[1]
    vision = w_ref.shape[0]
    seq_at = lax.axis_index("seq")
    start = first_positions((slots, parts, vision - (parts - 1) * width), meta_ref, rows)
    stats_ref[kv_local, 0:1, :] = jnp.concatenate([start] * group_size, axis=1)
    bias = kept_bias(seq_at, 0, count, start.astype(jnp.int32), group_size)
    spans = [slice(group * HD, (group + 1) * HD) for group in range(kv_local)]
    scores = [
        scaled_scores(pairs, columns, stacked_heads(q_ref, group, group_size), bias)
        for group, columns in enumerate(spans)
    ]
    weighted = []
    for group in range(kv_local):
        top = jnp.max(scores[group], axis=0, keepdims=True)
        exps = jnp.exp2(scores[group] - top)
        stats_ref[group, 0:1, :] = top
        stats_ref[group, 1:2, :] = jnp.sum(exps, axis=0, keepdims=True)
        weighted.append(exps.astype(jnp.bfloat16))
    for group, columns in enumerate(spans):
        self_ref[group] = weighted_values(pairs, columns, weighted[group])
    total = None
    for part in range(parts):
        cut = min(width, vision - part * width)
        stacked = stacked_features(rows, part, slots, cut)
        turned_ref[part * width : part * width + cut, :] = jnp.transpose(stacked)
        term = dot_nn(stacked, w_ref[part * width : part * width + cut, :])
        total = term if total is None else total + term
    values = total.astype(jnp.bfloat16)
    for group in range(kv_local):
        columns = slice(group * HD, (group + 1) * HD)
        cross_ref[group] = dot_tn(values[:, columns], weights_ref[group])


def absorbed(sizes, first, pair_ref, q_ref, stats_ref):
    kv_local, group_size = sizes
    seq_at = lax.axis_index("seq")
    start = stats_ref[kv_local, 0:1, : q_ref.shape[0]]
    bias = kept_bias(seq_at, first, 1, start.astype(jnp.int32), group_size)
    spans = [slice(group * HD, (group + 1) * HD) for group in range(kv_local)]
    pairs = (pair_ref,)
    scores = [
        scaled_scores(pairs, columns, stacked_heads(q_ref, group, group_size), bias)
        for group, columns in enumerate(spans)
    ]
    found = []
    for group in range(kv_local):
        before = stats_ref[group, 0:1, :]
        top = jnp.maximum(before, jnp.max(scores[group], axis=0, keepdims=True))
        exps = jnp.exp2(scores[group] - top)
        factor = jnp.exp2(before - top)
        total = factor * stats_ref[group, 1:2, :] + jnp.sum(exps, axis=0, keepdims=True)
        found.append((top, factor, total, exps.astype(jnp.bfloat16)))
    return [
        (top, factor, total, weighted_values(pairs, columns, exps))
        for columns, (top, factor, total, exps) in zip(spans, found)
    ]


def middle_kernel(sizes, q_ref, self_ref, stats_ref, pair_ref, out_ref, stats_out_ref):
    kv_local, group_size, first = sizes
    stats_out_ref[kv_local, 0:1, :] = stats_ref[kv_local, 0:1, :]
    found = absorbed((kv_local, group_size), first, pair_ref, q_ref, stats_ref)
    for group, (top, factor, total, added) in enumerate(found):
        out_ref[group] = self_ref[group] * factor + added
        stats_out_ref[group, 0:1, :] = top
        stats_out_ref[group, 1:2, :] = total


def late_kernel(
    sizes, q_ref, cross_ref, self_ref, stats_ref, pair_ref, out_hbm, out_ref, sems
):
    kv_local, group_size, first = sizes
    tok_rows = q_ref.shape[0]
    found = absorbed((kv_local, group_size), first, pair_ref, q_ref, stats_ref)
    copies = []
    for group, (_, factor, total, added) in enumerate(found):
        inverse = 1.0 / total
        self_out = self_ref[group] * (factor * inverse) + added * inverse
        merged = (self_out + cross_ref[group]).astype(jnp.bfloat16)
        for c in range(group_size):
            out_ref[group, :, c * HD : (c + 1) * HD] = jnp.transpose(
                merged[:, c * tok_rows : (c + 1) * tok_rows]
            )
        span = group_size * HD
        copies.append(
            pltpu.make_async_copy(
                out_ref.at[group], out_hbm.at[:, pl.ds(group * span, span)], sems.at[group]
            )
        )
        copies[-1].start()
    for copy in copies:
        copy.wait()


def product_kernel(sizes, turned_ref, *rest):
    slots, out_rows, steps, blocks = sizes
    terms, outs, sum_ref = rest[:blocks], rest[blocks:-1], rest[-1]
    seq_at, dp_at = lax.axis_index("seq"), lax.axis_index("dp")
    total = terms[0][...].astype(jnp.float32)
    for ref in terms[1:]:
        total = total + ref[...].astype(jnp.float32)
    sum_ref[...] = total.astype(jnp.bfloat16)
    grads = jnp.concatenate(
        [
            sum_ref[pl.ds(pl.multiple_of((seq_at ^ x) * slots, slots), slots), :]
            for x in range(blocks)
        ],
        axis=0,
    )
    for x in range(steps):
        row = pl.multiple_of(((dp_at ^ x) * blocks + seq_at) * out_rows, out_rows)
        block = dot_nn(turned_ref[pl.ds(row, out_rows), :], grads)
        outs[x][...] = block.astype(outs[x].dtype)


def vmem_specs(count):
    return [pl.BlockSpec(memory_space=pltpu.VMEM)] * count


def dp_order(size):
    return sorted(range(1, size), key=lambda x: (x == 1, x))


def on_device_small(
    seq_size,
    dp_size,
    q_self,
    k_self,
    v_self,
    docs,
    q_cross,
    cotangent,
    img_keys,
    features,
    w_value,
    tiles,
    cite,
):
    tok_rows = q_self.shape[1]
    width = k_self.shape[2]
    kv_local = width // HD
    heads_local = q_self.shape[2] // HD
    group_size = heads_local // kv_local
    slots = img_keys.shape[1]
    vision = features.shape[2]
    images = tiles.shape[1]
    out_rows = vision // (seq_size * dp_size)
    key_count = slots * seq_size
    hbm = pl.BlockSpec(memory_space=pltpu.HBM)
    parts = -(-vision // width)
    feature_rows = parts * slots
    far, near = seq_size // 2, 1

    def swapped(array, axis, size, x):
        return lax.ppermute(array, axis, [(i, i ^ x) for i in range(size)])

    def gathered(array):
        there = swapped(array, "seq", seq_size, far)
        beside = swapped(array, "seq", seq_size, near)
        across = swapped(there, "seq", seq_size, near)
        return (array, beside, there, across)

    key_blocks = gathered(img_keys[0])

    rows_own, kv_own, meta = pl.pallas_call(
        functools.partial(pack_kernel, (slots, parts, key_count // images)),
        out_shape=(
            jax.ShapeDtypeStruct((feature_rows, width), jnp.bfloat16),
            jax.ShapeDtypeStruct((2 * tok_rows, width), jnp.bfloat16),
            jax.ShapeDtypeStruct((8, tok_rows), jnp.int32),
        ),
        in_specs=[hbm] * 6,
        out_specs=tuple(vmem_specs(3)),
        scratch_shapes=[
            pltpu.VMEM(docs.shape, jnp.int32),
            pltpu.SMEM(tiles.shape, jnp.int32),
            pltpu.SMEM(cite.shape, jnp.int32),
            pltpu.SemaphoreType.DMA((5 + parts,)),
        ],
        compiler_params=pltpu.CompilerParams(vmem_limit_bytes=8 << 20),
        cost_estimate=pl.CostEstimate(flops=4 << 30, bytes_accessed=16 << 20, transcendentals=0),
        name="pack",
    )(
        *[
            pltpu.with_memory_space_constraint(array, pltpu.HBM)
            for array in (docs, tiles, cite, features, k_self, v_self)
        ]
    )
    row_blocks = gathered(rows_own)

    halves = 1
    half_width = width // halves
    weights, *grad_terms = pl.pallas_call(
        functools.partial(cross_kernel, (kv_local, group_size, slots, seq_size)),
        out_shape=(
            jax.ShapeDtypeStruct((kv_local, key_count, group_size * tok_rows), jnp.bfloat16),
        )
        + (jax.ShapeDtypeStruct((key_count, half_width), jnp.bfloat16),) * halves,
        in_specs=vmem_specs(3 + seq_size),
        out_specs=tuple(vmem_specs(1 + halves)),
        compiler_params=pltpu.CompilerParams(vmem_limit_bytes=24 << 20),
        name="cross",
    )(meta, q_cross[0], cotangent[0], *key_blocks)
    kv_blocks = gathered(kv_own)
    chip = seq_size // 2
    columns = group_size * tok_rows
    partial_shape = jax.ShapeDtypeStruct((kv_local, HD, columns), jnp.float32)
    stats_shape = jax.ShapeDtypeStruct((kv_local + 1, 8, columns), jnp.float32)
    cross_out, partial, stats, turned = pl.pallas_call(
        functools.partial(early_kernel, (kv_local, group_size, slots, parts, seq_size, chip)),
        out_shape=(
            partial_shape,
            partial_shape,
            stats_shape,
            jax.ShapeDtypeStruct((vision, key_count), jnp.bfloat16),
        ),
        in_specs=vmem_specs(4 + seq_size + chip),
        out_specs=tuple(vmem_specs(4)),
        compiler_params=pltpu.CompilerParams(vmem_limit_bytes=24 << 20),
        name="early",
    )(meta, q_self[0], w_value, weights, *row_blocks, *kv_blocks[:chip])
    sums = []
    for half in range(halves):
        term_blocks = gathered(grad_terms[half])
        blocks_out = pl.pallas_call(
            functools.partial(product_kernel, (slots, out_rows, dp_size, seq_size)),
            out_shape=tuple(
                jax.ShapeDtypeStruct(
                    (out_rows, half_width), jnp.bfloat16 if x else jnp.float32
                )
                for x in range(dp_size)
            ),
            in_specs=vmem_specs(1 + seq_size),
            out_specs=tuple(vmem_specs(dp_size)),
            scratch_shapes=[pltpu.VMEM((key_count, half_width), jnp.bfloat16)],
            compiler_params=pltpu.CompilerParams(vmem_limit_bytes=16 << 20),
            name="product",
        )(turned, *term_blocks)
        total = blocks_out[0]
        for x in dp_order(dp_size):
            arrived = swapped(blocks_out[x], "dp", dp_size, x)
            total = total + arrived.astype(jnp.float32)
        sums.append(total)
    weight_grad = jnp.concatenate(sums, axis=1)
    partial, stats = pl.pallas_call(
        functools.partial(middle_kernel, (kv_local, group_size, chip)),
        out_shape=(partial_shape, stats_shape),
        in_specs=vmem_specs(4),
        out_specs=tuple(vmem_specs(2)),
        compiler_params=pltpu.CompilerParams(vmem_limit_bytes=16 << 20),
        name="middle",
    )(q_self[0], partial, stats, kv_blocks[chip])
    merged = pl.pallas_call(
        functools.partial(late_kernel, (kv_local, group_size, chip + 1)),
        out_shape=jax.ShapeDtypeStruct((tok_rows, heads_local * HD), jnp.bfloat16),
        in_specs=vmem_specs(5),
        out_specs=hbm,
        scratch_shapes=[
            pltpu.VMEM((kv_local, tok_rows, group_size * HD), jnp.bfloat16),
            pltpu.SemaphoreType.DMA((kv_local,)),
        ],
        compiler_params=pltpu.CompilerParams(vmem_limit_bytes=16 << 20),
        name="late",
    )(q_self[0], cross_out, partial, stats, kv_blocks[chip + 1])
    return (merged[None], weight_grad)


def fits_small(mesh, shapes):
    seq_size, dp_size = mesh.shape["seq"], mesh.shape["dp"]
    q_self, k_self, img_keys, features, _, cite = shapes
    tensor = mesh.shape["tensor"]
    powers = all(n & (n - 1) == 0 for n in (seq_size, dp_size))
    tok_rows, width = q_self[1] // seq_size, k_self[2] // tensor
    slots = img_keys[1] // seq_size
    rows, left = divmod(features[2], seq_size * dp_size)
    return (
        powers
        and seq_size == 4
        and dp_size <= 8
        and tok_rows == HD
        and tok_rows <= width
        and slots % 32 == 0
        and slots * seq_size == HD
        and left == 0
        and rows % 16 == 0
        and features[2] % HD == 0
        and width % HD == 0
        and -features[2] % width >= tok_rows
        and cite[1] <= 256
    )


def solution(mesh):
    in_specs = (
        P("dp", "seq", "tensor"),
        P("dp", "seq", "tensor"),
        P("dp", "seq", "tensor"),
        P("dp", "seq"),
        P("dp", "seq", "tensor"),
        P("dp", "seq", "tensor"),
        P("dp", "seq", "tensor"),
        P("dp", "seq", None),
        P(None, "tensor"),
        P("dp", None),
        P("dp", None),
    )
    out_specs = (P("dp", "seq", "tensor"), P(("dp", "seq"), "tensor"))

    def run(*arrays):
        shapes = [arrays[i].shape for i in (0, 1, 6, 7, 8, 10)]
        body = on_device_general
        if fits_small(mesh, shapes):
            body = functools.partial(on_device_small, mesh.shape["seq"], mesh.shape["dp"])
        return jax.shard_map(
            body, mesh=mesh, in_specs=in_specs, out_specs=out_specs, check_vma=False
        )(*arrays)

    return run
```

```python
import functools
import math

import jax
import jax.numpy as jnp
from jax import lax
from jax.experimental import pallas as pl
from jax.experimental.pallas import tpu as pltpu
from jax.sharding import PartitionSpec as P


HD = 128
TILE_TOK = 8


MASK_FILL = -1e30
LOG2E = math.log2(math.e)


def absorb_block(
    running, queries, key_rows, value_rows, key_docs, key_pos, query_pos, my_docs, score_scale
):
    running_max, denominator, numerator = running
    kv_local = queries.shape[1]
    key_count = key_rows.shape[0]
    key_heads = key_rows.reshape(key_count, kv_local, HD)
    value_heads = value_rows.reshape(key_count, kv_local, HD)
    scores = (
        jnp.einsum("tgcd,sgd->gcts", queries, key_heads, preferred_element_type=jnp.float32)
        * score_scale
    )
    kept = (query_pos[:, None] >= key_pos[None, :]) & (my_docs[:, None] == key_docs[None, :])
    scores = jnp.where(kept, scores, MASK_FILL)
    new_max = jnp.maximum(running_max, jnp.max(scores, axis=-1))
    factor = jnp.exp(running_max - new_max)
    weights = jnp.where(kept, jnp.exp(scores - new_max[..., None]), 0.0)
    denominator = factor * denominator + jnp.sum(weights, axis=-1)
    numerator = factor[..., None] * numerator + jnp.einsum(
        "gcts,sgd->gctd",
        weights.astype(jnp.bfloat16),
        value_heads,
        preferred_element_type=jnp.float32,
    )
    return (new_max, denominator, numerator)


def on_device_general(
    q_self, k_self, v_self, docs, q_cross, cotangent, img_keys, features, w_value, tiles, cite
):
    tok_rows = q_self.shape[1]
    kv_local = k_self.shape[2] // HD
    heads_local = q_self.shape[2] // HD
    group_size = heads_local // kv_local
    score_scale = HD ** (-0.5)
    first_row = lax.axis_index("seq") * tok_rows
    query_pos = first_row + jnp.arange(tok_rows, dtype=jnp.int32)
    my_docs = docs[0]
    queries = q_self[0].reshape(tok_rows, kv_local, group_size, HD)
    start_state = (
        jnp.full((kv_local, group_size, tok_rows), MASK_FILL, jnp.float32),
        jnp.zeros((kv_local, group_size, tok_rows), jnp.float32),
        jnp.zeros((kv_local, group_size, tok_rows, HD), jnp.float32),
    )
    piece_keys = lax.all_gather(k_self, "seq", axis=1, tiled=True)
    piece_values = lax.all_gather(v_self, "seq", axis=1, tiled=True)
    piece_docs = lax.all_gather(docs, "seq", axis=1, tiled=True)
    key_count = piece_keys.shape[1]
    block_rows = math.gcd(key_count, 512)
    block_count = key_count // block_rows
    key_blocks = piece_keys[0].reshape(block_count, block_rows, -1)
    value_blocks = piece_values[0].reshape(block_count, block_rows, -1)
    doc_blocks = piece_docs[0].reshape(block_count, block_rows)
    pos_blocks = jnp.arange(key_count, dtype=jnp.int32).reshape(block_count, block_rows)

    def absorb_step(state_now, block_item):
        key_part, value_part, doc_part, pos_part = block_item
        return (
            absorb_block(
                state_now,
                queries,
                key_part,
                value_part,
                doc_part,
                pos_part,
                query_pos,
                my_docs,
                score_scale,
            ),
            None,
        )

    _, denominator, numerator = lax.scan(
        absorb_step, start_state, (key_blocks, value_blocks, doc_blocks, pos_blocks)
    )[0]
    self_out = numerator / denominator[..., None]
    values_own = jnp.dot(features[0], w_value, preferred_element_type=jnp.float32).astype(
        jnp.bfloat16
    )
    image_keys, image_values = (
        lax.all_gather(img_keys[0], "seq", axis=0, tiled=True),
        lax.all_gather(values_own, "seq", axis=0, tiled=True),
    )
    key_count = image_keys.shape[0]
    image_count = tiles.shape[1]
    slot_count = key_count // image_count
    doc_hit = my_docs[:, None] == jnp.arange(cite.shape[1], dtype=jnp.int32)[None, :]
    image_of = jnp.sum(jnp.where(doc_hit, cite[0][None, :], 0), axis=1)
    slot_ids = jnp.arange(key_count, dtype=jnp.int32)
    key_image = slot_ids // slot_count
    owner_hit = key_image[:, None] == jnp.arange(image_count, dtype=jnp.int32)[None, :]
    tile_limit = jnp.sum(jnp.where(owner_hit, tiles[0][None, :], 0), axis=1) * TILE_TOK
    cross_kept = (image_of[:, None] == key_image[None, :]) & (slot_ids % slot_count < tile_limit)[
        None, :
    ]
    cross_q = q_cross[0].reshape(tok_rows, kv_local, group_size, HD)
    cross_scores = (
        jnp.einsum(
            "tgcd,sgd->gcts",
            cross_q,
            image_keys.reshape(key_count, kv_local, HD),
            preferred_element_type=jnp.float32,
        )
        * score_scale
    )
    cross_scores = jnp.where(cross_kept, cross_scores, MASK_FILL)
    cross_exp = jnp.where(
        cross_kept, jnp.exp(cross_scores - jnp.max(cross_scores, axis=-1, keepdims=True)), 0.0
    )
    cross_weights = (cross_exp / jnp.sum(cross_exp, axis=-1, keepdims=True)).astype(jnp.bfloat16)
    cross_out = jnp.einsum(
        "gcts,sgd->gctd",
        cross_weights,
        image_values.reshape(key_count, kv_local, HD),
        preferred_element_type=jnp.float32,
    )
    merged = (
        (self_out + cross_out)
        .astype(jnp.bfloat16)
        .transpose(2, 0, 1, 3)
        .reshape(1, tok_rows, heads_local * HD)
    )
    cot_rows = cotangent[0].reshape(tok_rows, kv_local, group_size, HD)
    grad_terms = jnp.einsum(
        "gcts,tgcd->sgd", cross_weights, cot_rows, preferred_element_type=jnp.float32
    ).reshape(key_count, kv_local * HD)
    value_grad = lax.psum_scatter(
        grad_terms.astype(jnp.bfloat16), "seq", scatter_dimension=0, tiled=True
    )
    own_features = features[0]
    summed_samples = lax.psum_scatter(
        lax.dot_general(
            own_features, value_grad, (((0,), (0,)), ((), ())), preferred_element_type=jnp.float32
        ).astype(jnp.bfloat16),
        "dp",
        scatter_dimension=0,
        tiled=True,
    )
    weight_grad = lax.psum_scatter(summed_samples, "seq", scatter_dimension=0, tiled=True).astype(
        jnp.float32
    )
    return (merged, weight_grad)


def dot_nt(left, right):
    return lax.dot_general(
        left, right, (((1,), (1,)), ((), ())), preferred_element_type=jnp.float32
    )


def dot_nn(left, right):
    return lax.dot_general(
        left, right, (((1,), (0,)), ((), ())), preferred_element_type=jnp.float32
    )


def dot_tn(left, right):
    return lax.dot_general(
        left, right, (((0,), (0,)), ((), ())), preferred_element_type=jnp.float32
    )


def stacked_heads(ref, group, group_size):
    first = group * group_size
    return jnp.concatenate(
        [ref[:, (first + c) * HD : (first + c + 1) * HD] for c in range(group_size)], axis=0
    )


def pack_kernel(
    sizes,
    docs_hbm,
    tiles_hbm,
    cite_hbm,
    features_hbm,
    k_hbm,
    v_hbm,
    rows_ref,
    kv_ref,
    meta_ref,
    docs_ref,
    tiles_ref,
    cite_ref,
    sems,
):
    slots, parts, slot_count = sizes
    tok_rows = docs_ref.shape[1]
    width = kv_ref.shape[1]
    vision = features_hbm.shape[2]
    feature_rows = parts * slots
    pairs = [(docs_hbm, docs_ref), (tiles_hbm, tiles_ref), (cite_hbm, cite_ref)]
    for part in range(parts):
        cut = min(width, vision - part * width)
        pairs.append(
            (
                features_hbm.at[0, :, pl.ds(part * width, cut)],
                rows_ref.at[pl.ds(part * slots, slots), pl.ds(0, cut)],
            )
        )
    pairs.append((k_hbm.at[0], kv_ref.at[pl.ds(0, tok_rows), :]))
    pairs.append((v_hbm.at[0], kv_ref.at[pl.ds(tok_rows, tok_rows), :]))
    copies = [
        pltpu.make_async_copy(source, target, sems.at[n])
        for n, (source, target) in enumerate(pairs)
    ]
    for copy in copies:
        copy.start()
    for copy in copies[:3]:
        copy.wait()
    docs = docs_ref[...]
    image_of = jnp.zeros_like(docs)
    for doc in range(cite_ref.shape[1]):
        image_of = jnp.where(docs == doc, cite_ref[0, doc], image_of)
    count = jnp.zeros_like(docs)
    for image in range(tiles_ref.shape[1]):
        count = jnp.where(image_of == image, tiles_ref[0, image] * TILE_TOK, count)
    first = image_of * slot_count
    row = lax.broadcasted_iota(jnp.int32, meta_ref.shape, 0)
    meta_ref[...] = jnp.where(
        row == 0, docs, jnp.where(row == 1, first, jnp.where(row == 2, first + count, 0))
    )
    doc_rows = jnp.broadcast_to(docs.astype(jnp.float32), (slots, tok_rows))
    spare = jnp.zeros((slots, parts * width - vision - tok_rows), jnp.float32)
    tail = jnp.concatenate([doc_rows, spare], axis=1).astype(jnp.bfloat16)
    for copy in copies[3:]:
        copy.wait()
    last = vision - (parts - 1) * width
    rows_ref[feature_rows - slots : feature_rows, last:] = tail


def cross_kernel(sizes, meta_ref, q_ref, cot_ref, *rest):
    kv_local, group_size, slots, blocks = sizes
    key_refs, weights_ref, grad_refs = rest[:blocks], rest[blocks], rest[blocks + 1 :]
    share = kv_local // len(grad_refs)
    seq_at = lax.axis_index("seq")
    tok_rows = q_ref.shape[0]
    first, count = meta_ref[1:2, :], meta_ref[2:3, :] - meta_ref[1:2, :]
    chosen = [
        jnp.concatenate([first == (seq_at ^ x) * slots] * group_size, axis=1)
        for x in range(blocks)
    ]
    slot_ids = lax.broadcasted_iota(jnp.int32, (slots, tok_rows), 0)
    bias = jnp.where(slot_ids < count, 0.0, MASK_FILL)
    bias = jnp.concatenate([bias] * group_size, axis=1)
    scale = HD ** (-0.5) * LOG2E
    spans = [slice(group * HD, (group + 1) * HD) for group in range(kv_local)]
    scores = [
        dot_nt(
            jnp.concatenate([ref[:, columns] for ref in key_refs], axis=0),
            stacked_heads(q_ref, group, group_size),
        )
        for group, columns in enumerate(spans)
    ]
    flags = [jnp.where(pick, 1.0, 0.0).astype(jnp.bfloat16) for pick in chosen]
    for group in range(kv_local):
        picked = scores[group][(blocks - 1) * slots :]
        for x in range(blocks - 1):
            picked = jnp.where(chosen[x], scores[group][x * slots : (x + 1) * slots], picked)
        scaled = picked * scale + bias
        exps = jnp.exp2(scaled - jnp.max(scaled, axis=0, keepdims=True))
        inverse = 1.0 / jnp.sum(exps, axis=0, keepdims=True)
        weights = (exps * inverse).astype(jnp.bfloat16)
        for x in range(blocks):
            weights_ref[group, x * slots : (x + 1) * slots] = weights * flags[x]
    for group, columns in enumerate(spans):
        grads = dot_nn(weights_ref[group], stacked_heads(cot_ref, group, group_size)).astype(
            jnp.bfloat16
        )
        for x in range(blocks):
            at = pl.multiple_of((seq_at ^ x) * slots, slots)
            grad_refs[group // share][pl.ds(at, slots), spans[group % share]] = grads[
                x * slots : (x + 1) * slots
            ]


def stacked_features(rows, part, slots, cut):
    return jnp.concatenate(
        [ref[part * slots : (part + 1) * slots, :cut] for ref in rows], axis=0
    )


def first_positions(sizes, meta_ref, rows):
    slots, parts, last = sizes
    docs = meta_ref[0:1, :].astype(jnp.float32)
    tok_rows = docs.shape[1]
    start = jnp.zeros((1, tok_rows), jnp.float32)
    at = (parts - 1) * slots
    for ref in rows:
        row = ref[at : at + 16, last : last + tok_rows].astype(jnp.float32)[0:1]
        column = jnp.transpose(jnp.broadcast_to(row, (tok_rows, tok_rows)))
        start = start + jnp.sum(jnp.where(column < docs, 1.0, 0.0), axis=0, keepdims=True)
    return start


def kept_bias(seq_at, first, blocks, start, group_size):
    tok_rows = start.shape[1]
    query_pos = seq_at * tok_rows + lax.broadcasted_iota(jnp.int32, (1, tok_rows), 1)
    bias = []
    for x in range(first, first + blocks):
        key_pos = (seq_at ^ x) * tok_rows + lax.broadcasted_iota(
            jnp.int32, (tok_rows, tok_rows), 0
        )
        kept = (key_pos >= start) & (key_pos <= query_pos)
        bias.append(jnp.where(kept, 0.0, MASK_FILL))
    return jnp.concatenate([jnp.concatenate(bias, axis=0)] * group_size, axis=1)


def scaled_scores(pairs, columns, queries, bias):
    tok_rows = pairs[0].shape[0] // 2
    keys = jnp.concatenate([ref[:tok_rows, columns] for ref in pairs], axis=0)
    return dot_nt(keys, queries) * (HD ** (-0.5) * LOG2E) + bias


def weighted_values(pairs, columns, exps):
    tok_rows = pairs[0].shape[0] // 2
    vals = jnp.concatenate([ref[tok_rows:, columns] for ref in pairs], axis=0)
    return dot_tn(vals, exps)


def early_kernel(sizes, meta_ref, q_ref, w_ref, weights_ref, *rest):
    kv_local, group_size, slots, parts, blocks, count = sizes
    rows, pairs = rest[:blocks], rest[blocks : blocks + count]
    cross_ref, self_ref, stats_ref, turned_ref = rest[blocks + count :]
    width = pairs[0].shape[1]
    vision = w_ref.shape[0]
    seq_at = lax.axis_index("seq")
    start = first_positions((slots, parts, vision - (parts - 1) * width), meta_ref, rows)
    stats_ref[kv_local, 0:1, :] = jnp.concatenate([start] * group_size, axis=1)
    bias = kept_bias(seq_at, 0, count, start.astype(jnp.int32), group_size)
    spans = [slice(group * HD, (group + 1) * HD) for group in range(kv_local)]
    scores = [
        scaled_scores(pairs, columns, stacked_heads(q_ref, group, group_size), bias)
        for group, columns in enumerate(spans)
    ]
    weighted = []
    for group in range(kv_local):
        top = jnp.max(scores[group], axis=0, keepdims=True)
        exps = jnp.exp2(scores[group] - top)
        stats_ref[group, 0:1, :] = top
        stats_ref[group, 1:2, :] = jnp.sum(exps, axis=0, keepdims=True)
        weighted.append(exps.astype(jnp.bfloat16))
    for group, columns in enumerate(spans):
        self_ref[group] = weighted_values(pairs, columns, weighted[group])
    total = None
    for part in range(parts):
        cut = min(width, vision - part * width)
        stacked = stacked_features(rows, part, slots, cut)
        turned_ref[part * width : part * width + cut, :] = jnp.transpose(stacked)
        term = dot_nn(stacked, w_ref[part * width : part * width + cut, :])
        total = term if total is None else total + term
    values = total.astype(jnp.bfloat16)
    for group in range(kv_local):
        columns = slice(group * HD, (group + 1) * HD)
        cross_ref[group] = dot_tn(values[:, columns], weights_ref[group])


def absorbed(sizes, first, pair_ref, q_ref, stats_ref):
    kv_local, group_size = sizes
    seq_at = lax.axis_index("seq")
    start = stats_ref[kv_local, 0:1, : q_ref.shape[0]]
    bias = kept_bias(seq_at, first, 1, start.astype(jnp.int32), group_size)
    spans = [slice(group * HD, (group + 1) * HD) for group in range(kv_local)]
    pairs = (pair_ref,)
    scores = [
        scaled_scores(pairs, columns, stacked_heads(q_ref, group, group_size), bias)
        for group, columns in enumerate(spans)
    ]
    found = []
    for group in range(kv_local):
        before = stats_ref[group, 0:1, :]
        top = jnp.maximum(before, jnp.max(scores[group], axis=0, keepdims=True))
        exps = jnp.exp2(scores[group] - top)
        factor = jnp.exp2(before - top)
        total = factor * stats_ref[group, 1:2, :] + jnp.sum(exps, axis=0, keepdims=True)
        found.append((top, factor, total, exps.astype(jnp.bfloat16)))
    return [
        (top, factor, total, weighted_values(pairs, columns, exps))
        for columns, (top, factor, total, exps) in zip(spans, found)
    ]


def middle_kernel(sizes, q_ref, self_ref, stats_ref, pair_ref, out_ref, stats_out_ref):
    kv_local, group_size, first = sizes
    stats_out_ref[kv_local, 0:1, :] = stats_ref[kv_local, 0:1, :]
    found = absorbed((kv_local, group_size), first, pair_ref, q_ref, stats_ref)
    for group, (top, factor, total, added) in enumerate(found):
        out_ref[group] = self_ref[group] * factor + added
        stats_out_ref[group, 0:1, :] = top
        stats_out_ref[group, 1:2, :] = total


def late_kernel(
    sizes, q_ref, cross_ref, self_ref, stats_ref, pair_ref, out_hbm, out_ref, sems
):
    kv_local, group_size, first = sizes
    tok_rows = q_ref.shape[0]
    found = absorbed((kv_local, group_size), first, pair_ref, q_ref, stats_ref)
    copies = []
    for group, (_, factor, total, added) in enumerate(found):
        inverse = 1.0 / total
        self_out = self_ref[group] * (factor * inverse) + added * inverse
        merged = (self_out + cross_ref[group]).astype(jnp.bfloat16)
        for c in range(group_size):
            out_ref[group, :, c * HD : (c + 1) * HD] = jnp.transpose(
                merged[:, c * tok_rows : (c + 1) * tok_rows]
            )
        span = group_size * HD
        copies.append(
            pltpu.make_async_copy(
                out_ref.at[group], out_hbm.at[:, pl.ds(group * span, span)], sems.at[group]
            )
        )
        copies[-1].start()
    for copy in copies:
        copy.wait()


def product_kernel(sizes, turned_ref, *rest):
    slots, out_rows, steps, blocks = sizes
    terms, outs, sum_ref = rest[:blocks], rest[blocks:-1], rest[-1]
    seq_at, dp_at = lax.axis_index("seq"), lax.axis_index("dp")
    total = terms[0][...].astype(jnp.float32)
    for ref in terms[1:]:
        total = total + ref[...].astype(jnp.float32)
    sum_ref[...] = total.astype(jnp.bfloat16)
    grads = jnp.concatenate(
        [
            sum_ref[pl.ds(pl.multiple_of((seq_at ^ x) * slots, slots), slots), :]
            for x in range(blocks)
        ],
        axis=0,
    )
    for x in range(steps):
        row = pl.multiple_of(((dp_at ^ x) * blocks + seq_at) * out_rows, out_rows)
        block = dot_nn(turned_ref[pl.ds(row, out_rows), :], grads)
        outs[x][...] = block.astype(outs[x].dtype)


def vmem_specs(count):
    return [pl.BlockSpec(memory_space=pltpu.VMEM)] * count


def dp_order(size):
    return sorted(range(1, size), key=lambda x: (x == 1, x))


def on_device_small(
    seq_size,
    dp_size,
    q_self,
    k_self,
    v_self,
    docs,
    q_cross,
    cotangent,
    img_keys,
    features,
    w_value,
    tiles,
    cite,
):
    tok_rows = q_self.shape[1]
    width = k_self.shape[2]
    kv_local = width // HD
    heads_local = q_self.shape[2] // HD
    group_size = heads_local // kv_local
    slots = img_keys.shape[1]
    vision = features.shape[2]
    images = tiles.shape[1]
    out_rows = vision // (seq_size * dp_size)
    key_count = slots * seq_size
    hbm = pl.BlockSpec(memory_space=pltpu.HBM)
    parts = -(-vision // width)
    feature_rows = parts * slots
    far, near = seq_size // 2, 1

    def swapped(array, axis, size, x):
        return lax.ppermute(array, axis, [(i, i ^ x) for i in range(size)])

    def gathered(array):
        there = swapped(array, "seq", seq_size, far)
        beside = swapped(array, "seq", seq_size, near)
        across = swapped(there, "seq", seq_size, near)
        return (array, beside, there, across)

    key_blocks = gathered(img_keys[0])

    rows_own, kv_own, meta = pl.pallas_call(
        functools.partial(pack_kernel, (slots, parts, key_count // images)),
        out_shape=(
            jax.ShapeDtypeStruct((feature_rows, width), jnp.bfloat16),
            jax.ShapeDtypeStruct((2 * tok_rows, width), jnp.bfloat16),
            jax.ShapeDtypeStruct((8, tok_rows), jnp.int32),
        ),
        in_specs=[hbm] * 6,
        out_specs=tuple(vmem_specs(3)),
        scratch_shapes=[
            pltpu.VMEM(docs.shape, jnp.int32),
            pltpu.SMEM(tiles.shape, jnp.int32),
            pltpu.SMEM(cite.shape, jnp.int32),
            pltpu.SemaphoreType.DMA((5 + parts,)),
        ],
        compiler_params=pltpu.CompilerParams(vmem_limit_bytes=8 << 20),
        cost_estimate=pl.CostEstimate(flops=4 << 30, bytes_accessed=16 << 20, transcendentals=0),
        name="pack",
    )(
        *[
            pltpu.with_memory_space_constraint(array, pltpu.HBM)
            for array in (docs, tiles, cite, features, k_self, v_self)
        ]
    )
    row_blocks = gathered(rows_own)

    halves = 1
    half_width = width // halves
    weights, *grad_terms = pl.pallas_call(
        functools.partial(cross_kernel, (kv_local, group_size, slots, seq_size)),
        out_shape=(
            jax.ShapeDtypeStruct((kv_local, key_count, group_size * tok_rows), jnp.bfloat16),
        )
        + (jax.ShapeDtypeStruct((key_count, half_width), jnp.bfloat16),) * halves,
        in_specs=vmem_specs(3 + seq_size),
        out_specs=tuple(vmem_specs(1 + halves)),
        compiler_params=pltpu.CompilerParams(vmem_limit_bytes=24 << 20),
        name="cross",
    )(meta, q_cross[0], cotangent[0], *key_blocks)
    kv_blocks = gathered(kv_own)
    chip = seq_size // 2
    columns = group_size * tok_rows
    partial_shape = jax.ShapeDtypeStruct((kv_local, HD, columns), jnp.float32)
    stats_shape = jax.ShapeDtypeStruct((kv_local + 1, 8, columns), jnp.float32)
    cross_out, partial, stats, turned = pl.pallas_call(
        functools.partial(early_kernel, (kv_local, group_size, slots, parts, seq_size, chip)),
        out_shape=(
            partial_shape,
            partial_shape,
            stats_shape,
            jax.ShapeDtypeStruct((vision, key_count), jnp.bfloat16),
        ),
        in_specs=vmem_specs(4 + seq_size + chip),
        out_specs=tuple(vmem_specs(4)),
        compiler_params=pltpu.CompilerParams(vmem_limit_bytes=24 << 20),
        name="early",
    )(meta, q_self[0], w_value, weights, *row_blocks, *kv_blocks[:chip])
    sums = []
    for half in range(halves):
        term_blocks = gathered(grad_terms[half])
        blocks_out = pl.pallas_call(
            functools.partial(product_kernel, (slots, out_rows, dp_size, seq_size)),
            out_shape=tuple(
                jax.ShapeDtypeStruct(
                    (out_rows, half_width), jnp.bfloat16 if x else jnp.float32
                )
                for x in range(dp_size)
            ),
            in_specs=vmem_specs(1 + seq_size),
            out_specs=tuple(vmem_specs(dp_size)),
            scratch_shapes=[pltpu.VMEM((key_count, half_width), jnp.bfloat16)],
            compiler_params=pltpu.CompilerParams(vmem_limit_bytes=16 << 20),
            name="product",
        )(turned, *term_blocks)
        total = blocks_out[0]
        for x in dp_order(dp_size):
            arrived = swapped(blocks_out[x], "dp", dp_size, x)
            total = total + arrived.astype(jnp.float32)
        sums.append(total)
    weight_grad = jnp.concatenate(sums, axis=1)
    partial, stats = pl.pallas_call(
        functools.partial(middle_kernel, (kv_local, group_size, chip)),
        out_shape=(partial_shape, stats_shape),
        in_specs=vmem_specs(4),
        out_specs=tuple(vmem_specs(2)),
        compiler_params=pltpu.CompilerParams(vmem_limit_bytes=16 << 20),
        name="middle",
    )(q_self[0], partial, stats, kv_blocks[chip])
    merged = pl.pallas_call(
        functools.partial(late_kernel, (kv_local, group_size, chip + 1)),
        out_shape=jax.ShapeDtypeStruct((tok_rows, heads_local * HD), jnp.bfloat16),
        in_specs=vmem_specs(5),
        out_specs=hbm,
        scratch_shapes=[
            pltpu.VMEM((kv_local, tok_rows, group_size * HD), jnp.bfloat16),
            pltpu.SemaphoreType.DMA((kv_local,)),
        ],
        compiler_params=pltpu.CompilerParams(vmem_limit_bytes=16 << 20),
        name="late",
    )(q_self[0], cross_out, partial, stats, kv_blocks[chip + 1])
    return (merged[None], weight_grad)


def fits_small(mesh, shapes):
    seq_size, dp_size = mesh.shape["seq"], mesh.shape["dp"]
    q_self, k_self, img_keys, features, tiles, cite = shapes
    tensor = mesh.shape["tensor"]
    powers = all(n & (n - 1) == 0 for n in (seq_size, dp_size))
    tok_rows, width = q_self[1] // seq_size, k_self[2] // tensor
    slots = img_keys[1] // seq_size
    rows, left = divmod(features[2], seq_size * dp_size)
    return (
        powers
        and seq_size == 4
        and dp_size <= 8
        and tok_rows == HD
        and tok_rows <= width
        and slots % 32 == 0
        and slots * seq_size == HD
        and tiles[1] == seq_size
        and left == 0
        and rows % 16 == 0
        and features[2] % HD == 0
        and width % HD == 0
        and -features[2] % width >= tok_rows
        and cite[1] <= 256
    )


def solution(mesh):
    in_specs = (
        P("dp", "seq", "tensor"),
        P("dp", "seq", "tensor"),
        P("dp", "seq", "tensor"),
        P("dp", "seq"),
        P("dp", "seq", "tensor"),
        P("dp", "seq", "tensor"),
        P("dp", "seq", "tensor"),
        P("dp", "seq", None),
        P(None, "tensor"),
        P("dp", None),
        P("dp", None),
    )
    out_specs = (P("dp", "seq", "tensor"), P(("dp", "seq"), "tensor"))

    def run(*arrays):
        shapes = [arrays[i].shape for i in (0, 1, 6, 7, 9, 10)]
        body = on_device_general
        if fits_small(mesh, shapes):
            body = functools.partial(on_device_small, mesh.shape["seq"], mesh.shape["dp"])
        return jax.shard_map(
            body, mesh=mesh, in_specs=in_specs, out_specs=out_specs, check_vma=False
        )(*arrays)

    return run
```

```python
import functools
import math

import jax
import jax.numpy as jnp
from jax import lax
from jax.experimental import pallas as pl
from jax.experimental.pallas import tpu as pltpu
from jax.sharding import PartitionSpec as P


HD = 128
TILE_TOK = 8


MASK_FILL = -1e30
LOG2E = math.log2(math.e)


def absorb_block(
    running, queries, key_rows, value_rows, key_docs, key_pos, query_pos, my_docs, score_scale
):
    running_max, denominator, numerator = running
    kv_local = queries.shape[1]
    key_count = key_rows.shape[0]
    key_heads = key_rows.reshape(key_count, kv_local, HD)
    value_heads = value_rows.reshape(key_count, kv_local, HD)
    scores = (
        jnp.einsum("tgcd,sgd->gcts", queries, key_heads, preferred_element_type=jnp.float32)
        * score_scale
    )
    kept = (query_pos[:, None] >= key_pos[None, :]) & (my_docs[:, None] == key_docs[None, :])
    scores = jnp.where(kept, scores, MASK_FILL)
    new_max = jnp.maximum(running_max, jnp.max(scores, axis=-1))
    factor = jnp.exp(running_max - new_max)
    weights = jnp.where(kept, jnp.exp(scores - new_max[..., None]), 0.0)
    denominator = factor * denominator + jnp.sum(weights, axis=-1)
    numerator = factor[..., None] * numerator + jnp.einsum(
        "gcts,sgd->gctd",
        weights.astype(jnp.bfloat16),
        value_heads,
        preferred_element_type=jnp.float32,
    )
    return (new_max, denominator, numerator)


def on_device_general(
    q_self, k_self, v_self, docs, q_cross, cotangent, img_keys, features, w_value, tiles, cite
):
    tok_rows = q_self.shape[1]
    kv_local = k_self.shape[2] // HD
    heads_local = q_self.shape[2] // HD
    group_size = heads_local // kv_local
    score_scale = HD ** (-0.5)
    first_row = lax.axis_index("seq") * tok_rows
    query_pos = first_row + jnp.arange(tok_rows, dtype=jnp.int32)
    my_docs = docs[0]
    queries = q_self[0].reshape(tok_rows, kv_local, group_size, HD)
    start_state = (
        jnp.full((kv_local, group_size, tok_rows), MASK_FILL, jnp.float32),
        jnp.zeros((kv_local, group_size, tok_rows), jnp.float32),
        jnp.zeros((kv_local, group_size, tok_rows, HD), jnp.float32),
    )
    piece_keys = lax.all_gather(k_self, "seq", axis=1, tiled=True)
    piece_values = lax.all_gather(v_self, "seq", axis=1, tiled=True)
    piece_docs = lax.all_gather(docs, "seq", axis=1, tiled=True)
    key_count = piece_keys.shape[1]
    block_rows = math.gcd(key_count, 512)
    block_count = key_count // block_rows
    key_blocks = piece_keys[0].reshape(block_count, block_rows, -1)
    value_blocks = piece_values[0].reshape(block_count, block_rows, -1)
    doc_blocks = piece_docs[0].reshape(block_count, block_rows)
    pos_blocks = jnp.arange(key_count, dtype=jnp.int32).reshape(block_count, block_rows)

    def absorb_step(state_now, block_item):
        key_part, value_part, doc_part, pos_part = block_item
        return (
            absorb_block(
                state_now,
                queries,
                key_part,
                value_part,
                doc_part,
                pos_part,
                query_pos,
                my_docs,
                score_scale,
            ),
            None,
        )

    _, denominator, numerator = lax.scan(
        absorb_step, start_state, (key_blocks, value_blocks, doc_blocks, pos_blocks)
    )[0]
    self_out = numerator / denominator[..., None]
    values_own = jnp.dot(features[0], w_value, preferred_element_type=jnp.float32).astype(
        jnp.bfloat16
    )
    image_keys, image_values = (
        lax.all_gather(img_keys[0], "seq", axis=0, tiled=True),
        lax.all_gather(values_own, "seq", axis=0, tiled=True),
    )
    key_count = image_keys.shape[0]
    image_count = tiles.shape[1]
    slot_count = key_count // image_count
    doc_hit = my_docs[:, None] == jnp.arange(cite.shape[1], dtype=jnp.int32)[None, :]
    image_of = jnp.sum(jnp.where(doc_hit, cite[0][None, :], 0), axis=1)
    slot_ids = jnp.arange(key_count, dtype=jnp.int32)
    key_image = slot_ids // slot_count
    owner_hit = key_image[:, None] == jnp.arange(image_count, dtype=jnp.int32)[None, :]
    tile_limit = jnp.sum(jnp.where(owner_hit, tiles[0][None, :], 0), axis=1) * TILE_TOK
    cross_kept = (image_of[:, None] == key_image[None, :]) & (slot_ids % slot_count < tile_limit)[
        None, :
    ]
    cross_q = q_cross[0].reshape(tok_rows, kv_local, group_size, HD)
    cross_scores = (
        jnp.einsum(
            "tgcd,sgd->gcts",
            cross_q,
            image_keys.reshape(key_count, kv_local, HD),
            preferred_element_type=jnp.float32,
        )
        * score_scale
    )
    cross_scores = jnp.where(cross_kept, cross_scores, MASK_FILL)
    cross_exp = jnp.where(
        cross_kept, jnp.exp(cross_scores - jnp.max(cross_scores, axis=-1, keepdims=True)), 0.0
    )
    cross_weights = (cross_exp / jnp.sum(cross_exp, axis=-1, keepdims=True)).astype(jnp.bfloat16)
    cross_out = jnp.einsum(
        "gcts,sgd->gctd",
        cross_weights,
        image_values.reshape(key_count, kv_local, HD),
        preferred_element_type=jnp.float32,
    )
    merged = (
        (self_out + cross_out)
        .astype(jnp.bfloat16)
        .transpose(2, 0, 1, 3)
        .reshape(1, tok_rows, heads_local * HD)
    )
    cot_rows = cotangent[0].reshape(tok_rows, kv_local, group_size, HD)
    grad_terms = jnp.einsum(
        "gcts,tgcd->sgd", cross_weights, cot_rows, preferred_element_type=jnp.float32
    ).reshape(key_count, kv_local * HD)
    value_grad = lax.psum_scatter(
        grad_terms.astype(jnp.bfloat16), "seq", scatter_dimension=0, tiled=True
    )
    own_features = features[0]
    summed_samples = lax.psum_scatter(
        lax.dot_general(
            own_features, value_grad, (((0,), (0,)), ((), ())), preferred_element_type=jnp.float32
        ).astype(jnp.bfloat16),
        "dp",
        scatter_dimension=0,
        tiled=True,
    )
    weight_grad = lax.psum_scatter(summed_samples, "seq", scatter_dimension=0, tiled=True).astype(
        jnp.float32
    )
    return (merged, weight_grad)


def dot_nt(left, right):
    return lax.dot_general(
        left, right, (((1,), (1,)), ((), ())), preferred_element_type=jnp.float32
    )


def dot_nn(left, right):
    return lax.dot_general(
        left, right, (((1,), (0,)), ((), ())), preferred_element_type=jnp.float32
    )


def dot_tn(left, right):
    return lax.dot_general(
        left, right, (((0,), (0,)), ((), ())), preferred_element_type=jnp.float32
    )


def stacked_heads(ref, group, group_size):
    first = group * group_size
    return jnp.concatenate(
        [ref[:, (first + c) * HD : (first + c + 1) * HD] for c in range(group_size)], axis=0
    )


def pack_kernel(
    sizes,
    docs_hbm,
    tiles_hbm,
    cite_hbm,
    features_hbm,
    k_hbm,
    v_hbm,
    rows_ref,
    kv_ref,
    meta_ref,
    docs_ref,
    tiles_ref,
    cite_ref,
    sems,
):
    slots, parts, slot_count = sizes
    tok_rows = docs_ref.shape[1]
    width = kv_ref.shape[1]
    vision = features_hbm.shape[2]
    feature_rows = parts * slots
    pairs = [(docs_hbm, docs_ref), (tiles_hbm, tiles_ref), (cite_hbm, cite_ref)]
    for part in range(parts):
        cut = min(width, vision - part * width)
        pairs.append(
            (
                features_hbm.at[0, :, pl.ds(part * width, cut)],
                rows_ref.at[pl.ds(part * slots, slots), pl.ds(0, cut)],
            )
        )
    pairs.append((k_hbm.at[0], kv_ref.at[pl.ds(0, tok_rows), :]))
    pairs.append((v_hbm.at[0], kv_ref.at[pl.ds(tok_rows, tok_rows), :]))
    copies = [
        pltpu.make_async_copy(source, target, sems.at[n])
        for n, (source, target) in enumerate(pairs)
    ]
    for copy in copies:
        copy.start()
    for copy in copies[:3]:
        copy.wait()
    docs = docs_ref[...]
    image_of = jnp.zeros_like(docs)
    for doc in range(cite_ref.shape[1]):
        image_of = jnp.where(docs == doc, cite_ref[0, doc], image_of)
    count = jnp.zeros_like(docs)
    for image in range(tiles_ref.shape[1]):
        count = jnp.where(image_of == image, tiles_ref[0, image] * TILE_TOK, count)
    first = image_of * slot_count
    row = lax.broadcasted_iota(jnp.int32, meta_ref.shape, 0)
    meta_ref[...] = jnp.where(
        row == 0, docs, jnp.where(row == 1, first, jnp.where(row == 2, first + count, 0))
    )
    doc_rows = jnp.broadcast_to(docs.astype(jnp.float32), (slots, tok_rows))
    spare = jnp.zeros((slots, parts * width - vision - tok_rows), jnp.float32)
    tail = jnp.concatenate([doc_rows, spare], axis=1).astype(jnp.bfloat16)
    for copy in copies[3:]:
        copy.wait()
    last = vision - (parts - 1) * width
    rows_ref[feature_rows - slots : feature_rows, last:] = tail


def chosen_columns(meta_ref, seq_at, slots, x, group_size):
    return jnp.concatenate([meta_ref[1:2, :] == (seq_at ^ x) * slots] * group_size, axis=1)


def block_scores(spans, group_size, q_ref, key_refs):
    return [
        dot_nt(
            jnp.concatenate([ref[:, columns] for ref in key_refs], axis=0),
            stacked_heads(q_ref, group, group_size),
        )
        for group, columns in enumerate(spans)
    ]


def pick_kernel(sizes, meta_ref, q_ref, *rest):
    kv_local, group_size, slots = sizes
    key_refs, out_ref = rest[:-1], rest[-1]
    seq_at = lax.axis_index("seq")
    spans = [slice(group * HD, (group + 1) * HD) for group in range(kv_local)]
    scores = block_scores(spans, group_size, q_ref, key_refs)
    for group in range(kv_local):
        picked = scores[group][:slots]
        for x in range(1, len(key_refs)):
            pick = chosen_columns(meta_ref, seq_at, slots, x, group_size)
            picked = jnp.where(pick, scores[group][x * slots : (x + 1) * slots], picked)
        out_ref[group] = picked


def cross_kernel(sizes, meta_ref, q_ref, cot_ref, picked_ref, key_ref, weights_ref, grad_ref):
    kv_local, group_size, slots, blocks = sizes
    seq_at = lax.axis_index("seq")
    tok_rows = q_ref.shape[0]
    chosen = [
        chosen_columns(meta_ref, seq_at, slots, x, group_size) for x in range(blocks)
    ]
    count = meta_ref[2:3, :] - meta_ref[1:2, :]
    slot_ids = lax.broadcasted_iota(jnp.int32, (slots, tok_rows), 0)
    bias = jnp.where(slot_ids < count, 0.0, MASK_FILL)
    bias = jnp.concatenate([bias] * group_size, axis=1)
    scale = HD ** (-0.5) * LOG2E
    spans = [slice(group * HD, (group + 1) * HD) for group in range(kv_local)]
    scores = block_scores(spans, group_size, q_ref, (key_ref,))
    flags = [jnp.where(pick, 1.0, 0.0).astype(jnp.bfloat16) for pick in chosen]
    for group in range(kv_local):
        picked = jnp.where(chosen[blocks - 1], scores[group], picked_ref[group])
        scaled = picked * scale + bias
        exps = jnp.exp2(scaled - jnp.max(scaled, axis=0, keepdims=True))
        inverse = 1.0 / jnp.sum(exps, axis=0, keepdims=True)
        weights = (exps * inverse).astype(jnp.bfloat16)
        for x in range(blocks):
            weights_ref[group, x * slots : (x + 1) * slots] = weights * flags[x]
    for group, columns in enumerate(spans):
        grads = dot_nn(weights_ref[group], stacked_heads(cot_ref, group, group_size)).astype(
            jnp.bfloat16
        )
        for x in range(blocks):
            at = pl.multiple_of((seq_at ^ x) * slots, slots)
            grad_ref[pl.ds(at, slots), columns] = grads[x * slots : (x + 1) * slots]


def stacked_features(rows, part, slots, cut):
    return jnp.concatenate(
        [ref[part * slots : (part + 1) * slots, :cut] for ref in rows], axis=0
    )


def first_positions(sizes, meta_ref, rows):
    slots, parts, last = sizes
    docs = meta_ref[0:1, :].astype(jnp.float32)
    tok_rows = docs.shape[1]
    start = jnp.zeros((1, tok_rows), jnp.float32)
    at = (parts - 1) * slots
    for ref in rows:
        row = ref[at : at + 16, last : last + tok_rows].astype(jnp.float32)[0:1]
        column = jnp.transpose(jnp.broadcast_to(row, (tok_rows, tok_rows)))
        start = start + jnp.sum(jnp.where(column < docs, 1.0, 0.0), axis=0, keepdims=True)
    return start


def kept_bias(seq_at, first, blocks, start, group_size):
    tok_rows = start.shape[1]
    query_pos = seq_at * tok_rows + lax.broadcasted_iota(jnp.int32, (1, tok_rows), 1)
    bias = []
    for x in range(first, first + blocks):
        key_pos = (seq_at ^ x) * tok_rows + lax.broadcasted_iota(
            jnp.int32, (tok_rows, tok_rows), 0
        )
        kept = (key_pos >= start) & (key_pos <= query_pos)
        bias.append(jnp.where(kept, 0.0, MASK_FILL))
    return jnp.concatenate([jnp.concatenate(bias, axis=0)] * group_size, axis=1)


def scaled_scores(pairs, columns, queries, bias):
    tok_rows = pairs[0].shape[0] // 2
    keys = jnp.concatenate([ref[:tok_rows, columns] for ref in pairs], axis=0)
    return dot_nt(keys, queries) * (HD ** (-0.5) * LOG2E) + bias


def weighted_values(pairs, columns, exps):
    tok_rows = pairs[0].shape[0] // 2
    vals = jnp.concatenate([ref[tok_rows:, columns] for ref in pairs], axis=0)
    return dot_tn(vals, exps)


def early_kernel(sizes, meta_ref, q_ref, w_ref, weights_ref, *rest):
    kv_local, group_size, slots, parts, blocks, count = sizes
    rows, pairs = rest[:blocks], rest[blocks : blocks + count]
    cross_ref, self_ref, stats_ref, turned_ref = rest[blocks + count :]
    width = pairs[0].shape[1]
    vision = w_ref.shape[0]
    seq_at = lax.axis_index("seq")
    start = first_positions((slots, parts, vision - (parts - 1) * width), meta_ref, rows)
    stats_ref[kv_local, 0:1, :] = jnp.concatenate([start] * group_size, axis=1)
    bias = kept_bias(seq_at, 0, count, start.astype(jnp.int32), group_size)
    spans = [slice(group * HD, (group + 1) * HD) for group in range(kv_local)]
    scores = [
        scaled_scores(pairs, columns, stacked_heads(q_ref, group, group_size), bias)
        for group, columns in enumerate(spans)
    ]
    weighted = []
    for group in range(kv_local):
        top = jnp.max(scores[group], axis=0, keepdims=True)
        exps = jnp.exp2(scores[group] - top)
        stats_ref[group, 0:1, :] = top
        stats_ref[group, 1:2, :] = jnp.sum(exps, axis=0, keepdims=True)
        weighted.append(exps.astype(jnp.bfloat16))
    for group, columns in enumerate(spans):
        self_ref[group] = weighted_values(pairs, columns, weighted[group])
    total = None
    for part in range(parts):
        cut = min(width, vision - part * width)
        stacked = stacked_features(rows, part, slots, cut)
        turned_ref[part * width : part * width + cut, :] = jnp.transpose(stacked)
        term = dot_nn(stacked, w_ref[part * width : part * width + cut, :])
        total = term if total is None else total + term
    values = total.astype(jnp.bfloat16)
    for group in range(kv_local):
        columns = slice(group * HD, (group + 1) * HD)
        cross_ref[group] = dot_tn(values[:, columns], weights_ref[group])


def absorbed(sizes, first, pair_ref, q_ref, stats_ref):
    kv_local, group_size = sizes
    seq_at = lax.axis_index("seq")
    start = stats_ref[kv_local, 0:1, : q_ref.shape[0]]
    bias = kept_bias(seq_at, first, 1, start.astype(jnp.int32), group_size)
    spans = [slice(group * HD, (group + 1) * HD) for group in range(kv_local)]
    pairs = (pair_ref,)
    scores = [
        scaled_scores(pairs, columns, stacked_heads(q_ref, group, group_size), bias)
        for group, columns in enumerate(spans)
    ]
    found = []
    for group in range(kv_local):
        before = stats_ref[group, 0:1, :]
        top = jnp.maximum(before, jnp.max(scores[group], axis=0, keepdims=True))
        exps = jnp.exp2(scores[group] - top)
        factor = jnp.exp2(before - top)
        total = factor * stats_ref[group, 1:2, :] + jnp.sum(exps, axis=0, keepdims=True)
        found.append((top, factor, total, exps.astype(jnp.bfloat16)))
    return [
        (top, factor, total, weighted_values(pairs, columns, exps))
        for columns, (top, factor, total, exps) in zip(spans, found)
    ]


def middle_kernel(sizes, q_ref, self_ref, stats_ref, pair_ref, out_ref, stats_out_ref):
    kv_local, group_size, first = sizes
    stats_out_ref[kv_local, 0:1, :] = stats_ref[kv_local, 0:1, :]
    found = absorbed((kv_local, group_size), first, pair_ref, q_ref, stats_ref)
    for group, (top, factor, total, added) in enumerate(found):
        out_ref[group] = self_ref[group] * factor + added
        stats_out_ref[group, 0:1, :] = top
        stats_out_ref[group, 1:2, :] = total


def late_kernel(
    sizes, q_ref, cross_ref, self_ref, stats_ref, pair_ref, out_hbm, out_ref, sems
):
    kv_local, group_size, first = sizes
    tok_rows = q_ref.shape[0]
    found = absorbed((kv_local, group_size), first, pair_ref, q_ref, stats_ref)
    copies = []
    for group, (_, factor, total, added) in enumerate(found):
        inverse = 1.0 / total
        self_out = self_ref[group] * (factor * inverse) + added * inverse
        merged = (self_out + cross_ref[group]).astype(jnp.bfloat16)
        for c in range(group_size):
            out_ref[group, :, c * HD : (c + 1) * HD] = jnp.transpose(
                merged[:, c * tok_rows : (c + 1) * tok_rows]
            )
        span = group_size * HD
        copies.append(
            pltpu.make_async_copy(
                out_ref.at[group], out_hbm.at[:, pl.ds(group * span, span)], sems.at[group]
            )
        )
        copies[-1].start()
    for copy in copies:
        copy.wait()


def presum_kernel(*refs):
    total = refs[0][...].astype(jnp.float32)
    for ref in refs[1:-1]:
        total = total + ref[...].astype(jnp.float32)
    refs[-1][...] = total


def product_kernel(sizes, turned_ref, *rest):
    slots, out_rows, steps, blocks = sizes
    terms, outs, sum_ref = rest[:2], rest[2:-1], rest[-1]
    seq_at, dp_at = lax.axis_index("seq"), lax.axis_index("dp")
    total = terms[0][...].astype(jnp.float32)
    for ref in terms[1:]:
        total = total + ref[...].astype(jnp.float32)
    sum_ref[...] = total.astype(jnp.bfloat16)
    grads = jnp.concatenate(
        [
            sum_ref[pl.ds(pl.multiple_of((seq_at ^ x) * slots, slots), slots), :]
            for x in range(blocks)
        ],
        axis=0,
    )
    for x in range(steps):
        row = pl.multiple_of(((dp_at ^ x) * blocks + seq_at) * out_rows, out_rows)
        block = dot_nn(turned_ref[pl.ds(row, out_rows), :], grads)
        outs[x][...] = block.astype(outs[x].dtype)


def vmem_specs(count):
    return [pl.BlockSpec(memory_space=pltpu.VMEM)] * count


def dp_order(size):
    return sorted(range(1, size), key=lambda x: (x == 1, x))


def on_device_small(
    seq_size,
    dp_size,
    q_self,
    k_self,
    v_self,
    docs,
    q_cross,
    cotangent,
    img_keys,
    features,
    w_value,
    tiles,
    cite,
):
    tok_rows = q_self.shape[1]
    width = k_self.shape[2]
    kv_local = width // HD
    heads_local = q_self.shape[2] // HD
    group_size = heads_local // kv_local
    slots = img_keys.shape[1]
    vision = features.shape[2]
    images = tiles.shape[1]
    out_rows = vision // (seq_size * dp_size)
    key_count = slots * seq_size
    hbm = pl.BlockSpec(memory_space=pltpu.HBM)
    parts = -(-vision // width)
    feature_rows = parts * slots
    far, near = seq_size // 2, 1

    def swapped(array, axis, size, x):
        return lax.ppermute(array, axis, [(i, i ^ x) for i in range(size)])

    def gathered(array):
        there = swapped(array, "seq", seq_size, far)
        beside = swapped(array, "seq", seq_size, near)
        across = swapped(there, "seq", seq_size, near)
        return (array, beside, there, across)

    key_blocks = gathered(img_keys[0])

    rows_own, kv_own, meta = pl.pallas_call(
        functools.partial(pack_kernel, (slots, parts, key_count // images)),
        out_shape=(
            jax.ShapeDtypeStruct((feature_rows, width), jnp.bfloat16),
            jax.ShapeDtypeStruct((2 * tok_rows, width), jnp.bfloat16),
            jax.ShapeDtypeStruct((8, tok_rows), jnp.int32),
        ),
        in_specs=[hbm] * 6,
        out_specs=tuple(vmem_specs(3)),
        scratch_shapes=[
            pltpu.VMEM(docs.shape, jnp.int32),
            pltpu.SMEM(tiles.shape, jnp.int32),
            pltpu.SMEM(cite.shape, jnp.int32),
            pltpu.SemaphoreType.DMA((5 + parts,)),
        ],
        compiler_params=pltpu.CompilerParams(vmem_limit_bytes=8 << 20),
        cost_estimate=pl.CostEstimate(flops=4 << 30, bytes_accessed=16 << 20, transcendentals=0),
        name="pack",
    )(
        *[
            pltpu.with_memory_space_constraint(array, pltpu.HBM)
            for array in (docs, tiles, cite, features, k_self, v_self)
        ]
    )
    row_blocks = gathered(rows_own)

    halves, half_width = 1, width
    columns = group_size * tok_rows
    *keys_in, keys_last = key_blocks
    picked = pl.pallas_call(
        functools.partial(pick_kernel, (kv_local, group_size, slots)),
        out_shape=jax.ShapeDtypeStruct((kv_local, slots, columns), jnp.float32),
        in_specs=vmem_specs(1 + seq_size),
        out_specs=vmem_specs(1)[0],
        compiler_params=pltpu.CompilerParams(vmem_limit_bytes=16 << 20),
        name="pick",
    )(meta, q_cross[0], *keys_in)
    weights, grad_terms = pl.pallas_call(
        functools.partial(cross_kernel, (kv_local, group_size, slots, seq_size)),
        out_shape=(
            jax.ShapeDtypeStruct((kv_local, key_count, columns), jnp.bfloat16),
            jax.ShapeDtypeStruct((key_count, width), jnp.bfloat16),
        ),
        in_specs=vmem_specs(5),
        out_specs=tuple(vmem_specs(2)),
        compiler_params=pltpu.CompilerParams(vmem_limit_bytes=16 << 20),
        name="cross",
    )(meta, q_cross[0], cotangent[0], picked, keys_last)
    kv_blocks = gathered(kv_own)
    chip = seq_size // 2
    partial_shape = jax.ShapeDtypeStruct((kv_local, HD, columns), jnp.float32)
    stats_shape = jax.ShapeDtypeStruct((kv_local + 1, 8, columns), jnp.float32)
    cross_out, partial, stats, turned = pl.pallas_call(
        functools.partial(early_kernel, (kv_local, group_size, slots, parts, seq_size, chip)),
        out_shape=(
            partial_shape,
            partial_shape,
            stats_shape,
            jax.ShapeDtypeStruct((vision, key_count), jnp.bfloat16),
        ),
        in_specs=vmem_specs(4 + seq_size + chip),
        out_specs=tuple(vmem_specs(4)),
        compiler_params=pltpu.CompilerParams(vmem_limit_bytes=24 << 20),
        name="early",
    )(meta, q_self[0], w_value, weights, *row_blocks, *kv_blocks[:chip])
    sums = []
    for _ in range(halves):
        *terms_in, terms_last = gathered(grad_terms)
        terms_sum = pl.pallas_call(
            presum_kernel,
            out_shape=jax.ShapeDtypeStruct((key_count, half_width), jnp.float32),
            in_specs=vmem_specs(seq_size - 1),
            out_specs=vmem_specs(1)[0],
            compiler_params=pltpu.CompilerParams(vmem_limit_bytes=8 << 20),
            name="presum",
        )(*terms_in)
        term_blocks = (terms_sum, terms_last)
        blocks_out = pl.pallas_call(
            functools.partial(product_kernel, (slots, out_rows, dp_size, seq_size)),
            out_shape=tuple(
                jax.ShapeDtypeStruct(
                    (out_rows, half_width), jnp.bfloat16 if x else jnp.float32
                )
                for x in range(dp_size)
            ),
            in_specs=vmem_specs(3),
            out_specs=tuple(vmem_specs(dp_size)),
            scratch_shapes=[pltpu.VMEM((key_count, half_width), jnp.bfloat16)],
            compiler_params=pltpu.CompilerParams(vmem_limit_bytes=16 << 20),
            name="product",
        )(turned, *term_blocks)
        total = blocks_out[0]
        for x in dp_order(dp_size):
            arrived = swapped(blocks_out[x], "dp", dp_size, x)
            total = total + arrived.astype(jnp.float32)
        sums.append(total)
    weight_grad = jnp.concatenate(sums, axis=1)
    partial, stats = pl.pallas_call(
        functools.partial(middle_kernel, (kv_local, group_size, chip)),
        out_shape=(partial_shape, stats_shape),
        in_specs=vmem_specs(4),
        out_specs=tuple(vmem_specs(2)),
        compiler_params=pltpu.CompilerParams(vmem_limit_bytes=16 << 20),
        name="middle",
    )(q_self[0], partial, stats, kv_blocks[chip])
    merged = pl.pallas_call(
        functools.partial(late_kernel, (kv_local, group_size, chip + 1)),
        out_shape=jax.ShapeDtypeStruct((tok_rows, heads_local * HD), jnp.bfloat16),
        in_specs=vmem_specs(5),
        out_specs=hbm,
        scratch_shapes=[
            pltpu.VMEM((kv_local, tok_rows, group_size * HD), jnp.bfloat16),
            pltpu.SemaphoreType.DMA((kv_local,)),
        ],
        compiler_params=pltpu.CompilerParams(vmem_limit_bytes=16 << 20),
        name="late",
    )(q_self[0], cross_out, partial, stats, kv_blocks[chip + 1])
    return (merged[None], weight_grad)


def fits_small(mesh, shapes):
    seq_size, dp_size = mesh.shape["seq"], mesh.shape["dp"]
    q_self, k_self, img_keys, features, tiles, cite = shapes
    tensor = mesh.shape["tensor"]
    powers = all(n & (n - 1) == 0 for n in (seq_size, dp_size))
    tok_rows, width = q_self[1] // seq_size, k_self[2] // tensor
    slots = img_keys[1] // seq_size
    rows, left = divmod(features[2], seq_size * dp_size)
    return (
        powers
        and seq_size == 4
        and dp_size <= 8
        and tok_rows == HD
        and tok_rows <= width
        and slots % 32 == 0
        and slots * seq_size == HD
        and tiles[1] == seq_size
        and left == 0
        and rows % 16 == 0
        and features[2] % HD == 0
        and width % HD == 0
        and -features[2] % width >= tok_rows
        and cite[1] <= 256
    )


def solution(mesh):
    in_specs = (
        P("dp", "seq", "tensor"),
        P("dp", "seq", "tensor"),
        P("dp", "seq", "tensor"),
        P("dp", "seq"),
        P("dp", "seq", "tensor"),
        P("dp", "seq", "tensor"),
        P("dp", "seq", "tensor"),
        P("dp", "seq", None),
        P(None, "tensor"),
        P("dp", None),
        P("dp", None),
    )
    out_specs = (P("dp", "seq", "tensor"), P(("dp", "seq"), "tensor"))

    def run(*arrays):
        shapes = [arrays[i].shape for i in (0, 1, 6, 7, 9, 10)]
        body = on_device_general
        if fits_small(mesh, shapes):
            body = functools.partial(on_device_small, mesh.shape["seq"], mesh.shape["dp"])
        return jax.shard_map(
            body, mesh=mesh, in_specs=in_specs, out_specs=out_specs, check_vma=False
        )(*arrays)

    return run
```

```python
import functools
import math

import jax
import jax.numpy as jnp
from jax import lax
from jax.experimental import pallas as pl
from jax.experimental.pallas import tpu as pltpu
from jax.sharding import PartitionSpec as P


HD = 128
TILE_TOK = 8


MASK_FILL = -1e30
LOG2E = math.log2(math.e)


def absorb_block(
    running, queries, key_rows, value_rows, key_docs, key_pos, query_pos, my_docs, score_scale
):
    running_max, denominator, numerator = running
    kv_local = queries.shape[1]
    key_count = key_rows.shape[0]
    key_heads = key_rows.reshape(key_count, kv_local, HD)
    value_heads = value_rows.reshape(key_count, kv_local, HD)
    scores = (
        jnp.einsum("tgcd,sgd->gcts", queries, key_heads, preferred_element_type=jnp.float32)
        * score_scale
    )
    kept = (query_pos[:, None] >= key_pos[None, :]) & (my_docs[:, None] == key_docs[None, :])
    scores = jnp.where(kept, scores, MASK_FILL)
    new_max = jnp.maximum(running_max, jnp.max(scores, axis=-1))
    factor = jnp.exp(running_max - new_max)
    weights = jnp.where(kept, jnp.exp(scores - new_max[..., None]), 0.0)
    denominator = factor * denominator + jnp.sum(weights, axis=-1)
    numerator = factor[..., None] * numerator + jnp.einsum(
        "gcts,sgd->gctd",
        weights.astype(jnp.bfloat16),
        value_heads,
        preferred_element_type=jnp.float32,
    )
    return (new_max, denominator, numerator)


def on_device_general(
    q_self, k_self, v_self, docs, q_cross, cotangent, img_keys, features, w_value, tiles, cite
):
    tok_rows = q_self.shape[1]
    kv_local = k_self.shape[2] // HD
    heads_local = q_self.shape[2] // HD
    group_size = heads_local // kv_local
    score_scale = HD ** (-0.5)
    first_row = lax.axis_index("seq") * tok_rows
    query_pos = first_row + jnp.arange(tok_rows, dtype=jnp.int32)
    my_docs = docs[0]
    queries = q_self[0].reshape(tok_rows, kv_local, group_size, HD)
    start_state = (
        jnp.full((kv_local, group_size, tok_rows), MASK_FILL, jnp.float32),
        jnp.zeros((kv_local, group_size, tok_rows), jnp.float32),
        jnp.zeros((kv_local, group_size, tok_rows, HD), jnp.float32),
    )
    piece_keys = lax.all_gather(k_self, "seq", axis=1, tiled=True)
    piece_values = lax.all_gather(v_self, "seq", axis=1, tiled=True)
    piece_docs = lax.all_gather(docs, "seq", axis=1, tiled=True)
    key_count = piece_keys.shape[1]
    block_rows = math.gcd(key_count, 512)
    block_count = key_count // block_rows
    key_blocks = piece_keys[0].reshape(block_count, block_rows, -1)
    value_blocks = piece_values[0].reshape(block_count, block_rows, -1)
    doc_blocks = piece_docs[0].reshape(block_count, block_rows)
    pos_blocks = jnp.arange(key_count, dtype=jnp.int32).reshape(block_count, block_rows)

    def absorb_step(state_now, block_item):
        key_part, value_part, doc_part, pos_part = block_item
        return (
            absorb_block(
                state_now,
                queries,
                key_part,
                value_part,
                doc_part,
                pos_part,
                query_pos,
                my_docs,
                score_scale,
            ),
            None,
        )

    _, denominator, numerator = lax.scan(
        absorb_step, start_state, (key_blocks, value_blocks, doc_blocks, pos_blocks)
    )[0]
    self_out = numerator / denominator[..., None]
    values_own = jnp.dot(features[0], w_value, preferred_element_type=jnp.float32).astype(
        jnp.bfloat16
    )
    image_keys, image_values = (
        lax.all_gather(img_keys[0], "seq", axis=0, tiled=True),
        lax.all_gather(values_own, "seq", axis=0, tiled=True),
    )
    key_count = image_keys.shape[0]
    image_count = tiles.shape[1]
    slot_count = key_count // image_count
    doc_hit = my_docs[:, None] == jnp.arange(cite.shape[1], dtype=jnp.int32)[None, :]
    image_of = jnp.sum(jnp.where(doc_hit, cite[0][None, :], 0), axis=1)
    slot_ids = jnp.arange(key_count, dtype=jnp.int32)
    key_image = slot_ids // slot_count
    owner_hit = key_image[:, None] == jnp.arange(image_count, dtype=jnp.int32)[None, :]
    tile_limit = jnp.sum(jnp.where(owner_hit, tiles[0][None, :], 0), axis=1) * TILE_TOK
    cross_kept = (image_of[:, None] == key_image[None, :]) & (slot_ids % slot_count < tile_limit)[
        None, :
    ]
    cross_q = q_cross[0].reshape(tok_rows, kv_local, group_size, HD)
    cross_scores = (
        jnp.einsum(
            "tgcd,sgd->gcts",
            cross_q,
            image_keys.reshape(key_count, kv_local, HD),
            preferred_element_type=jnp.float32,
        )
        * score_scale
    )
    cross_scores = jnp.where(cross_kept, cross_scores, MASK_FILL)
    cross_exp = jnp.where(
        cross_kept, jnp.exp(cross_scores - jnp.max(cross_scores, axis=-1, keepdims=True)), 0.0
    )
    cross_weights = (cross_exp / jnp.sum(cross_exp, axis=-1, keepdims=True)).astype(jnp.bfloat16)
    cross_out = jnp.einsum(
        "gcts,sgd->gctd",
        cross_weights,
        image_values.reshape(key_count, kv_local, HD),
        preferred_element_type=jnp.float32,
    )
    merged = (
        (self_out + cross_out)
        .astype(jnp.bfloat16)
        .transpose(2, 0, 1, 3)
        .reshape(1, tok_rows, heads_local * HD)
    )
    cot_rows = cotangent[0].reshape(tok_rows, kv_local, group_size, HD)
    grad_terms = jnp.einsum(
        "gcts,tgcd->sgd", cross_weights, cot_rows, preferred_element_type=jnp.float32
    ).reshape(key_count, kv_local * HD)
    value_grad = lax.psum_scatter(
        grad_terms.astype(jnp.bfloat16), "seq", scatter_dimension=0, tiled=True
    )
    own_features = features[0]
    summed_samples = lax.psum_scatter(
        lax.dot_general(
            own_features, value_grad, (((0,), (0,)), ((), ())), preferred_element_type=jnp.float32
        ).astype(jnp.bfloat16),
        "dp",
        scatter_dimension=0,
        tiled=True,
    )
    weight_grad = lax.psum_scatter(summed_samples, "seq", scatter_dimension=0, tiled=True).astype(
        jnp.float32
    )
    return (merged, weight_grad)


def dot_nt(left, right):
    return lax.dot_general(
        left, right, (((1,), (1,)), ((), ())), preferred_element_type=jnp.float32
    )


def dot_nn(left, right):
    return lax.dot_general(
        left, right, (((1,), (0,)), ((), ())), preferred_element_type=jnp.float32
    )


def dot_tn(left, right):
    return lax.dot_general(
        left, right, (((0,), (0,)), ((), ())), preferred_element_type=jnp.float32
    )


def stacked_heads(ref, group, group_size):
    first = group * group_size
    return jnp.concatenate(
        [ref[:, (first + c) * HD : (first + c + 1) * HD] for c in range(group_size)], axis=0
    )


def pack_kernel(
    sizes,
    docs_hbm,
    tiles_hbm,
    cite_hbm,
    features_hbm,
    k_hbm,
    v_hbm,
    rows_ref,
    kv_ref,
    meta_ref,
    docs_ref,
    tiles_ref,
    cite_ref,
    sems,
):
    slots, parts, slot_count = sizes
    tok_rows = docs_ref.shape[1]
    width = kv_ref.shape[1]
    vision = features_hbm.shape[2]
    feature_rows = parts * slots
    pairs = [(docs_hbm, docs_ref), (tiles_hbm, tiles_ref), (cite_hbm, cite_ref)]
    for part in range(parts):
        cut = min(width, vision - part * width)
        pairs.append(
            (
                features_hbm.at[0, :, pl.ds(part * width, cut)],
                rows_ref.at[pl.ds(part * slots, slots), pl.ds(0, cut)],
            )
        )
    pairs.append((k_hbm.at[0], kv_ref.at[pl.ds(0, tok_rows), :]))
    pairs.append((v_hbm.at[0], kv_ref.at[pl.ds(tok_rows, tok_rows), :]))
    copies = [
        pltpu.make_async_copy(source, target, sems.at[n])
        for n, (source, target) in enumerate(pairs)
    ]
    for copy in copies:
        copy.start()
    for copy in copies[:3]:
        copy.wait()
    docs = docs_ref[...]
    image_of = jnp.zeros_like(docs)
    for doc in range(cite_ref.shape[1]):
        image_of = jnp.where(docs == doc, cite_ref[0, doc], image_of)
    count = jnp.zeros_like(docs)
    for image in range(tiles_ref.shape[1]):
        count = jnp.where(image_of == image, tiles_ref[0, image] * TILE_TOK, count)
    first = image_of * slot_count
    row = lax.broadcasted_iota(jnp.int32, meta_ref.shape, 0)
    meta_ref[...] = jnp.where(
        row == 0, docs, jnp.where(row == 1, first, jnp.where(row == 2, first + count, 0))
    )
    doc_rows = jnp.broadcast_to(docs.astype(jnp.float32), (slots, tok_rows))
    spare = jnp.zeros((slots, parts * width - vision - tok_rows), jnp.float32)
    tail = jnp.concatenate([doc_rows, spare], axis=1).astype(jnp.bfloat16)
    for copy in copies[3:]:
        copy.wait()
    last = vision - (parts - 1) * width
    rows_ref[feature_rows - slots : feature_rows, last:] = tail


def chosen_columns(meta_ref, seq_at, slots, x, group_size):
    return jnp.concatenate([meta_ref[1:2, :] == (seq_at ^ x) * slots] * group_size, axis=1)


def block_scores(spans, group_size, q_ref, key_refs):
    return [
        dot_nt(
            jnp.concatenate([ref[:, columns] for ref in key_refs], axis=0),
            stacked_heads(q_ref, group, group_size),
        )
        for group, columns in enumerate(spans)
    ]


def pick_kernel(sizes, meta_ref, q_ref, *rest):
    kv_local, group_size, slots = sizes
    key_refs, out_ref = rest[:-1], rest[-1]
    seq_at = lax.axis_index("seq")
    spans = [slice(group * HD, (group + 1) * HD) for group in range(kv_local)]
    scores = block_scores(spans, group_size, q_ref, key_refs)
    for group in range(kv_local):
        picked = scores[group][:slots]
        for x in range(1, len(key_refs)):
            pick = chosen_columns(meta_ref, seq_at, slots, x, group_size)
            picked = jnp.where(pick, scores[group][x * slots : (x + 1) * slots], picked)
        out_ref[group] = picked


def cross_kernel(sizes, meta_ref, q_ref, cot_ref, picked_ref, key_ref, weights_ref, grad_ref):
    kv_local, group_size, slots, blocks = sizes
    seq_at = lax.axis_index("seq")
    tok_rows = q_ref.shape[0]
    chosen = [
        chosen_columns(meta_ref, seq_at, slots, x, group_size) for x in range(blocks)
    ]
    count = meta_ref[2:3, :] - meta_ref[1:2, :]
    slot_ids = lax.broadcasted_iota(jnp.int32, (slots, tok_rows), 0)
    bias = jnp.where(slot_ids < count, 0.0, MASK_FILL)
    bias = jnp.concatenate([bias] * group_size, axis=1)
    scale = HD ** (-0.5) * LOG2E
    spans = [slice(group * HD, (group + 1) * HD) for group in range(kv_local)]
    scores = block_scores(spans, group_size, q_ref, (key_ref,))
    flags = [jnp.where(pick, 1.0, 0.0).astype(jnp.bfloat16) for pick in chosen]
    for group in range(kv_local):
        picked = jnp.where(chosen[blocks - 1], scores[group], picked_ref[group])
        scaled = picked * scale + bias
        exps = jnp.exp2(scaled - jnp.max(scaled, axis=0, keepdims=True))
        inverse = 1.0 / jnp.sum(exps, axis=0, keepdims=True)
        weights = (exps * inverse).astype(jnp.bfloat16)
        for x in range(blocks):
            weights_ref[group, x * slots : (x + 1) * slots] = weights * flags[x]
        columns = spans[group]
        full = jnp.concatenate([weights * flag for flag in flags], axis=0)
        grads = dot_nn(full, stacked_heads(cot_ref, group, group_size)).astype(jnp.bfloat16)
        for x in range(blocks):
            at = pl.multiple_of((seq_at ^ x) * slots, slots)
            grad_ref[pl.ds(at, slots), columns] = grads[x * slots : (x + 1) * slots]


def stacked_features(rows, part, slots, cut):
    return jnp.concatenate(
        [ref[part * slots : (part + 1) * slots, :cut] for ref in rows], axis=0
    )


def first_positions(sizes, meta_ref, rows):
    slots, parts, last = sizes
    docs = meta_ref[0:1, :].astype(jnp.float32)
    tok_rows = docs.shape[1]
    start = jnp.zeros((1, tok_rows), jnp.float32)
    at = (parts - 1) * slots
    for ref in rows:
        row = ref[at : at + 16, last : last + tok_rows].astype(jnp.float32)[0:1]
        column = jnp.transpose(jnp.broadcast_to(row, (tok_rows, tok_rows)))
        start = start + jnp.sum(jnp.where(column < docs, 1.0, 0.0), axis=0, keepdims=True)
    return start


def kept_bias(seq_at, first, blocks, start, group_size):
    tok_rows = start.shape[1]
    query_pos = seq_at * tok_rows + lax.broadcasted_iota(jnp.int32, (1, tok_rows), 1)
    bias = []
    for x in range(first, first + blocks):
        key_pos = (seq_at ^ x) * tok_rows + lax.broadcasted_iota(
            jnp.int32, (tok_rows, tok_rows), 0
        )
        kept = (key_pos >= start) & (key_pos <= query_pos)
        bias.append(jnp.where(kept, 0.0, MASK_FILL))
    return jnp.concatenate([jnp.concatenate(bias, axis=0)] * group_size, axis=1)


def scaled_scores(pairs, columns, queries, bias):
    tok_rows = pairs[0].shape[0] // 2
    keys = jnp.concatenate([ref[:tok_rows, columns] for ref in pairs], axis=0)
    return dot_nt(keys, queries) * (HD ** (-0.5) * LOG2E) + bias


def weighted_values(pairs, columns, exps):
    tok_rows = pairs[0].shape[0] // 2
    vals = jnp.concatenate([ref[tok_rows:, columns] for ref in pairs], axis=0)
    return dot_tn(vals, exps)


def early_kernel(sizes, meta_ref, q_ref, w_ref, weights_ref, *rest):
    kv_local, group_size, slots, parts, blocks, count = sizes
    rows, pairs = rest[:blocks], rest[blocks : blocks + count]
    cross_ref, self_ref, stats_ref, turned_ref = rest[blocks + count :]
    width = pairs[0].shape[1]
    vision = w_ref.shape[0]
    seq_at = lax.axis_index("seq")
    start = first_positions((slots, parts, vision - (parts - 1) * width), meta_ref, rows)
    stats_ref[kv_local, 0:1, :] = jnp.concatenate([start] * group_size, axis=1)
    bias = kept_bias(seq_at, 0, count, start.astype(jnp.int32), group_size)
    spans = [slice(group * HD, (group + 1) * HD) for group in range(kv_local)]
    scores = [
        scaled_scores(pairs, columns, stacked_heads(q_ref, group, group_size), bias)
        for group, columns in enumerate(spans)
    ]
    weighted = []
    for group in range(kv_local):
        top = jnp.max(scores[group], axis=0, keepdims=True)
        exps = jnp.exp2(scores[group] - top)
        stats_ref[group, 0:1, :] = top
        stats_ref[group, 1:2, :] = jnp.sum(exps, axis=0, keepdims=True)
        weighted.append(exps.astype(jnp.bfloat16))
    for group, columns in enumerate(spans):
        self_ref[group] = weighted_values(pairs, columns, weighted[group])
    total = None
    for part in range(parts):
        cut = min(width, vision - part * width)
        stacked = stacked_features(rows, part, slots, cut)
        turned_ref[part * width : part * width + cut, :] = jnp.transpose(stacked)
        term = dot_nn(stacked, w_ref[part * width : part * width + cut, :])
        total = term if total is None else total + term
    values = total.astype(jnp.bfloat16)
    for group in range(kv_local):
        columns = slice(group * HD, (group + 1) * HD)
        cross_ref[group] = dot_tn(values[:, columns], weights_ref[group])


def absorbed(sizes, first, pair_ref, q_ref, stats_ref):
    kv_local, group_size = sizes
    seq_at = lax.axis_index("seq")
    start = stats_ref[kv_local, 0:1, : q_ref.shape[0]]
    bias = kept_bias(seq_at, first, 1, start.astype(jnp.int32), group_size)
    spans = [slice(group * HD, (group + 1) * HD) for group in range(kv_local)]
    pairs = (pair_ref,)
    scores = [
        scaled_scores(pairs, columns, stacked_heads(q_ref, group, group_size), bias)
        for group, columns in enumerate(spans)
    ]
    found = []
    for group in range(kv_local):
        before = stats_ref[group, 0:1, :]
        top = jnp.maximum(before, jnp.max(scores[group], axis=0, keepdims=True))
        exps = jnp.exp2(scores[group] - top)
        factor = jnp.exp2(before - top)
        total = factor * stats_ref[group, 1:2, :] + jnp.sum(exps, axis=0, keepdims=True)
        found.append((top, factor, total, exps.astype(jnp.bfloat16)))
    return [
        (top, factor, total, weighted_values(pairs, columns, exps))
        for columns, (top, factor, total, exps) in zip(spans, found)
    ]


def middle_kernel(sizes, q_ref, self_ref, stats_ref, pair_ref, out_ref, stats_out_ref):
    kv_local, group_size, first = sizes
    stats_out_ref[kv_local, 0:1, :] = stats_ref[kv_local, 0:1, :]
    found = absorbed((kv_local, group_size), first, pair_ref, q_ref, stats_ref)
    for group, (top, factor, total, added) in enumerate(found):
        out_ref[group] = self_ref[group] * factor + added
        stats_out_ref[group, 0:1, :] = top
        stats_out_ref[group, 1:2, :] = total


def late_kernel(
    sizes, q_ref, cross_ref, self_ref, stats_ref, pair_ref, out_hbm, out_ref, sems
):
    kv_local, group_size, first = sizes
    tok_rows = q_ref.shape[0]
    found = absorbed((kv_local, group_size), first, pair_ref, q_ref, stats_ref)
    copies = []
    for group, (_, factor, total, added) in enumerate(found):
        inverse = 1.0 / total
        self_out = self_ref[group] * (factor * inverse) + added * inverse
        merged = (self_out + cross_ref[group]).astype(jnp.bfloat16)
        for c in range(group_size):
            out_ref[group, :, c * HD : (c + 1) * HD] = jnp.transpose(
                merged[:, c * tok_rows : (c + 1) * tok_rows]
            )
        span = group_size * HD
        copies.append(
            pltpu.make_async_copy(
                out_ref.at[group], out_hbm.at[:, pl.ds(group * span, span)], sems.at[group]
            )
        )
        copies[-1].start()
    for copy in copies:
        copy.wait()


def presum_kernel(*refs):
    total = refs[0][...].astype(jnp.float32)
    for ref in refs[1:-1]:
        total = total + ref[...].astype(jnp.float32)
    refs[-1][...] = total


def product_kernel(sizes, turned_ref, *rest):
    slots, out_rows, steps, blocks = sizes
    terms, outs, sum_ref = rest[:2], rest[2:-1], rest[-1]
    seq_at, dp_at = lax.axis_index("seq"), lax.axis_index("dp")
    total = terms[0][...].astype(jnp.float32)
    for ref in terms[1:]:
        total = total + ref[...].astype(jnp.float32)
    sum_ref[...] = total.astype(jnp.bfloat16)
    grads = jnp.concatenate(
        [
            sum_ref[pl.ds(pl.multiple_of((seq_at ^ x) * slots, slots), slots), :]
            for x in range(blocks)
        ],
        axis=0,
    )
    for x in range(steps):
        row = pl.multiple_of(((dp_at ^ x) * blocks + seq_at) * out_rows, out_rows)
        block = dot_nn(turned_ref[pl.ds(row, out_rows), :], grads)
        outs[x][...] = block.astype(outs[x].dtype)


def vmem_specs(count):
    return [pl.BlockSpec(memory_space=pltpu.VMEM)] * count


def dp_order(size):
    return sorted(range(1, size), key=lambda x: (x == 1, x))


def on_device_small(
    seq_size,
    dp_size,
    q_self,
    k_self,
    v_self,
    docs,
    q_cross,
    cotangent,
    img_keys,
    features,
    w_value,
    tiles,
    cite,
):
    tok_rows = q_self.shape[1]
    width = k_self.shape[2]
    kv_local = width // HD
    heads_local = q_self.shape[2] // HD
    group_size = heads_local // kv_local
    slots = img_keys.shape[1]
    vision = features.shape[2]
    images = tiles.shape[1]
    out_rows = vision // (seq_size * dp_size)
    key_count = slots * seq_size
    hbm = pl.BlockSpec(memory_space=pltpu.HBM)
    parts = -(-vision // width)
    feature_rows = parts * slots
    far, near = seq_size // 2, 1

    def swapped(array, axis, size, x):
        return lax.ppermute(array, axis, [(i, i ^ x) for i in range(size)])

    def gathered(array):
        there = swapped(array, "seq", seq_size, far)
        beside = swapped(array, "seq", seq_size, near)
        across = swapped(there, "seq", seq_size, near)
        return (array, beside, there, across)

    key_blocks = gathered(img_keys[0])

    rows_own, kv_own, meta = pl.pallas_call(
        functools.partial(pack_kernel, (slots, parts, key_count // images)),
        out_shape=(
            jax.ShapeDtypeStruct((feature_rows, width), jnp.bfloat16),
            jax.ShapeDtypeStruct((2 * tok_rows, width), jnp.bfloat16),
            jax.ShapeDtypeStruct((8, tok_rows), jnp.int32),
        ),
        in_specs=[hbm] * 6,
        out_specs=tuple(vmem_specs(3)),
        scratch_shapes=[
            pltpu.VMEM(docs.shape, jnp.int32),
            pltpu.SMEM(tiles.shape, jnp.int32),
            pltpu.SMEM(cite.shape, jnp.int32),
            pltpu.SemaphoreType.DMA((5 + parts,)),
        ],
        compiler_params=pltpu.CompilerParams(vmem_limit_bytes=8 << 20),
        cost_estimate=pl.CostEstimate(flops=4 << 30, bytes_accessed=16 << 20, transcendentals=0),
        name="pack",
    )(
        *[
            pltpu.with_memory_space_constraint(array, pltpu.HBM)
            for array in (docs, tiles, cite, features, k_self, v_self)
        ]
    )
    row_blocks = gathered(rows_own)

    halves, half_width = 1, width
    columns = group_size * tok_rows
    *keys_in, keys_last = key_blocks
    picked = pl.pallas_call(
        functools.partial(pick_kernel, (kv_local, group_size, slots)),
        out_shape=jax.ShapeDtypeStruct((kv_local, slots, columns), jnp.float32),
        in_specs=vmem_specs(1 + seq_size),
        out_specs=vmem_specs(1)[0],
        compiler_params=pltpu.CompilerParams(vmem_limit_bytes=16 << 20),
        name="pick",
    )(meta, q_cross[0], *keys_in)
    weights, grad_terms = pl.pallas_call(
        functools.partial(cross_kernel, (kv_local, group_size, slots, seq_size)),
        out_shape=(
            jax.ShapeDtypeStruct((kv_local, key_count, columns), jnp.bfloat16),
            jax.ShapeDtypeStruct((key_count, width), jnp.bfloat16),
        ),
        in_specs=vmem_specs(5),
        out_specs=tuple(vmem_specs(2)),
        compiler_params=pltpu.CompilerParams(vmem_limit_bytes=16 << 20),
        name="cross",
    )(meta, q_cross[0], cotangent[0], picked, keys_last)
    kv_blocks = gathered(kv_own)
    chip = seq_size // 2
    partial_shape = jax.ShapeDtypeStruct((kv_local, HD, columns), jnp.float32)
    stats_shape = jax.ShapeDtypeStruct((kv_local + 1, 8, columns), jnp.float32)
    cross_out, partial, stats, turned = pl.pallas_call(
        functools.partial(early_kernel, (kv_local, group_size, slots, parts, seq_size, chip)),
        out_shape=(
            partial_shape,
            partial_shape,
            stats_shape,
            jax.ShapeDtypeStruct((vision, key_count), jnp.bfloat16),
        ),
        in_specs=vmem_specs(4 + seq_size + chip),
        out_specs=tuple(vmem_specs(4)),
        compiler_params=pltpu.CompilerParams(vmem_limit_bytes=24 << 20),
        name="early",
    )(meta, q_self[0], w_value, weights, *row_blocks, *kv_blocks[:chip])
    sums = []
    for _ in range(halves):
        *terms_in, terms_last = gathered(grad_terms)
        terms_sum = pl.pallas_call(
            presum_kernel,
            out_shape=jax.ShapeDtypeStruct((key_count, half_width), jnp.float32),
            in_specs=vmem_specs(seq_size - 1),
            out_specs=vmem_specs(1)[0],
            compiler_params=pltpu.CompilerParams(vmem_limit_bytes=8 << 20),
            name="presum",
        )(*terms_in)
        term_blocks = (terms_sum, terms_last)
        blocks_out = pl.pallas_call(
            functools.partial(product_kernel, (slots, out_rows, dp_size, seq_size)),
            out_shape=tuple(
                jax.ShapeDtypeStruct(
                    (out_rows, half_width), jnp.bfloat16 if x else jnp.float32
                )
                for x in range(dp_size)
            ),
            in_specs=vmem_specs(3),
            out_specs=tuple(vmem_specs(dp_size)),
            scratch_shapes=[pltpu.VMEM((key_count, half_width), jnp.bfloat16)],
            compiler_params=pltpu.CompilerParams(vmem_limit_bytes=16 << 20),
            name="product",
        )(turned, *term_blocks)
        total = blocks_out[0]
        for x in dp_order(dp_size):
            arrived = swapped(blocks_out[x], "dp", dp_size, x)
            total = total + arrived.astype(jnp.float32)
        sums.append(total)
    weight_grad = jnp.concatenate(sums, axis=1)
    partial, stats = pl.pallas_call(
        functools.partial(middle_kernel, (kv_local, group_size, chip)),
        out_shape=(partial_shape, stats_shape),
        in_specs=vmem_specs(4),
        out_specs=tuple(vmem_specs(2)),
        compiler_params=pltpu.CompilerParams(vmem_limit_bytes=16 << 20),
        name="middle",
    )(q_self[0], partial, stats, kv_blocks[chip])
    merged = pl.pallas_call(
        functools.partial(late_kernel, (kv_local, group_size, chip + 1)),
        out_shape=jax.ShapeDtypeStruct((tok_rows, heads_local * HD), jnp.bfloat16),
        in_specs=vmem_specs(5),
        out_specs=hbm,
        scratch_shapes=[
            pltpu.VMEM((kv_local, tok_rows, group_size * HD), jnp.bfloat16),
            pltpu.SemaphoreType.DMA((kv_local,)),
        ],
        compiler_params=pltpu.CompilerParams(vmem_limit_bytes=16 << 20),
        name="late",
    )(q_self[0], cross_out, partial, stats, kv_blocks[chip + 1])
    return (merged[None], weight_grad)


def fits_small(mesh, shapes):
    seq_size, dp_size = mesh.shape["seq"], mesh.shape["dp"]
    q_self, k_self, img_keys, features, tiles, cite = shapes
    tensor = mesh.shape["tensor"]
    powers = all(n & (n - 1) == 0 for n in (seq_size, dp_size))
    tok_rows, width = q_self[1] // seq_size, k_self[2] // tensor
    slots = img_keys[1] // seq_size
    rows, left = divmod(features[2], seq_size * dp_size)
    return (
        powers
        and seq_size == 4
        and dp_size <= 8
        and tok_rows == HD
        and tok_rows <= width
        and slots % 32 == 0
        and slots * seq_size == HD
        and tiles[1] == seq_size
        and left == 0
        and rows % 16 == 0
        and features[2] % HD == 0
        and width % HD == 0
        and -features[2] % width >= tok_rows
        and cite[1] <= 256
    )


def solution(mesh):
    in_specs = (
        P("dp", "seq", "tensor"),
        P("dp", "seq", "tensor"),
        P("dp", "seq", "tensor"),
        P("dp", "seq"),
        P("dp", "seq", "tensor"),
        P("dp", "seq", "tensor"),
        P("dp", "seq", "tensor"),
        P("dp", "seq", None),
        P(None, "tensor"),
        P("dp", None),
        P("dp", None),
    )
    out_specs = (P("dp", "seq", "tensor"), P(("dp", "seq"), "tensor"))

    def run(*arrays):
        shapes = [arrays[i].shape for i in (0, 1, 6, 7, 9, 10)]
        body = on_device_general
        if fits_small(mesh, shapes):
            body = functools.partial(on_device_small, mesh.shape["seq"], mesh.shape["dp"])
        return jax.shard_map(
            body, mesh=mesh, in_specs=in_specs, out_specs=out_specs, check_vma=False
        )(*arrays)

    return run
```
